32 devices in a mesh: groups: 2 (over x), space: 4 (over y, core), pair: 4 (over z).
Axes of the slice: x: 2, y: 2, z: 4, core: 2. Of those that a mesh axis runs over, the one named last changes fastest.
Arguments:
- source_feats: bfloat16 [8, 64, 128, 256], P(('groups', 'pair'), 'space'), parts along dimension 0, may hold values from -46.1 to 46.1
- edit_feats: bfloat16 [8, 64, 128, 256], P(('groups', 'pair'), 'space'), parts along dimension 0, may hold values from -60 to 60
- conv_weight: bfloat16 [128, 289], replicated, may hold values from -0.375 to 0.375
- conv_bias: float32 [128], replicated, may hold values from -3 to 3
- head_weight: float32 [128], replicated, may hold values from -4 to 4
- comp_first: int32 [32], P('groups'), parts along dimension 0, may hold values from 0 to 3
- comp_second: int32 [32], P('groups'), parts along dimension 0, may hold values from 0 to 3
- comp_win: int32 [32], P('groups'), parts along dimension 0, may hold values 0 or 1
Outputs:
- grad_source: bfloat16 [8, 64, 128, 256], P(('groups', 'pair'), 'space'), parts along dimension 0
- grad_edit: bfloat16 [8, 64, 128, 256], P(('groups', 'pair'), 'space'), parts along dimension 0
- grad_conv: float32 [256, 289], P('groups'), parts along dimension 0
- grad_bias: float32 [256], P('groups'), parts along dimension 0
- grad_head: float32 [256], P('groups'), parts along dimension 0
- loss_mean: float32 [2], P('groups'), parts along dimension 0
The draws below stay inside these ranges and needn't reach their ends.
There are 2 independent parts, one for each index of `groups`. The reference program is written for one: setup_inputs(seed, part) draws one part's arguments, and reference() takes and returns one part's arrays. A program takes and returns all parts, laid end to end along the dimension named above; an argument that names none is the same for every part. Nothing has to cross between parts.
All inputs are finite; a program needn't handle non-finite values.
Results may differ from the reference program's by a relative error of at most 0.0076.
Values may be sent and summed in bfloat16 or wider, within the bound.
No kernel may reach another device: no remote copies, remote signals or barrier semaphores. Data moves between devices by JAX's collectives and lax.ppermute only.
A program may use at most 64 MiB of HBM per device.

```python
import math
import jax
import jax.numpy as jnp
from jax import lax

CHAN = 256
CONV_OUT = 128
RADIUS = 8
COLS = 128
DISP = 289
ROWS = 64
PAIRS = 4
COMPS = 16
PIXELS = 8192


def feature_field(subkeys):
    full_shape = (PAIRS, ROWS, COLS, CHAN)
    noise_base = jnp.clip(jax.random.normal(subkeys[0], full_shape, jnp.float32), -4.0, 4.0)
    row_scale = jnp.exp(jax.random.uniform(subkeys[1], (PAIRS, ROWS, 1, 1), jnp.float32, -0.6, 0.6))
    col_scale = jnp.exp(jax.random.uniform(subkeys[2], (PAIRS, 1, COLS, 1), jnp.float32, -0.6, 0.6))
    chan_scale = jnp.exp(jax.random.uniform(subkeys[3], (1, 1, 1, CHAN), jnp.float32, math.log(0.5), math.log(2.0)))
    row_ramp = jnp.sqrt(1.0 + 2.0 * jnp.arange(ROWS, dtype=jnp.float32) / ROWS)[None, :, None, None]
    return noise_base * row_scale * col_scale * chan_scale * row_ramp


def feature_pair(key):
    base_key = jax.random.fold_in(key, 7)
    subkeys = jax.random.split(base_key, 8)
    source_field = feature_field(subkeys[:4])
    own_field = feature_field(subkeys[4:])
    edit_field = 0.5 * jnp.roll(source_field, (3, -2), axis=(1, 2)) + 0.8 * own_field
    return (source_field, edit_field)


def draw_source_feats(key, part):
    return feature_pair(key)[0].astype(jnp.bfloat16)


def draw_edit_feats(key, part):
    return feature_pair(key)[1].astype(jnp.bfloat16)


def with_ends(entries, stream_key, smallest, high):
    index_at = [jax.random.randint(jax.random.fold_in(stream_key, axis), (), 0, length) for axis, length in enumerate(entries.shape)]
    widest = entries.shape.index(max(entries.shape))
    neighbour = index_at[:widest] + [(index_at[widest] + 1) % entries.shape[widest]] + index_at[widest + 1:]
    return entries.at[tuple(index_at)].set(smallest).at[tuple(neighbour)].set(high)


def bell_draw(own_key, extent, width, bound, held_as=jnp.bfloat16):
    array = jax.random.normal(own_key, extent, jnp.float32) * width
    return jnp.minimum(jnp.maximum(array, -bound), bound).astype(held_as)


def setup_inputs(seed: int = 0, part: int = 0) -> dict:
    key_of = jax.random.split(jax.random.key(seed), 9)
    part_keys = jax.random.split(jax.random.fold_in(key_of[8], part), 9)
    source_feats = draw_source_feats(jax.random.fold_in(jax.random.fold_in(key_of[8], part), 71), part)
    edit_feats = draw_edit_feats(jax.random.fold_in(jax.random.fold_in(key_of[8], part), 71), part)
    conv_weight = bell_draw(key_of[2], (CONV_OUT, DISP), DISP ** -0.5, 0.375)
    conv_bias = bell_draw(key_of[3], (CONV_OUT,), 0.5, 3.0, jnp.float32)
    head_weight = bell_draw(key_of[4], (CONV_OUT,), 1.0, 4.0, jnp.float32)
    comp_first = with_ends(jax.random.randint(part_keys[5], (COMPS,), 0, PAIRS), jax.random.fold_in(part_keys[5], 1), 0, PAIRS - 1).astype(jnp.int32)
    comp_second = with_ends(jax.random.randint(part_keys[6], (COMPS,), 0, PAIRS), jax.random.fold_in(part_keys[6], 1), 0, PAIRS - 1).astype(jnp.int32)
    comp_win = with_ends((jax.random.randint(part_keys[7], (COMPS,), 0, 2) < 1).astype(jnp.int32), jax.random.fold_in(part_keys[7], 1), 0, 1)
    return {"source_feats": source_feats, "edit_feats": edit_feats, "conv_weight": conv_weight, "conv_bias": conv_bias, "head_weight": head_weight, "comp_first": comp_first, "comp_second": comp_second, "comp_win": comp_win}


def skew_band(matrix, span_len):
    leading = matrix.shape[:-2]
    columns, full_len = matrix.shape[-2:]
    flattened = matrix.reshape(leading + (columns * full_len,))
    flattened = jnp.pad(flattened, [(0, 0)] * len(leading) + [(0, columns)])
    return flattened.reshape(leading + (columns, full_len + 1))[..., :span_len]

def unskew_band(banded, full_len):
    leading = banded.shape[:-2]
    columns, span_len = banded.shape[-2:]
    padded = jnp.pad(banded, [(0, 0)] * len(leading) + [(0, 0), (0, full_len + 1 - span_len)])
    flattened = padded.reshape(leading + (columns * (full_len + 1),))[..., :columns * full_len]
    return flattened.reshape(leading + (columns, full_len))

def correlate(source, edit_pad, inv_root):
    pairs_here, rows_here, columns = source.shape[:3]
    span_len = edit_pad.shape[1] - rows_here + 1

    def one_shift(offset):
        window = lax.dynamic_slice_in_dim(edit_pad, offset, rows_here, 1)
        matrix = jnp.einsum('pyxc,pyjc->pyxj', source, window, preferred_element_type=jnp.float32)
        return skew_band(matrix, span_len)
    stacked = lax.map(one_shift, jnp.arange(span_len, dtype=jnp.int32))
    ordered = jnp.transpose(stacked, (1, 2, 0, 4, 3)).reshape(pairs_here, rows_here, span_len * span_len, columns)
    return (ordered * inv_root).astype(jnp.bfloat16)

def correlate_back(corr_grad, source, edit_pad):
    pairs_here, rows_here, disp_len, columns = corr_grad.shape
    span_len = math.isqrt(disp_len)
    full_len = columns + span_len - 1
    channels = source.shape[-1]
    shaped = corr_grad.reshape(pairs_here, rows_here, span_len, span_len, columns)

    def one_shift(totals, offset):
        edit_total, source_total = totals
        banded = jnp.swapaxes(lax.dynamic_index_in_dim(shaped, offset, 2, keepdims=False), 2, 3)
        matrix = unskew_band(banded, full_len)
        contrib = jnp.einsum('pyxj,pyxc->pyjc', matrix, source, preferred_element_type=jnp.float32)
        current = lax.dynamic_slice_in_dim(edit_total, offset, rows_here, 1)
        edit_total = lax.dynamic_update_slice_in_dim(edit_total, current + contrib, offset, 1)
        window = lax.dynamic_slice_in_dim(edit_pad, offset, rows_here, 1)
        source_total = source_total + jnp.einsum('pyxj,pyjc->pyxc', matrix, window, preferred_element_type=jnp.float32)
        return ((edit_total, source_total), None)
    edit_init = jnp.zeros((pairs_here, rows_here + span_len - 1, full_len, channels), jnp.float32)
    source_init = jnp.zeros((pairs_here, rows_here, columns, channels), jnp.float32)
    (edit_total, source_total), ignored = lax.scan(one_shift, (edit_init, source_init), jnp.arange(span_len, dtype=jnp.int32))
    return (edit_total, source_total)

def reference(source_feats, edit_feats, conv_weight, conv_bias, head_weight, comp_first, comp_second, comp_win):
    inv_root = CHAN ** (-0.5)
    source_wide = source_feats.astype(jnp.float32)
    edit_pad = jnp.pad(edit_feats.astype(jnp.float32), ((0, 0), (RADIUS, RADIUS), (RADIUS, RADIUS), (0, 0)))
    correlation = correlate(source_wide, edit_pad, inv_root)
    corr_wide = correlation.astype(jnp.float32)
    conv_wide = conv_weight.astype(jnp.float32)
    preact = jnp.einsum('kd,pydx->pykx', conv_wide, corr_wide) + conv_bias[None, None, :, None]
    gating = jax.nn.sigmoid(preact)
    hidden_act = preact * gating
    scores = lax.optimization_barrier(jnp.sum(hidden_act * head_weight[None, None, :, None], axis=(1, 2, 3))) / PIXELS
    pair_ids = jnp.arange(PAIRS, dtype=jnp.int32)
    first_hot = (comp_first[:, None] == pair_ids[None, :]).astype(jnp.float32)
    second_hot = (comp_second[:, None] == pair_ids[None, :]).astype(jnp.float32)
    margin = lax.optimization_barrier(jnp.sum((first_hot - second_hot) * scores[None, :], axis=1))
    win_sign = 2.0 * comp_win.astype(jnp.float32) - 1.0
    loss_mean = jnp.reshape(jnp.mean(jax.nn.softplus(-win_sign * margin)), (1,))
    margin_grad = -win_sign * jax.nn.sigmoid(-win_sign * margin)
    score_grad = lax.optimization_barrier(jnp.sum(margin_grad[:, None] * (first_hot - second_hot), axis=0))
    silu_slope = gating * (1.0 + preact * (1.0 - gating))
    pre_grad = score_grad[:, None, None, None] * head_weight[None, None, :, None] * silu_slope
    pre_rounded = pre_grad.astype(jnp.bfloat16)
    bias_grad = lax.optimization_barrier(jnp.sum(pre_grad, axis=(0, 1, 3))) / PIXELS
    head_grad = lax.optimization_barrier(jnp.sum(score_grad[:, None, None, None] * hidden_act, axis=(0, 1, 3))) / PIXELS
    pre_wide = pre_rounded.astype(jnp.float32)
    conv_grad = jnp.einsum('pykx,pydx->kd', pre_wide, corr_wide) / PIXELS
    corr_grad = jnp.einsum('kd,pykx->pydx', conv_wide, pre_wide).astype(jnp.bfloat16)
    edit_total, source_total = correlate_back(corr_grad.astype(jnp.float32), source_wide, edit_pad)
    edit_sum = edit_total[:, RADIUS:RADIUS + ROWS, RADIUS:RADIUS + COLS]
    return ((source_total * inv_root).astype(jnp.bfloat16), (edit_sum * inv_root).astype(jnp.bfloat16), conv_grad, bias_grad, head_grad, loss_mean)
```

```python
import functools

import jax
import jax.numpy as jnp
from jax import lax
from jax.experimental import pallas as pl
from jax.experimental.pallas import tpu as pltpu
from jax.sharding import PartitionSpec as P

RADIUS = 8
SPAN = 2 * RADIUS + 1
GROUP = 16
WIN = GROUP + 2 * RADIUS
LANES = 128
PER = LANES // WIN
POS = 5
STAT = SPAN * SPAN
F32 = jnp.float32
BF16 = jnp.bfloat16
VMEM_LIMIT = 24 * 1024 * 1024


def nt(a, b):
    return lax.dot_general(a, b, (((1,), (1,)), ((), ())), preferred_element_type=F32)


def nn(a, b):
    return lax.dot_general(a, b, (((1,), (0,)), ((), ())), preferred_element_type=F32)


def tn(a, b):
    return lax.dot_general(a, b, (((0,), (0,)), ((), ())), preferred_element_type=F32)


def iota(shape, dim):
    return lax.broadcasted_iota(jnp.int32, shape, dim)


def mirror(size):
    row, col = iota((size, size), 0), iota((size, size), 1)
    return (col == (row ^ (GROUP - 1))).astype(F32).astype(BF16)


def spread_table(rows):
    row, lane = iota((rows, POS * LANES), 0), iota((rows, POS * LANES), 1)
    dy, t = lane // WIN, lane % WIN
    hit = (row == dy * SPAN + t) & (t < SPAN) & (dy < SPAN)
    return hit.astype(F32).astype(BF16)


def skew(values, shift):
    return pltpu.roll(values, shift, 2, stride=1, stride_axis=1)


def skew_wide(values, shift):
    parts = []
    for start in range(0, values.shape[-1], LANES):
        parts.append(skew(values[:, :, start : start + LANES], shift))
    return parts


def fill_columns(pad_ref, row, rows, cols):
    zero = jnp.zeros((rows, RADIUS, pad_ref.shape[2]), BF16)
    pad_ref[row : row + rows, 0:RADIUS] = zero
    pad_ref[row : row + rows, RADIUS + cols :] = zero


def fill_padded(pad_ref, row, block_ref):
    rows, cols = block_ref.shape[:2]
    fill_columns(pad_ref, row, rows, cols)
    pad_ref[row : row + rows, RADIUS : RADIUS + cols] = block_ref[...]


def fill_halos(pad_ref, low, high, across_ref, beyond_ref, parts):
    me = lax.axis_index("space")
    odd = lax.rem(me, 2) == 1
    cols = across_ref.shape[1]
    for row, edge, mine in ((low, 0, odd), (high, parts - 1, ~odd)):
        fill_columns(pad_ref, row, 8, cols)
        at = (slice(row, row + 8), slice(RADIUS, RADIUS + cols))

        @pl.when(me == edge)
        def _():
            pad_ref[at] = jnp.zeros(across_ref.shape, BF16)

        @pl.when((me != edge) & mine)
        def _():
            pad_ref[at] = across_ref[...]

        @pl.when((me != edge) & ~mine)
        def _():
            pad_ref[at] = beyond_ref[...]


def window(pad_ref, row, rows, g):
    block = pad_ref[row : row + rows, g * GROUP : g * GROUP + WIN, :]
    return block.reshape(rows * WIN, block.shape[2])


def correlate_set(lhs, pad_ref, row, g, inv_root, out_ref, y0, lane):
    ys = lhs.shape[0] // GROUP
    scores = nt(lhs, window(pad_ref, row, 8, g)) * inv_root
    scores = scores.reshape(ys, GROUP, 8 * WIN)
    for i, part in enumerate(skew_wide(scores, LANES - GROUP + 1)):
        at = lane + i * LANES
        out_ref[y0 : y0 + ys, g, :, at : at + LANES] = part.astype(BF16)


def inner_kernel(inv_root, source_ref, edit_ref, weight_ref, turned_ref, corr_ref, wide_ref, pad):
    rows, groups, _, chan = source_ref.shape
    fill_padded(pad, 0, edit_ref)
    table = spread_table(SPAN * SPAN)
    base = tn(weight_ref[...], table)
    for r in range(PER):
        wide_ref[r] = (base if r == 0 else pltpu.roll(base, r * WIN, 1)).astype(BF16)
    turn = mirror(rows * GROUP)

    def body(g, carry):
        block = source_ref[:, g].reshape(rows * GROUP, chan)
        lhs = nn(turn, block).astype(BF16)
        turned_ref[:, g] = lhs.reshape(rows, GROUP, chan)
        for s in range(rows // 8):
            correlate_set(lhs, pad, 8 * s, g, inv_root, corr_ref, 0, 2 * s * LANES)
        return carry

    for g in range(groups):
        body(g, 0)


def row_chunks(rim_lo, corr_ref, rim_hi, r, rows):
    pieces = []
    half = rows // 2
    for q in range(rows // PER):
        y = q * PER + r
        parts = []
        for c in range(q, q + POS):
            if c < 2:
                part = rim_lo[y, :, :, c * LANES : (c + 1) * LANES]
            elif c < 2 + rows // PER:
                part = corr_ref[y, :, :, (c - 2) * LANES : (c - 1) * LANES]
            else:
                at = c - 2 - rows // PER
                part = rim_hi[y - half, :, :, at * LANES : (at + 1) * LANES]
            parts.append(part.reshape(part.shape[0] * part.shape[1], LANES))
        pieces.append(jnp.concatenate(parts, axis=1))
    return jnp.concatenate(pieces, axis=0)


def outer_kernel(
    inv_root,
    pixels,
    parts,
    turned_ref,
    corr_ref,
    across_ref,
    beyond_ref,
    wide_ref,
    bias_ref,
    head_ref,
    *rest,
):
    gate_ref = rest[0]
    piece_refs = rest[1 : 1 + parts]
    pad, rim_lo, rim_hi, stage = rest[1 + parts :]
    rows, groups, _, chan = turned_ref.shape
    half = rows // 2
    fill_halos(pad, 0, 8, across_ref, beyond_ref, parts)

    def body(g, carry):
        lhs = turned_ref[:half, g].reshape(half * GROUP, chan)
        correlate_set(lhs, pad, 0, g, inv_root, rim_lo, 0, 0)
        lhs = turned_ref[half:, g].reshape(half * GROUP, chan)
        correlate_set(lhs, pad, 8, g, inv_root, rim_hi, 0, 0)
        return carry

    for g in range(groups):
        body(g, 0)

    bias, head = bias_ref[...], head_ref[...]
    kout = bias.shape[1]
    cols = groups * GROUP
    turn = mirror(cols)
    hidden = jnp.zeros((1, kout), F32)
    slopes = jnp.zeros((1, kout), F32)
    total = None
    for r in range(PER):
        corr = row_chunks(rim_lo, corr_ref, rim_hi, r, rows)
        value = nt(corr, wide_ref[r]) + bias
        gating = jax.nn.sigmoid(value)
        act = value * gating
        slope = gating * (1.0 + value * (1.0 - gating))
        hidden = hidden + jnp.sum(act, axis=0, keepdims=True)
        slopes = slopes + jnp.sum(slope, axis=0, keepdims=True)
        pre = (slope * head).astype(BF16)
        for q in range(rows // PER):
            gate_ref[q * PER + r] = nn(turn, pre[q * cols : (q + 1) * cols]).astype(BF16)
        grad = tn(pre, corr)
        if r:
            grad = pltpu.roll(grad, POS * LANES - r * WIN, 1)
        total = grad if total is None else total + grad
    share = stage.shape[0] // parts
    table = spread_table(stage.shape[0])
    first = total.astype(BF16)
    left = total - first.astype(F32)
    second = left.astype(BF16)
    third = (left - second.astype(F32)).astype(BF16)
    packed = nt(table, first) + nt(table, second) + nt(table, third)
    scale = 1.0 / pixels
    stage[...] = packed * scale
    stage[STAT : STAT + 1] = head * slopes * scale
    stage[STAT + 1 : STAT + 2] = hidden * scale
    score = jnp.sum(hidden * head, axis=1, keepdims=True) * scale
    me = lax.axis_index("space")
    for k in range(parts):
        start = pl.multiple_of(lax.rem(me + k, parts) * share, 8)
        piece_refs[k][:share] = stage[pl.ds(start, share), :]
        piece_refs[k][share:] = jnp.broadcast_to(score, (8, kout))


def back_chunks(gate_ref, wide_ref, r, rows, groups):
    quarter = rows // PER
    lhs = jnp.concatenate([gate_ref[q * PER + r] for q in range(quarter)], axis=0)
    out = []
    for pos in range(POS):
        grad = nn(lhs, wide_ref[r, :, pos * LANES : (pos + 1) * LANES])
        grad = skew(grad.reshape(quarter * groups, GROUP, LANES), 0)
        out.append(grad.astype(BF16).reshape(quarter, groups, GROUP, LANES))
    return out


def rim_kernel(gate_ref, wide_ref, source_ref, across_ref, beyond_ref, band_lo, band_hi, sums):
    rows, groups, _, chan = source_ref.shape
    half = rows // 2
    quarter = rows // PER
    zero = jnp.zeros((groups, GROUP, LANES), BF16)
    for r in range(PER):
        for q in range(quarter):
            y = q * PER + r
            for c in (0, 1, 6, 7):
                pos = c - q
                band, row = (band_lo, y) if c < 2 else (band_hi, y - half)
                if not 0 <= row < half:
                    continue
                at = (c if c < 2 else c - 6) * LANES
                if 0 <= pos < POS:
                    grad = nn(gate_ref[y], wide_ref[r, :, pos * LANES : (pos + 1) * LANES])
                    part = skew(grad.reshape(groups, GROUP, LANES), 0).astype(BF16)
                else:
                    part = zero
                band[row, :, :, at : at + LANES] = part
    sums[...] = jnp.zeros(sums.shape, F32)

    def body(g, carry):
        start = g * GROUP
        for i, band in enumerate((band_lo, band_hi)):
            lhs = band[:, g].reshape(half * GROUP, 2 * LANES)
            rhs = source_ref[i * half : (i + 1) * half, g].reshape(half * GROUP, chan)
            grad = tn(lhs, rhs).reshape(8, WIN, chan)
            sums[8 * i : 8 * i + 8, start : start + WIN, :] += grad
        return carry

    for g in range(groups):
        body(g, 0)
    cols = groups * GROUP
    odd = lax.rem(lax.axis_index("space"), 2)
    low = pl.multiple_of(8 * odd, 8)
    high = pl.multiple_of(8 - 8 * odd, 8)
    across_ref[...] = sums[pl.ds(high, 8), RADIUS : RADIUS + cols].astype(BF16)
    beyond_ref[...] = sums[pl.ds(low, 8), RADIUS : RADIUS + cols].astype(BF16)


def back_kernel(
    parts,
    gate_ref,
    wide_ref,
    source_ref,
    edit_ref,
    across_ref,
    beyond_ref,
    source_out,
    edit_out,
    pad,
    band,
    sums,
):
    rows, groups, _, chan = source_ref.shape
    half = rows // 2
    quarter = rows // PER
    fill_halos(pad, 0, 8 + rows, across_ref, beyond_ref, parts)
    fill_padded(pad, 8, edit_ref)
    zero = jnp.zeros((PER, groups, GROUP, LANES), BF16)
    for q, c in ((1, 0), (3, 2), (0, 5), (2, 7)):
        band[q * PER : (q + 1) * PER, :, :, c * LANES : (c + 1) * LANES] = zero
    for r in range(PER):
        for pos, part in enumerate(back_chunks(gate_ref, wide_ref, r, rows, groups)):
            for q in range(quarter):
                at = (q + pos) * LANES
                band[q * PER + r, :, :, at : at + LANES] = part[q]
    sums[...] = jnp.zeros(sums.shape, F32)

    def body(g, carry):
        start = g * GROUP
        rhs = source_ref[:, g].reshape(rows * GROUP, chan)
        for s in range(rows // 8):
            at = (2 + 2 * s) * LANES
            lhs = band[:, g, :, at : at + 2 * LANES].reshape(rows * GROUP, 2 * LANES)
            grad = tn(lhs, rhs).reshape(8, WIN, chan)
            sums[8 * s : 8 * s + 8, start : start + WIN, :] += grad
        for i in range(2):
            at = i * 2 * LANES
            lhs = band[i * half : (i + 1) * half, g, :, at : at + 6 * LANES]
            grad = nn(lhs.reshape(half * GROUP, 6 * LANES), window(pad, 8 * i, 24, g))
            source_out[i * half : (i + 1) * half, g] = grad.reshape(half, GROUP, chan)
        return carry

    for g in range(groups):
        body(g, 0)
    cols = groups * GROUP
    edit_out[...] = sums[:, RADIUS : RADIUS + cols]


def judge_kernel(pairs, comp_ref, *rest):
    piece_refs = rest[:pairs]
    total_ref, grad_ref, loss_ref = rest[pairs:]
    share = total_ref.shape[0]
    me = lax.axis_index("pair")
    first, second, win = comp_ref[0:1], comp_ref[1:2], comp_ref[2:3]
    hots, margin = [], jnp.zeros(first.shape, F32)
    for k in range(pairs):
        pid = lax.rem(me - k + pairs, pairs)
        hot = (first == pid).astype(F32) - (second == pid).astype(F32)
        score = piece_refs[k][share : share + 1, 0:1]
        margin = margin + hot * score
        hots.append(hot)
    sign = 2.0 * win.astype(F32) - 1.0
    loss = jnp.mean(jax.nn.softplus(-sign * margin), axis=1, keepdims=True)
    loss_ref[...] = jnp.broadcast_to(loss, loss_ref.shape)
    margin_grad = -sign * jax.nn.sigmoid(-sign * margin)
    total = jnp.zeros(total_ref.shape, F32)
    for k in range(pairs):
        grad = jnp.sum(margin_grad * hots[k], axis=1, keepdims=True)
        if k == 0:
            grad_ref[...] = jnp.broadcast_to(grad, grad_ref.shape)
        total = total + grad * piece_refs[k][:share]
    total_ref[...] = total


def gather_kernel(parts, *rest):
    piece_refs = rest[:parts]
    conv_ref, bias_ref, head_ref, stage = rest[parts:]
    share = piece_refs[0].shape[0]
    me = lax.axis_index("space")
    for k in range(parts):
        start = pl.multiple_of(lax.rem(me - k + parts, parts) * share, 8)
        stage[pl.ds(start, share), :] = piece_refs[k][...]
    conv_ref[...] = stage[: conv_ref.shape[0]]
    bias_ref[...] = stage[STAT : STAT + 1]
    head_ref[...] = stage[STAT + 1 : STAT + 2]


def finish_kernel(
    inv_root, parts, grad_ref, source_ref, edit_ref, across_ref, beyond_ref, source_out, edit_out
):
    scale = grad_ref[0:1, 0:1].reshape(1, 1, 1) * inv_root
    source_out[...] = (source_ref[...] * scale).astype(BF16)
    rows = edit_ref.shape[0]
    me = lax.axis_index("space")
    odd = lax.rem(me, 2) == 1
    for row, edge, mine in ((0, 0, odd), (rows - 8, parts - 1, ~odd)):
        own = edit_ref[row : row + 8]
        for picked, ref in ((mine, across_ref), (~mine, beyond_ref)):

            @pl.when((me != edge) & picked)
            def _():
                edit_out[row : row + 8] = ((own + ref[...].astype(F32)) * scale).astype(BF16)

        @pl.when(me == edge)
        def _():
            edit_out[row : row + 8] = (own * scale).astype(BF16)


def call(kernel, outs, scratch, flops, *args):
    nbytes = sum(a.size * a.dtype.itemsize for a in args)
    return pl.pallas_call(
        kernel,
        out_shape=outs,
        in_specs=[pl.BlockSpec(memory_space=pltpu.VMEM)] * len(args),
        scratch_shapes=scratch,
        compiler_params=pltpu.CompilerParams(vmem_limit_bytes=VMEM_LIMIT),
        cost_estimate=pl.CostEstimate(flops=flops, bytes_accessed=nbytes, transcendentals=0),
    )(*(pltpu.with_memory_space_constraint(a, pltpu.VMEM) for a in args))


def result(dims, dtype=F32):
    return jax.ShapeDtypeStruct(dims, dtype)


def shape(dims, dtype=F32):
    return pltpu.VMEM(dims, dtype)


def around(axis, step):
    count = lax.axis_size(axis)
    return [(i, (i + step) % count) for i in range(count)]


def local(
    source_feats, edit_feats, conv_weight, conv_bias, head_weight, comp_first, comp_second, comp_win
):
    _, rows, columns, chan = source_feats.shape
    kout, disp = conv_weight.shape
    inv_root = chan ** (-0.5)
    space, pairs = lax.axis_size("space"), lax.axis_size("pair")
    pixels = rows * space * columns
    groups = columns // GROUP
    wide_cols = columns + 2 * RADIUS
    share = -(-(disp + 2) // (8 * space)) * 8
    edit = edit_feats[0]
    source = source_feats.reshape(rows, groups, GROUP, chan)
    odd = lax.rem(lax.axis_index("space"), 2)
    to_across = [(i, i ^ 1 if i ^ 1 < space else i) for i in range(space)]
    to_beyond = [(i, b if 0 <= (b := i + 1 - 2 * ((i + 1) % 2)) < space else i) for i in range(space)]
    edge_rows = rows - RADIUS
    across = lax.dynamic_slice_in_dim(edit, edge_rows * (1 - odd), RADIUS, 0)
    beyond = lax.dynamic_slice_in_dim(edit, edge_rows * odd, RADIUS, 0)
    across = lax.ppermute(across, "space", to_across)
    beyond = lax.ppermute(beyond, "space", to_beyond)
    turned, corr, wide = call(
        functools.partial(inner_kernel, inv_root),
        (
            shape((rows, groups, GROUP, chan), BF16),
            shape((rows, groups, GROUP, rows * WIN), BF16),
            shape((PER, kout, POS * LANES), BF16),
        ),
        [pltpu.VMEM((rows, wide_cols, chan), BF16)],
        2 * 10**9,
        source,
        edit,
        conv_weight.T,
    )
    gate, *pieces = call(
        functools.partial(outer_kernel, inv_root, pixels, space),
        (shape((rows, columns, kout), BF16),) + (shape((share + 8, kout)),) * space,
        [
            pltpu.VMEM((2 * RADIUS, wide_cols, chan), BF16),
            pltpu.VMEM((rows // 2, groups, GROUP, 8 * WIN), BF16),
            pltpu.VMEM((rows // 2, groups, GROUP, 8 * WIN), BF16),
            pltpu.VMEM((share * space, kout), F32),
        ],
        2 * 10**9,
        turned,
        corr,
        across,
        beyond,
        wide,
        conv_bias[None],
        head_weight[None],
    )
    quarter = pieces[0]
    for k in range(1, space):
        quarter = quarter + lax.ppermute(pieces[k], "space", around("space", k))
    rim_across, rim_beyond = call(
        rim_kernel,
        (shape((RADIUS, columns, chan), BF16),) * 2,
        [
            pltpu.VMEM((rows // 2, groups, GROUP, 8 * WIN), BF16),
            pltpu.VMEM((rows // 2, groups, GROUP, 8 * WIN), BF16),
            pltpu.VMEM((2 * RADIUS, wide_cols, chan), F32),
        ],
        10**9,
        gate,
        wide,
        source,
    )
    from_across = lax.ppermute(rim_across, "space", to_across)
    from_beyond = lax.ppermute(rim_beyond, "space", to_beyond)
    source_sum, edit_sum = call(
        functools.partial(back_kernel, space),
        (shape((rows, groups, GROUP, chan)), shape((rows, columns, chan))),
        [
            pltpu.VMEM((rows + 2 * RADIUS, wide_cols, chan), BF16),
            pltpu.VMEM((rows, groups, GROUP, (rows + 2 * RADIUS) * WIN), BF16),
            pltpu.VMEM((rows, wide_cols, chan), F32),
        ],
        4 * 10**9,
        gate,
        wide,
        source,
        edit,
        across,
        beyond,
    )
    others = [quarter] + [lax.ppermute(quarter, "pair", around("pair", k)) for k in range(1, pairs)]
    comps = jnp.stack([comp_first, comp_second, comp_win])
    total, score_grad, loss = call(
        functools.partial(judge_kernel, pairs),
        (shape((share, kout)), shape((8, LANES)), shape((1, LANES))),
        [],
        10**6,
        comps,
        *others,
    )
    gathered = [total] + [lax.ppermute(total, "space", around("space", k)) for k in range(1, space)]
    source_grad, edit_grad = call(
        functools.partial(finish_kernel, inv_root, space),
        (result((rows, columns, chan), BF16),) * 2,
        [],
        10**7,
        score_grad,
        source_sum.reshape(rows, columns, chan),
        edit_sum,
        from_across,
        from_beyond,
    )
    conv_grad, bias_grad, head_grad = call(
        functools.partial(gather_kernel, space),
        (result((disp, kout)), result((1, kout)), result((1, kout))),
        [pltpu.VMEM((share * space, kout), F32)],
        10**6,
        *gathered,
    )
    return (
        source_grad[None],
        edit_grad[None],
        conv_grad.T,
        bias_grad[0],
        head_grad[0],
        loss[0, :1],
    )


def solution(mesh):
    in_specs = (
        P(("groups", "pair"), "space", None, None),
        P(("groups", "pair"), "space", None, None),
        P(),
        P(),
        P(),
        P("groups"),
        P("groups"),
        P("groups"),
    )
    out_specs = (
        P(("groups", "pair"), "space", None, None),
        P(("groups", "pair"), "space", None, None),
        P("groups", None),
        P("groups"),
        P("groups"),
        P("groups"),
    )
    return jax.shard_map(local, mesh=mesh, in_specs=in_specs, out_specs=out_specs, check_vma=False)
```

```python
import functools

import jax
import jax.numpy as jnp
from jax import lax
from jax.experimental import pallas as pl
from jax.experimental.pallas import tpu as pltpu
from jax.sharding import PartitionSpec as P

RADIUS = 8
SPAN = 2 * RADIUS + 1
GROUP = 16
WIN = GROUP + 2 * RADIUS
LANES = 128
PER = LANES // WIN
POS = 5
STAT = SPAN * SPAN
F32 = jnp.float32
BF16 = jnp.bfloat16
VMEM_LIMIT = 24 * 1024 * 1024


def nt(a, b):
    return lax.dot_general(a, b, (((1,), (1,)), ((), ())), preferred_element_type=F32)


def nn(a, b):
    return lax.dot_general(a, b, (((1,), (0,)), ((), ())), preferred_element_type=F32)


def tn(a, b):
    return lax.dot_general(a, b, (((0,), (0,)), ((), ())), preferred_element_type=F32)


def iota(shape, dim):
    return lax.broadcasted_iota(jnp.int32, shape, dim)


def mirror(size):
    row, col = iota((size, size), 0), iota((size, size), 1)
    return (col == (row ^ (GROUP - 1))).astype(F32).astype(BF16)


def spread_table(rows):
    row, lane = iota((rows, POS * LANES), 0), iota((rows, POS * LANES), 1)
    dy, t = lane // WIN, lane % WIN
    hit = (row == dy * SPAN + t) & (t < SPAN) & (dy < SPAN)
    return hit.astype(F32).astype(BF16)


def skew(values, shift):
    return pltpu.roll(values, shift, 2, stride=1, stride_axis=1)


def skew_wide(values, shift):
    parts = []
    for start in range(0, values.shape[-1], LANES):
        parts.append(skew(values[:, :, start : start + LANES], shift))
    return parts


def fill_columns(pad_ref, row, rows, cols):
    zero = jnp.zeros((rows, RADIUS, pad_ref.shape[2]), BF16)
    pad_ref[row : row + rows, 0:RADIUS] = zero
    pad_ref[row : row + rows, RADIUS + cols :] = zero


def fill_padded(pad_ref, row, block_ref):
    rows, cols = block_ref.shape[:2]
    fill_columns(pad_ref, row, rows, cols)
    pad_ref[row : row + rows, RADIUS : RADIUS + cols] = block_ref[...]


def window(pad_ref, row, rows, g):
    block = pad_ref[row : row + rows, g * GROUP : g * GROUP + WIN, :]
    return block.reshape(rows * WIN, block.shape[2])


def correlate_set(lhs, pad_ref, row, g, inv_root, out_ref, spot, lane):
    ys = lhs.shape[0] // GROUP
    scores = nt(lhs, window(pad_ref, row, 8, g)) * inv_root
    scores = scores.reshape(ys, GROUP, 8 * WIN)
    for i, part in enumerate(skew_wide(scores, LANES - GROUP + 1)):
        at = lane + i * LANES
        out_ref[spot, g, :, at : at + LANES] = part.astype(BF16)


def inner_kernel(
    inv_root,
    source_ref,
    edit_ref,
    weight_ref,
    turned_ref,
    corr_ref,
    wide_ref,
    pad,
    weight,
    weight_sem,
):
    rows, groups, _, chan = source_ref.shape
    copy = pltpu.make_async_copy(weight_ref, weight, weight_sem)
    copy.start()
    fill_padded(pad, 0, edit_ref)
    turn = mirror(rows * GROUP)

    def body(g, carry):
        block = source_ref[:, g].reshape(rows * GROUP, chan)
        lhs = nn(turn, block).astype(BF16)
        turned_ref[:, g] = lhs.reshape(rows, GROUP, chan)
        for s in range(rows // 8):
            correlate_set(lhs, pad, 8 * s, g, inv_root, corr_ref, slice(0, rows), 2 * s * LANES)
        return carry

    for g in range(groups):
        body(g, 0)
    copy.wait()
    base = tn(weight[...], spread_table(SPAN * SPAN))
    for r in range(PER):
        wide_ref[r] = (base if r == 0 else pltpu.roll(base, r * WIN, 1)).astype(BF16)


def edge_spot(parts, kind):
    me = lax.axis_index("space")
    above = lax.rem(me, 2) ^ 1 if kind == 0 else lax.rem(me, 2)
    inside = jnp.where(above == 1, me != parts - 1, me != 0)
    return above, inside


def fill_halo(pad_ref, row, halo_ref, inside):
    cols = halo_ref.shape[1]
    pad_ref[pl.ds(row, 8), RADIUS : RADIUS + cols] = jnp.where(
        inside, halo_ref[...], jnp.zeros(halo_ref.shape, BF16)
    )


def rim_scores(inv_root, parts, kind, turned_ref, halo_ref, pad, rim_ref):
    rows, groups, _, chan = turned_ref.shape
    half = rows // 2
    above, inside = edge_spot(parts, kind)
    fill_columns(pad, 0, 8, groups * GROUP)
    fill_halo(pad, 0, halo_ref, inside)
    start = half * above
    for g in range(groups):
        lhs = turned_ref[pl.ds(start, half), g].reshape(half * GROUP, chan)
        correlate_set(lhs, pad, 0, g, inv_root, rim_ref, slice(0, half), 0)
    return above


def across_kernel(inv_root, parts, turned_ref, halo_ref, rim_ref, pad):
    rim_scores(inv_root, parts, 0, turned_ref, halo_ref, pad, rim_ref)


def slice_kernel(edit_ref, across_ref, beyond_ref, sems):
    rows = edit_ref.shape[0]
    odd = lax.rem(lax.axis_index("space"), 2)
    copies = []
    for i, (start, ref) in enumerate(((odd, beyond_ref), (1 - odd, across_ref))):
        block = edit_ref.at[pl.ds((rows - RADIUS) * start, RADIUS)]
        copies.append(pltpu.make_async_copy(block, ref, sems.at[i]))
        copies[i].start()
    for copy in copies:
        copy.wait()


def row_chunks(rims, corr_ref, r, rows):
    pieces = []
    half = rows // 2
    for q in range(rows // PER):
        y = q * PER + r
        parts = []
        for c in range(q, q + POS):
            if c < 2:
                part = rims[0, y, :, :, c * LANES : (c + 1) * LANES]
            elif c < 2 + rows // PER:
                part = corr_ref[y, :, :, (c - 2) * LANES : (c - 1) * LANES]
            else:
                at = c - 2 - rows // PER
                part = rims[1, y - half, :, :, at * LANES : (at + 1) * LANES]
            parts.append(part.reshape(part.shape[0] * part.shape[1], LANES))
        pieces.append(jnp.concatenate(parts, axis=1))
    return jnp.concatenate(pieces, axis=0)


def outer_kernel(
    inv_root,
    pixels,
    parts,
    turned_ref,
    corr_ref,
    rim_ref,
    beyond_ref,
    wide_ref,
    bias_ref,
    head_ref,
    *rest,
):
    gate_ref = rest[0]
    piece_refs = rest[1 : 1 + parts]
    pad, rims, stage = rest[1 + parts :]
    rows, groups = turned_ref.shape[:2]
    above, _ = edge_spot(parts, 1)
    rims[1 - above] = rim_ref[...]
    rim_scores(inv_root, parts, 1, turned_ref, beyond_ref, pad, rims.at[above])
    bias, head = bias_ref[...], head_ref[...]
    kout = bias.shape[1]
    cols = groups * GROUP
    turn = mirror(cols)
    hidden = jnp.zeros((1, kout), F32)
    slopes = jnp.zeros((1, kout), F32)
    total = None
    for r in range(PER):
        corr = row_chunks(rims, corr_ref, r, rows)
        value = nt(corr, wide_ref[r]) + bias
        gating = jax.nn.sigmoid(value)
        act = value * gating
        slope = gating * (1.0 + value * (1.0 - gating))
        hidden = hidden + jnp.sum(act, axis=0, keepdims=True)
        slopes = slopes + jnp.sum(slope, axis=0, keepdims=True)
        pre = (slope * head).astype(BF16)
        for q in range(rows // PER):
            gate_ref[q * PER + r] = nn(turn, pre[q * cols : (q + 1) * cols]).astype(BF16)
        grad = tn(pre, corr)
        if r:
            grad = pltpu.roll(grad, POS * LANES - r * WIN, 1)
        total = grad if total is None else total + grad
    share = stage.shape[0] // parts
    table = spread_table(stage.shape[0])
    first = total.astype(BF16)
    left = total - first.astype(F32)
    second = left.astype(BF16)
    third = (left - second.astype(F32)).astype(BF16)
    packed = nt(table, first) + nt(table, second) + nt(table, third)
    scale = 1.0 / pixels
    stage[...] = packed * scale
    stage[STAT : STAT + 1] = head * slopes * scale
    stage[STAT + 1 : STAT + 2] = hidden * scale
    score = jnp.sum(hidden * head, axis=1, keepdims=True) * scale
    me = lax.axis_index("space")
    for k in range(parts):
        start = pl.multiple_of(lax.rem(me + k, parts) * share, 8)
        piece_refs[k][:share] = stage[pl.ds(start, share), :]
        piece_refs[k][share:] = jnp.broadcast_to(score, (8, kout))


def back_chunks(gate_ref, wide_ref, r, rows, groups):
    quarter = rows // PER
    lhs = jnp.concatenate([gate_ref[q * PER + r] for q in range(quarter)], axis=0)
    out = []
    for pos in range(POS):
        grad = nn(lhs, wide_ref[r, :, pos * LANES : (pos + 1) * LANES])
        grad = skew(grad.reshape(quarter * groups, GROUP, LANES), 0)
        out.append(grad.astype(BF16).reshape(quarter, groups, GROUP, LANES))
    return out


def rim_kernel(gate_ref, wide_ref, source_ref, across_ref, beyond_ref, band_lo, band_hi, sums):
    rows, groups, _, chan = source_ref.shape
    half = rows // 2
    quarter = rows // PER
    zero = jnp.zeros((groups, GROUP, LANES), BF16)
    for r in range(PER):
        for q in range(quarter):
            y = q * PER + r
            for c in (0, 1, 6, 7):
                pos = c - q
                band, row = (band_lo, y) if c < 2 else (band_hi, y - half)
                if not 0 <= row < half:
                    continue
                at = (c if c < 2 else c - 6) * LANES
                if 0 <= pos < POS:
                    grad = nn(gate_ref[y], wide_ref[r, :, pos * LANES : (pos + 1) * LANES])
                    part = skew(grad.reshape(groups, GROUP, LANES), 0).astype(BF16)
                else:
                    part = zero
                band[row, :, :, at : at + LANES] = part
    sums[...] = jnp.zeros(sums.shape, F32)

    def body(g, carry):
        start = g * GROUP
        for i, band in enumerate((band_lo, band_hi)):
            lhs = band[:, g].reshape(half * GROUP, 2 * LANES)
            rhs = source_ref[i * half : (i + 1) * half, g].reshape(half * GROUP, chan)
            grad = tn(lhs, rhs).reshape(8, WIN, chan)
            sums[8 * i : 8 * i + 8, start : start + WIN, :] += grad
        return carry

    for g in range(groups):
        body(g, 0)
    cols = groups * GROUP
    odd = lax.rem(lax.axis_index("space"), 2)
    low = pl.multiple_of(8 * odd, 8)
    high = pl.multiple_of(8 - 8 * odd, 8)
    across_ref[...] = sums[pl.ds(high, 8), RADIUS : RADIUS + cols].astype(BF16)
    beyond_ref[...] = sums[pl.ds(low, 8), RADIUS : RADIUS + cols].astype(BF16)


def back_kernel(
    parts,
    gate_ref,
    wide_ref,
    source_ref,
    edit_ref,
    across_ref,
    beyond_ref,
    source_out,
    edit_out,
    pad,
    band,
    sums,
):
    rows, groups, _, chan = source_ref.shape
    half = rows // 2
    quarter = rows // PER
    for kind, ref in ((0, across_ref), (1, beyond_ref)):
        above, inside = edge_spot(parts, kind)
        fill_halo(pad, (8 + rows) * above, ref, inside)
    fill_columns(pad, 0, 16 + rows, groups * GROUP)
    pad[8 : 8 + rows, RADIUS : RADIUS + groups * GROUP] = edit_ref[...]
    zero = jnp.zeros((PER, groups, GROUP, LANES), BF16)
    for q, c in ((1, 0), (3, 2), (0, 5), (2, 7)):
        band[q * PER : (q + 1) * PER, :, :, c * LANES : (c + 1) * LANES] = zero
    for r in range(PER):
        for pos, part in enumerate(back_chunks(gate_ref, wide_ref, r, rows, groups)):
            for q in range(quarter):
                at = (q + pos) * LANES
                band[q * PER + r, :, :, at : at + LANES] = part[q]
    sums[...] = jnp.zeros(sums.shape, F32)

    def body(g, carry):
        start = g * GROUP
        rhs = source_ref[:, g].reshape(rows * GROUP, chan)
        for s in range(rows // 8):
            at = (2 + 2 * s) * LANES
            lhs = band[:, g, :, at : at + 2 * LANES].reshape(rows * GROUP, 2 * LANES)
            grad = tn(lhs, rhs).reshape(8, WIN, chan)
            sums[8 * s : 8 * s + 8, start : start + WIN, :] += grad
        for i in range(2):
            at = i * 2 * LANES
            lhs = band[i * half : (i + 1) * half, g, :, at : at + 6 * LANES]
            grad = nn(lhs.reshape(half * GROUP, 6 * LANES), window(pad, 8 * i, 24, g))
            source_out[i * half : (i + 1) * half, g] = grad.reshape(half, GROUP, chan)
        return carry

    for g in range(groups):
        body(g, 0)
    cols = groups * GROUP
    edit_out[...] = sums[:, RADIUS : RADIUS + cols]


def judge_kernel(pairs, comp_ref, *rest):
    piece_refs = rest[:pairs]
    total_ref, grad_ref, loss_ref = rest[pairs:]
    share = total_ref.shape[0]
    me = lax.axis_index("pair")
    first, second, win = comp_ref[0:1], comp_ref[1:2], comp_ref[2:3]
    hots, margin = [], jnp.zeros(first.shape, F32)
    for k in range(pairs):
        pid = lax.rem(me - k + pairs, pairs)
        hot = (first == pid).astype(F32) - (second == pid).astype(F32)
        score = piece_refs[k][share : share + 1, 0:1]
        margin = margin + hot * score
        hots.append(hot)
    sign = 2.0 * win.astype(F32) - 1.0
    loss = jnp.mean(jax.nn.softplus(-sign * margin), axis=1, keepdims=True)
    loss_ref[...] = jnp.broadcast_to(loss, loss_ref.shape)
    margin_grad = -sign * jax.nn.sigmoid(-sign * margin)
    total = jnp.zeros(total_ref.shape, F32)
    for k in range(pairs):
        grad = jnp.sum(margin_grad * hots[k], axis=1, keepdims=True)
        if k == 0:
            grad_ref[...] = jnp.broadcast_to(grad, grad_ref.shape)
        total = total + grad * piece_refs[k][:share]
    total_ref[...] = total


def gather_kernel(parts, *rest):
    piece_refs = rest[:parts]
    loss_ref, conv_ref, bias_ref, head_ref, loss_out, stage = rest[parts:]
    loss_out[...] = loss_ref[...]
    share = piece_refs[0].shape[0]
    me = lax.axis_index("space")
    for k in range(parts):
        start = pl.multiple_of(lax.rem(me - k + parts, parts) * share, 8)
        stage[pl.ds(start, share), :] = piece_refs[k][...]
    conv_ref[...] = stage[: conv_ref.shape[0]]
    bias_ref[...] = stage[STAT : STAT + 1]
    head_ref[...] = stage[STAT + 1 : STAT + 2]


def finish_kernel(
    inv_root, parts, grad_ref, source_ref, edit_ref, across_ref, beyond_ref, source_out, edit_out
):
    scale = grad_ref[0:1, 0:1].reshape(1, 1, 1) * inv_root
    source_out[...] = (source_ref[...] * scale).astype(BF16)
    rows = edit_ref.shape[0]
    for kind, ref in ((0, across_ref), (1, beyond_ref)):
        above, inside = edge_spot(parts, kind)
        at = pl.ds((rows - 8) * above, 8)
        extra = jnp.where(inside, ref[...].astype(F32), 0.0)
        edit_out[at] = ((edit_ref[at] + extra) * scale).astype(BF16)


def call(kernel, outs, scratch, flops, *args, far=()):
    nbytes = sum(a.size * a.dtype.itemsize for a in args)
    spaces = [pltpu.HBM if i in far else pltpu.VMEM for i in range(len(args))]
    return pl.pallas_call(
        kernel,
        out_shape=outs,
        in_specs=[pl.BlockSpec(memory_space=space) for space in spaces],
        scratch_shapes=scratch,
        compiler_params=pltpu.CompilerParams(vmem_limit_bytes=VMEM_LIMIT),
        cost_estimate=pl.CostEstimate(flops=flops, bytes_accessed=nbytes, transcendentals=0),
    )(*map(pltpu.with_memory_space_constraint, args, spaces))


def result(dims, dtype=F32):
    return jax.ShapeDtypeStruct(dims, dtype)


def shape(dims, dtype=F32):
    return pltpu.VMEM(dims, dtype)


def around(axis, step):
    count = lax.axis_size(axis)
    return [(i, (i + step) % count) for i in range(count)]


def local(
    source_feats, edit_feats, conv_weight, conv_bias, head_weight, comp_first, comp_second, comp_win
):
    _, rows, columns, chan = source_feats.shape
    kout, disp = conv_weight.shape
    inv_root = chan ** (-0.5)
    space, pairs = lax.axis_size("space"), lax.axis_size("pair")
    pixels = rows * space * columns
    groups = columns // GROUP
    wide_cols = columns + 2 * RADIUS
    share = -(-(disp + 2) // (8 * space)) * 8
    edit = edit_feats[0]
    source = source_feats.reshape(rows, groups, GROUP, chan)
    to_across = [(i, i ^ 1 if i ^ 1 < space else i) for i in range(space)]
    to_beyond = [(i, b if 0 <= (b := i + 1 - 2 * ((i + 1) % 2)) < space else i) for i in range(space)]
    across, beyond = call(
        slice_kernel,
        (shape((RADIUS, columns, chan), BF16),) * 2,
        [pltpu.SemaphoreType.DMA((2,))],
        10**4,
        edit,
        far=(0,),
    )
    across = lax.ppermute(across, "space", to_across)
    beyond = lax.ppermute(beyond, "space", to_beyond)
    turned, corr, wide = call(
        functools.partial(inner_kernel, inv_root),
        (
            shape((rows, groups, GROUP, chan), BF16),
            shape((rows, groups, GROUP, rows * WIN), BF16),
            shape((PER, kout, POS * LANES), BF16),
        ),
        [
            pltpu.VMEM((rows, wide_cols, chan), BF16),
            pltpu.VMEM((disp, kout), BF16),
            pltpu.SemaphoreType.DMA,
        ],
        2 * 10**9,
        source,
        edit,
        conv_weight.T,
        far=(2,),
    )
    (rim,) = call(
        functools.partial(across_kernel, inv_root, space),
        (shape((rows // 2, groups, GROUP, 8 * WIN), BF16),),
        [pltpu.VMEM((RADIUS, wide_cols, chan), BF16)],
        10**9,
        turned,
        across,
    )
    gate, *pieces = call(
        functools.partial(outer_kernel, inv_root, pixels, space),
        (shape((rows, columns, kout), BF16),) + (shape((share + 8, kout)),) * space,
        [
            pltpu.VMEM((RADIUS, wide_cols, chan), BF16),
            pltpu.VMEM((2, rows // 2, groups, GROUP, 8 * WIN), BF16),
            pltpu.VMEM((share * space, kout), F32),
        ],
        2 * 10**9,
        turned,
        corr,
        rim,
        beyond,
        wide,
        conv_bias[None],
        head_weight[None],
    )
    quarter = pieces[0]
    for k in range(1, space):
        quarter = quarter + lax.ppermute(pieces[k], "space", around("space", k))
    rim_across, rim_beyond = call(
        rim_kernel,
        (shape((RADIUS, columns, chan), BF16),) * 2,
        [
            pltpu.VMEM((rows // 2, groups, GROUP, 8 * WIN), BF16),
            pltpu.VMEM((rows // 2, groups, GROUP, 8 * WIN), BF16),
            pltpu.VMEM((2 * RADIUS, wide_cols, chan), F32),
        ],
        10**9,
        gate,
        wide,
        source,
    )
    from_across = lax.ppermute(rim_across, "space", to_across)
    from_beyond = lax.ppermute(rim_beyond, "space", to_beyond)
    source_sum, edit_sum = call(
        functools.partial(back_kernel, space),
        (shape((rows, groups, GROUP, chan)), shape((rows, columns, chan))),
        [
            pltpu.VMEM((rows + 2 * RADIUS, wide_cols, chan), BF16),
            pltpu.VMEM((rows, groups, GROUP, (rows + 2 * RADIUS) * WIN), BF16),
            pltpu.VMEM((rows, wide_cols, chan), F32),
        ],
        4 * 10**9,
        gate,
        wide,
        source,
        edit,
        across,
        beyond,
    )
    others = [quarter] + [lax.ppermute(quarter, "pair", around("pair", k)) for k in range(1, pairs)]
    *others, source_sum, edit_sum = lax.optimization_barrier((*others, source_sum, edit_sum))
    comps = jnp.stack([comp_first, comp_second, comp_win])
    total, score_grad, loss = call(
        functools.partial(judge_kernel, pairs),
        (shape((share, kout)), shape((8, LANES)), shape((1, LANES))),
        [],
        10**6,
        comps,
        *others,
    )
    gathered = [total] + [lax.ppermute(total, "space", around("space", k)) for k in range(1, space)]
    source_grad, edit_grad = call(
        functools.partial(finish_kernel, inv_root, space),
        (result((rows, columns, chan), BF16),) * 2,
        [],
        10**7,
        score_grad,
        source_sum.reshape(rows, columns, chan),
        edit_sum,
        from_across,
        from_beyond,
    )
    *gathered, source_grad, edit_grad = lax.optimization_barrier((*gathered, source_grad, edit_grad))
    conv_grad, bias_grad, head_grad, loss = call(
        functools.partial(gather_kernel, space),
        (result((disp, kout)), result((1, kout)), result((1, kout)), result((1, LANES))),
        [pltpu.VMEM((share * space, kout), F32)],
        10**6,
        *gathered,
        loss,
    )
    return (
        source_grad[None],
        edit_grad[None],
        conv_grad.T,
        bias_grad[0],
        head_grad[0],
        loss[0, :1],
    )


def solution(mesh):
    in_specs = (
        P(("groups", "pair"), "space", None, None),
        P(("groups", "pair"), "space", None, None),
        P(),
        P(),
        P(),
        P("groups"),
        P("groups"),
        P("groups"),
    )
    out_specs = (
        P(("groups", "pair"), "space", None, None),
        P(("groups", "pair"), "space", None, None),
        P("groups", None),
        P("groups"),
        P("groups"),
        P("groups"),
    )
    return jax.shard_map(local, mesh=mesh, in_specs=in_specs, out_specs=out_specs, check_vma=False)
```

```python
import functools

import jax
import jax.numpy as jnp
from jax import lax
from jax.experimental import pallas as pl
from jax.experimental.pallas import tpu as pltpu
from jax.sharding import PartitionSpec as P

RADIUS = 8
SPAN = 2 * RADIUS + 1
GROUP = 16
WIN = GROUP + 2 * RADIUS
LANES = 128
PER = LANES // WIN
POS = 5
STAT = SPAN * SPAN
F32 = jnp.float32
BF16 = jnp.bfloat16
VMEM_LIMIT = 24 * 1024 * 1024


def nt(a, b):
    return lax.dot_general(a, b, (((1,), (1,)), ((), ())), preferred_element_type=F32)


def nn(a, b):
    return lax.dot_general(a, b, (((1,), (0,)), ((), ())), preferred_element_type=F32)


def tn(a, b):
    return lax.dot_general(a, b, (((0,), (0,)), ((), ())), preferred_element_type=F32)


def iota(shape, dim):
    return lax.broadcasted_iota(jnp.int32, shape, dim)


def mirror(size):
    row, col = iota((size, size), 0), iota((size, size), 1)
    return (col == (row ^ (GROUP - 1))).astype(F32).astype(BF16)


def spread(p):
    first = p * PER * SPAN
    return first // 8 * 8, first % 8


def spread_table(p, dim):
    _, offset = spread(p)
    count = (PER if p < POS - 1 else 1) * SPAN
    dims = [LANES, LANES]
    dims[dim] = -(-(count + offset) // 8) * 8 if p < POS - 1 else count
    place, lane = iota(dims, dim), iota(dims, 1 - dim)
    dy, t = lane // WIN, lane % WIN
    hit = (place == dy * SPAN + t + offset) & (t < SPAN) & (dy * SPAN < count)
    return hit.astype(F32).astype(BF16)


def skew(values, shift):
    return pltpu.roll(values, shift, 2, stride=1, stride_axis=1)


def skew_wide(values, shift):
    parts = []
    for start in range(0, values.shape[-1], LANES):
        parts.append(skew(values[:, :, start : start + LANES], shift))
    return parts


def fill_columns(pad_ref, row, rows, cols):
    zero = jnp.zeros((rows, RADIUS, pad_ref.shape[2]), BF16)
    pad_ref[row : row + rows, 0:RADIUS] = zero
    pad_ref[row : row + rows, RADIUS + cols :] = zero


def fill_padded(pad_ref, row, block_ref):
    rows, cols = block_ref.shape[:2]
    fill_columns(pad_ref, row, rows, cols)
    pad_ref[row : row + rows, RADIUS : RADIUS + cols] = block_ref[...]


def window(pad_ref, row, rows, g):
    block = pad_ref[row : row + rows, g * GROUP : g * GROUP + WIN, :]
    return block.reshape(rows * WIN, block.shape[2])


def correlate_set(lhs, pad_ref, row, g, inv_root, out_ref, spot, lane):
    ys = lhs.shape[0] // GROUP
    scores = nt(lhs, window(pad_ref, row, 8, g)) * inv_root
    scores = scores.reshape(ys, GROUP, 8 * WIN)
    for i, part in enumerate(skew_wide(scores, LANES - GROUP + 1)):
        at = lane + i * LANES
        out_ref[spot, g, :, at : at + LANES] = part.astype(BF16)


def spread_weights(weight, wide_ref, tall_ref):
    kout = weight.shape[1]
    wides, talls = [], []
    for p in range(POS):
        row, _ = spread(p)
        table = spread_table(p, 0)
        part = weight[row : row + table.shape[0], :]
        wides.append(tn(part, table))
        talls.append(nn(spread_table(p, 1), part))
    base = jnp.concatenate(wides, axis=1)
    tall = jnp.concatenate(talls, axis=0).astype(BF16)[: SPAN * WIN]
    tall_rows = tall_ref.shape[1]
    for r in range(PER):
        wide_ref[r] = (base if r == 0 else pltpu.roll(base, r * WIN, 1)).astype(BF16)
        start = LANES + r * WIN
        tall_ref[r, :start] = jnp.zeros((start, kout), BF16)
        tall_ref[r, start : start + SPAN * WIN] = tall
        tall_ref[r, start + SPAN * WIN :] = jnp.zeros((tall_rows - start - SPAN * WIN, kout), BF16)


def inner_kernel(
    inv_root,
    source_hbm,
    edit_hbm,
    weight_hbm,
    source_ref,
    pad,
    turned_ref,
    corr_ref,
    wide_ref,
    tall_ref,
    own_ref,
    weight,
    sems,
):
    rows, groups, _, chan = source_ref.shape
    weight_copy = pltpu.make_async_copy(weight_hbm, weight, sems.at[2])
    weight_copy.start()
    copies = []
    cols = groups * GROUP
    edit_copy = pltpu.make_async_copy(edit_hbm, pad.at[:, RADIUS : RADIUS + cols], sems.at[0])
    source_copy = pltpu.make_async_copy(source_hbm, source_ref, sems.at[1])
    edit_copy.start()
    source_copy.start()
    fill_columns(pad, 0, rows, groups * GROUP)
    turn = mirror(rows * GROUP)
    weight_copy.wait()
    spread_weights(weight, wide_ref, tall_ref)
    source_copy.wait()
    edit_copy.wait()
    for g in range(groups):
        lhs = nn(turn, source_ref[:, g].reshape(rows * GROUP, chan)).astype(BF16)
        turned_ref[:, g] = lhs.reshape(rows, GROUP, chan)
        for s in range(rows // 8):
            correlate_set(lhs, pad, 8 * s, g, inv_root, corr_ref, slice(0, rows), 2 * s * LANES)
    cols = groups * GROUP
    for q in range(rows // PER):
        start = (3 - q) * LANES
        for r in range(PER):
            lhs = corr_ref[q * PER + r].reshape(cols, 4 * LANES)
            own_ref[q * PER + r] = nn(lhs, tall_ref[r, start : start + 4 * LANES])


def edge_spot(parts, kind):
    me = lax.axis_index("space")
    above = lax.rem(me, 2) ^ 1 if kind == 0 else lax.rem(me, 2)
    inside = jnp.where(above == 1, me != parts - 1, me != 0)
    return above, inside


def fill_halo(pad_ref, row, halo_ref, inside):
    cols = halo_ref.shape[1]
    pad_ref[pl.ds(row, 8), RADIUS : RADIUS + cols] = jnp.where(
        inside, halo_ref[...], jnp.zeros(halo_ref.shape, BF16)
    )


def rim_scores(inv_root, parts, kind, turned_ref, halo_ref, pad, rim_ref):
    rows, groups, _, chan = turned_ref.shape
    half = rows // 2
    above, inside = edge_spot(parts, kind)
    fill_columns(pad, 0, 8, groups * GROUP)
    fill_halo(pad, 0, halo_ref, inside)
    start = half * above
    for g in range(groups):
        lhs = turned_ref[pl.ds(start, half), g].reshape(half * GROUP, chan)
        correlate_set(lhs, pad, 0, g, inv_root, rim_ref, slice(0, half), 0)
    return above


def rim_values(rim_ref, tall_ref, above, out_ref):
    half, groups, _, lanes = rim_ref.shape
    for i in range(half):
        q, r = i // PER, i % PER
        start = pl.multiple_of((1 - q) * LANES + above * 4 * LANES, LANES)
        lhs = rim_ref[i].reshape(groups * GROUP, lanes)
        out_ref[i] = nn(lhs, tall_ref[r, pl.ds(start, lanes), :])


def across_kernel(
    inv_root, parts, turned_ref, halo_ref, tall_ref, rim_ref, extra_ref, pad
):
    above = rim_scores(inv_root, parts, 0, turned_ref, halo_ref, pad, rim_ref)
    rim_values(rim_ref, tall_ref, above, extra_ref)


def slice_kernel(edit_ref, across_ref, beyond_ref, sems):
    rows = edit_ref.shape[0]
    odd = lax.rem(lax.axis_index("space"), 2)
    copies = []
    count = sems.shape[0] // 2
    step = RADIUS // count
    for start, ref in ((odd, beyond_ref), (1 - odd, across_ref)):
        for i in range(count):
            block = edit_ref.at[pl.ds((rows - RADIUS) * start + i * step, step)]
            copies.append(
                pltpu.make_async_copy(
                    block, ref.at[i * step : (i + 1) * step], sems.at[len(copies)]
                )
            )
            copies[-1].start()
    for copy in copies:
        copy.wait()


def row_chunks(rims, corr_ref, r, rows):
    pieces = []
    half = rows // 2
    for q in range(rows // PER):
        y = q * PER + r
        parts = []
        for c in range(q, q + POS):
            if c < 2:
                part = rims[0, y, :, :, c * LANES : (c + 1) * LANES]
            elif c < 2 + rows // PER:
                part = corr_ref[y, :, :, (c - 2) * LANES : (c - 1) * LANES]
            else:
                at = c - 2 - rows // PER
                part = rims[1, y - half, :, :, at * LANES : (at + 1) * LANES]
            parts.append(part.reshape(part.shape[0] * part.shape[1], LANES))
        pieces.append(jnp.concatenate(parts, axis=1))
    return jnp.concatenate(pieces, axis=0)


def outer_kernel(
    inv_root,
    pixels,
    parts,
    turned_ref,
    corr_ref,
    rim_ref,
    extra_ref,
    own_ref,
    beyond_ref,
    tall_ref,
    bias_ref,
    head_ref,
    *rest,
):
    gate_ref = rest[0]
    piece_refs = rest[1 : 1 + parts]
    pad, rims, extra, stage = rest[1 + parts :]
    rows, groups = turned_ref.shape[:2]
    above, _ = edge_spot(parts, 1)
    rims[1 - above] = rim_ref[...]
    extra[1 - above] = extra_ref[...]
    rim_scores(inv_root, parts, 1, turned_ref, beyond_ref, pad, rims.at[above])
    rim_values(rims.at[above], tall_ref, above, extra.at[above])
    bias, head = bias_ref[...], head_ref[...]
    kout = bias.shape[1]
    cols = groups * GROUP
    turn = mirror(cols)
    hidden = jnp.zeros((1, kout), F32)
    slopes = jnp.zeros((1, kout), F32)
    total = None
    for r in range(PER):
        corr = row_chunks(rims, corr_ref, r, rows)
        spots = [(q * PER + r, q // 2, q % 2 * PER + r) for q in range(rows // PER)]
        value = jnp.concatenate([own_ref[y] + extra[h, i] for y, h, i in spots], axis=0) + bias
        gating = jax.nn.sigmoid(value)
        act = value * gating
        slope = gating * (1.0 + value * (1.0 - gating))
        hidden = hidden + jnp.sum(act, axis=0, keepdims=True)
        slopes = slopes + jnp.sum(slope, axis=0, keepdims=True)
        pre = (slope * head).astype(BF16)
        for q in range(rows // PER):
            gate_ref[q * PER + r] = nn(turn, pre[q * cols : (q + 1) * cols]).astype(BF16)
        grad = tn(pre, corr)
        if r:
            grad = pltpu.roll(grad, POS * LANES - r * WIN, 1)
        total = grad if total is None else total + grad
    share = stage.shape[0] // parts
    stage[...] = jnp.zeros(stage.shape, F32)
    for p in range(POS):
        row, _ = spread(p)
        table = spread_table(p, 0)
        left = total[:, p * LANES : (p + 1) * LANES]
        packed = None
        for _ in range(3):
            term = left.astype(BF16)
            left = left - term.astype(F32)
            part = nt(table, term)
            packed = part if packed is None else packed + part
        stage[row : row + table.shape[0]] += packed
    scale = 1.0 / pixels
    stage[:STAT] = stage[:STAT] * scale
    stage[STAT : STAT + 1] = head * slopes * scale
    stage[STAT + 1 : STAT + 2] = hidden * scale
    score = jnp.sum(hidden * head, axis=1, keepdims=True) * scale
    me = lax.axis_index("space")
    for k in range(parts):
        start = pl.multiple_of(partner(me, k, parts) * share, 8)
        piece_refs[k][:share] = stage[pl.ds(start, share), :]
        piece_refs[k][share:] = jnp.broadcast_to(score, (8, kout))


def back_chunks(gate_ref, wide_ref, r, rows, groups):
    quarter = rows // PER
    lhs = jnp.concatenate([gate_ref[q * PER + r] for q in range(quarter)], axis=0)
    out = []
    for pos in range(POS):
        grad = nn(lhs, wide_ref[r, :, pos * LANES : (pos + 1) * LANES])
        grad = skew(grad.reshape(quarter * groups, GROUP, LANES), 0)
        out.append(grad.astype(BF16).reshape(quarter, groups, GROUP, LANES))
    return out


def rim_kernel(gate_ref, wide_ref, source_ref, across_ref, beyond_ref, band_lo, band_hi, sums):
    rows, groups, _, chan = source_ref.shape
    half = rows // 2
    quarter = rows // PER
    zero = jnp.zeros((groups, GROUP, LANES), BF16)
    for r in range(PER):
        for q in range(quarter):
            y = q * PER + r
            for c in (0, 1, 6, 7):
                pos = c - q
                band, row = (band_lo, y) if c < 2 else (band_hi, y - half)
                if not 0 <= row < half:
                    continue
                at = (c if c < 2 else c - 6) * LANES
                if 0 <= pos < POS:
                    grad = nn(gate_ref[y], wide_ref[r, :, pos * LANES : (pos + 1) * LANES])
                    part = skew(grad.reshape(groups, GROUP, LANES), 0).astype(BF16)
                else:
                    part = zero
                band[row, :, :, at : at + LANES] = part
    sums[...] = jnp.zeros(sums.shape, F32)

    def body(g, carry):
        start = g * GROUP
        for i, band in enumerate((band_lo, band_hi)):
            lhs = band[:, g].reshape(half * GROUP, 2 * LANES)
            rhs = source_ref[i * half : (i + 1) * half, g].reshape(half * GROUP, chan)
            grad = tn(lhs, rhs).reshape(8, WIN, chan)
            sums[8 * i : 8 * i + 8, start : start + WIN, :] += grad
        return carry

    for g in range(groups):
        body(g, 0)
    cols = groups * GROUP
    odd = lax.rem(lax.axis_index("space"), 2)
    low = pl.multiple_of(8 * odd, 8)
    high = pl.multiple_of(8 - 8 * odd, 8)
    across_ref[...] = sums[pl.ds(high, 8), RADIUS : RADIUS + cols].astype(BF16)
    beyond_ref[...] = sums[pl.ds(low, 8), RADIUS : RADIUS + cols].astype(BF16)


def back_kernel(
    parts,
    gate_ref,
    wide_ref,
    source_ref,
    own_pad,
    across_ref,
    beyond_ref,
    source_out,
    edit_out,
    pad,
    band,
    sums,
):
    rows, groups, _, chan = source_ref.shape
    half = rows // 2
    quarter = rows // PER
    for kind, ref in ((0, across_ref), (1, beyond_ref)):
        above, inside = edge_spot(parts, kind)
        fill_halo(pad, 8 * above, ref, inside)
    fill_columns(pad, 0, 16, groups * GROUP)
    zero = jnp.zeros((PER, groups, GROUP, LANES), BF16)
    for q, c in ((1, 0), (3, 2), (0, 5), (2, 7)):
        band[q * PER : (q + 1) * PER, :, :, c * LANES : (c + 1) * LANES] = zero
    for r in range(PER):
        for pos, part in enumerate(back_chunks(gate_ref, wide_ref, r, rows, groups)):
            for q in range(quarter):
                at = (q + pos) * LANES
                band[q * PER + r, :, :, at : at + LANES] = part[q]
    sums[...] = jnp.zeros(sums.shape, F32)

    def body(g, carry):
        start = g * GROUP
        near = source_ref[:, g].reshape(rows * GROUP, chan)
        for s in range(rows // 8):
            at = (2 + 2 * s) * LANES
            lhs = band[:, g, :, at : at + 2 * LANES].reshape(rows * GROUP, 2 * LANES)
            grad = tn(lhs, near).reshape(8, WIN, chan)
            sums[8 * s : 8 * s + 8, start : start + WIN, :] += grad
        for i in range(2):
            at = i * 2 * LANES
            lhs = band[i * half : (i + 1) * half, g, :, at : at + 6 * LANES]
            spots = [window(pad, 8 * i, 8, g), window(own_pad, 0, rows, g)]
            rhs = jnp.concatenate(spots[::-1] if i else spots, axis=0)
            grad = nn(lhs.reshape(half * GROUP, 6 * LANES), rhs)
            source_out[i * half : (i + 1) * half, g] = grad.reshape(half, GROUP, chan)
        return carry

    for g in range(groups):
        body(g, 0)
    cols = groups * GROUP
    edit_out[...] = sums[:, RADIUS : RADIUS + cols]


def partner(me, step, count):
    if count & (count - 1):
        return (me + step + count) % count
    return me ^ abs(step)


def judge_kernel(pairs, first_ref, second_ref, win_ref, *rest):
    piece_refs = rest[:pairs]
    total_ref, grad_ref, loss_ref = rest[pairs:]
    share = total_ref.shape[0]
    me = lax.axis_index("pair")
    first, second, win = first_ref[...], second_ref[...], win_ref[...]
    hots, margin = [], jnp.zeros(first.shape, F32)
    for k in range(pairs):
        pid = partner(me, -k, pairs)
        hot = (first == pid).astype(F32) - (second == pid).astype(F32)
        score = piece_refs[k][share : share + 1, 0:1]
        margin = margin + hot * score
        hots.append(hot)
    sign = 2.0 * win.astype(F32) - 1.0
    loss = jnp.mean(jax.nn.softplus(-sign * margin), axis=1, keepdims=True)
    loss_ref[...] = jnp.broadcast_to(loss, loss_ref.shape)
    margin_grad = -sign * jax.nn.sigmoid(-sign * margin)
    total = jnp.zeros(total_ref.shape, F32)
    for k in range(pairs):
        grad = jnp.sum(margin_grad * hots[k], axis=1, keepdims=True)
        if k == 0:
            grad_ref[...] = jnp.broadcast_to(grad, grad_ref.shape)
        total = total + grad * piece_refs[k][:share]
    total_ref[...] = total


def gather_kernel(parts, *rest):
    piece_refs = rest[:parts]
    loss_ref, conv_ref, bias_ref, head_ref, loss_out, stage = rest[parts:]
    loss_out[...] = loss_ref[...]
    share = piece_refs[0].shape[0]
    me = lax.axis_index("space")
    for k in range(parts):
        start = pl.multiple_of(partner(me, -k, parts) * share, 8)
        stage[pl.ds(start, share), :] = piece_refs[k][...]
    conv_ref[...] = stage[: conv_ref.shape[0]]
    bias_ref[...] = stage[STAT : STAT + 1]
    head_ref[...] = stage[STAT + 1 : STAT + 2]


def finish_kernel(
    inv_root,
    parts,
    grad_ref,
    source_ref,
    edit_ref,
    across_ref,
    beyond_ref,
    source_hbm,
    edit_hbm,
    source_out,
    edit_out,
    sems,
):
    scale = grad_ref[0:1, 0:1].reshape(1, 1, 1) * inv_root
    rows = edit_ref.shape[0]
    copies = []

    def send(out, hbm, at):
        copies.append(pltpu.make_async_copy(out.at[at], hbm.at[at], sems.at[len(copies)]))
        copies[-1].start()

    for y in range(0, rows, 4):
        at = slice(y, y + 4)
        source_out[at] = (source_ref[at] * scale).astype(BF16)
        send(source_out, source_hbm, at)
    for kind, ref in ((0, across_ref), (1, beyond_ref)):
        above, inside = edge_spot(parts, kind)
        for y in (0, 4):
            at = pl.ds((rows - 8) * above + y, 4)
            extra = jnp.where(inside, ref[y : y + 4].astype(F32), 0.0)
            edit_out[at] = ((edit_ref[at] + extra) * scale).astype(BF16)
            send(edit_out, edit_hbm, at)
    for copy in copies:
        copy.wait()


def call(kernel, outs, scratch, flops, *args, far=(), far_out=False):
    nbytes = sum(a.size * a.dtype.itemsize for a in args)
    spaces = [pltpu.HBM if i in far else pltpu.VMEM for i in range(len(args))]
    return pl.pallas_call(
        kernel,
        out_shape=outs,
        in_specs=[pl.BlockSpec(memory_space=space) for space in spaces],
        **({"out_specs": [pl.BlockSpec(memory_space=pltpu.HBM)] * len(outs)} if far_out else {}),
        scratch_shapes=scratch,
        compiler_params=pltpu.CompilerParams(vmem_limit_bytes=VMEM_LIMIT),
        cost_estimate=pl.CostEstimate(flops=flops, bytes_accessed=nbytes, transcendentals=0),
    )(*map(pltpu.with_memory_space_constraint, args, spaces))


def result(dims, dtype=F32):
    return jax.ShapeDtypeStruct(dims, dtype)


def shape(dims, dtype=F32):
    return pltpu.VMEM(dims, dtype)


def around(axis, step):
    count = lax.axis_size(axis)
    return [(i, partner(i, step, count)) for i in range(count)]


def local(
    source_feats, edit_feats, conv_weight, conv_bias, head_weight, comp_first, comp_second, comp_win
):
    _, rows, columns, chan = source_feats.shape
    kout, disp = conv_weight.shape
    inv_root = chan ** (-0.5)
    space, pairs = lax.axis_size("space"), lax.axis_size("pair")
    pixels = rows * space * columns
    groups = columns // GROUP
    wide_cols = columns + 2 * RADIUS
    share = -(-(disp + 2) // (8 * space)) * 8
    edit = edit_feats[0]
    source = source_feats.reshape(rows, groups, GROUP, chan)
    to_across = [(i, i ^ 1 if i ^ 1 < space else i) for i in range(space)]
    to_beyond = [(i, b if 0 <= (b := i + 1 - 2 * ((i + 1) % 2)) < space else i) for i in range(space)]
    across, beyond = call(
        slice_kernel,
        (shape((RADIUS, columns, chan), BF16),) * 2,
        [pltpu.SemaphoreType.DMA((2,))],
        10**4,
        edit,
        far=(0,),
    )
    across = lax.ppermute(across, "space", to_across)
    beyond = lax.ppermute(beyond, "space", to_beyond)
    near = (rows, groups, GROUP, chan)
    rim_shape = (rows // 2, groups, GROUP, 8 * WIN)
    held, own_pad, turned, corr, wide, tall, own = call(
        functools.partial(inner_kernel, inv_root),
        (
            shape(near, BF16),
            shape((rows, wide_cols, chan), BF16),
            shape(near, BF16),
            shape((rows, groups, GROUP, rows * WIN), BF16),
            shape((PER, kout, POS * LANES), BF16),
            shape((PER, (POS + 2) * LANES, kout), BF16),
            shape((rows, columns, kout)),
        ),
        [pltpu.VMEM((disp, kout), BF16), pltpu.SemaphoreType.DMA((3,))],
        2 * 10**9,
        source,
        edit,
        conv_weight.T,
        far=(0, 1, 2),
    )
    rim, extra = call(
        functools.partial(across_kernel, inv_root, space),
        (shape(rim_shape, BF16), shape((rows // 2, columns, kout))),
        [pltpu.VMEM((RADIUS, wide_cols, chan), BF16)],
        10**9,
        turned,
        across,
        tall,
    )
    gate, *pieces = call(
        functools.partial(outer_kernel, inv_root, pixels, space),
        (shape((rows, columns, kout), BF16),) + (shape((share + 8, kout)),) * space,
        [
            pltpu.VMEM((RADIUS, wide_cols, chan), BF16),
            pltpu.VMEM((2,) + rim_shape, BF16),
            pltpu.VMEM((2, rows // 2, columns, kout), F32),
            pltpu.VMEM((share * space, kout), F32),
        ],
        2 * 10**9,
        turned,
        corr,
        rim,
        extra,
        own,
        beyond,
        tall,
        conv_bias[None],
        head_weight[None],
    )
    quarter = pieces[0]
    for k in range(1, space):
        quarter = quarter + lax.ppermute(pieces[k], "space", around("space", k))
    rim_across, rim_beyond = call(
        rim_kernel,
        (shape((RADIUS, columns, chan), BF16),) * 2,
        [
            pltpu.VMEM((rows // 2, groups, GROUP, 8 * WIN), BF16),
            pltpu.VMEM((rows // 2, groups, GROUP, 8 * WIN), BF16),
            pltpu.VMEM((2 * RADIUS, wide_cols, chan), F32),
        ],
        10**9,
        gate,
        wide,
        held,
    )
    from_across = lax.ppermute(rim_across, "space", to_across)
    from_beyond = lax.ppermute(rim_beyond, "space", to_beyond)
    source_sum, edit_sum = call(
        functools.partial(back_kernel, space),
        (shape((rows, groups, GROUP, chan)), shape((rows, columns, chan))),
        [
            pltpu.VMEM((2 * RADIUS, wide_cols, chan), BF16),
            pltpu.VMEM((rows, groups, GROUP, (rows + 2 * RADIUS) * WIN), BF16),
            pltpu.VMEM((rows, wide_cols, chan), F32),
        ],
        4 * 10**9,
        gate,
        wide,
        held,
        own_pad,
        across,
        beyond,
    )
    others = [quarter] + [lax.ppermute(quarter, "pair", around("pair", k)) for k in range(1, pairs)]
    *others, source_sum, edit_sum = lax.optimization_barrier((*others, source_sum, edit_sum))
    total, score_grad, loss = call(
        functools.partial(judge_kernel, pairs),
        (shape((share, kout)), shape((8, LANES)), shape((1, LANES))),
        [],
        10**6,
        comp_first[None],
        comp_second[None],
        comp_win[None],
        *others,
    )
    gathered = [total] + [lax.ppermute(total, "space", around("space", k)) for k in range(1, space)]
    source_grad, edit_grad = call(
        functools.partial(finish_kernel, inv_root, space),
        (result((rows, columns, chan), BF16),) * 2,
        [
            pltpu.VMEM((rows, columns, chan), BF16),
            pltpu.VMEM((rows, columns, chan), BF16),
            pltpu.SemaphoreType.DMA((8,)),
        ],
        10**7,
        score_grad,
        source_sum.reshape(rows, columns, chan),
        edit_sum,
        from_across,
        from_beyond,
        far_out=True,
    )
    *gathered, source_grad, edit_grad = lax.optimization_barrier((*gathered, source_grad, edit_grad))
    conv_grad, bias_grad, head_grad, loss = call(
        functools.partial(gather_kernel, space),
        (result((disp, kout)), result((1, kout)), result((1, kout)), result((1, LANES))),
        [pltpu.VMEM((share * space, kout), F32)],
        10**6,
        *gathered,
        loss,
    )
    return (
        source_grad[None],
        edit_grad[None],
        conv_grad.T,
        bias_grad[0],
        head_grad[0],
        loss[0, :1],
    )


def solution(mesh):
    in_specs = (
        P(("groups", "pair"), "space", None, None),
        P(("groups", "pair"), "space", None, None),
        P(),
        P(),
        P(),
        P("groups"),
        P("groups"),
        P("groups"),
    )
    out_specs = (
        P(("groups", "pair"), "space", None, None),
        P(("groups", "pair"), "space", None, None),
        P("groups", None),
        P("groups"),
        P("groups"),
        P("groups"),
    )
    return jax.shard_map(local, mesh=mesh, in_specs=in_specs, out_specs=out_specs, check_vma=False)
```

```python
import functools

import jax
import jax.numpy as jnp
from jax import lax
from jax.experimental import pallas as pl
from jax.experimental.pallas import tpu as pltpu
from jax.sharding import PartitionSpec as P

RADIUS = 8
SPAN = 2 * RADIUS + 1
GROUP = 16
WIN = GROUP + 2 * RADIUS
LANES = 128
PER = LANES // WIN
POS = 5
STAT = SPAN * SPAN
F32 = jnp.float32
BF16 = jnp.bfloat16
VMEM_LIMIT = 24 * 1024 * 1024


def nt(a, b):
    return lax.dot_general(a, b, (((1,), (1,)), ((), ())), preferred_element_type=F32)


def nn(a, b):
    return lax.dot_general(a, b, (((1,), (0,)), ((), ())), preferred_element_type=F32)


def tn(a, b):
    return lax.dot_general(a, b, (((0,), (0,)), ((), ())), preferred_element_type=F32)


def iota(shape, dim):
    return lax.broadcasted_iota(jnp.int32, shape, dim)


def mirror(size):
    row, col = iota((size, size), 0), iota((size, size), 1)
    return (col == (row ^ (GROUP - 1))).astype(F32).astype(BF16)


def spread(p):
    first = p * PER * SPAN
    return first // 8 * 8, first % 8


def spread_table(p, dim):
    _, offset = spread(p)
    count = (PER if p < POS - 1 else 1) * SPAN
    dims = [LANES, LANES]
    dims[dim] = -(-(count + offset) // 8) * 8 if p < POS - 1 else count
    place, lane = iota(dims, dim), iota(dims, 1 - dim)
    dy, t = lane // WIN, lane % WIN
    hit = (place == dy * SPAN + t + offset) & (t < SPAN) & (dy * SPAN < count)
    return hit.astype(F32).astype(BF16)


def skew(values, shift):
    return pltpu.roll(values, shift, 2, stride=1, stride_axis=1)


def skew_wide(values, shift):
    parts = []
    for start in range(0, values.shape[-1], LANES):
        parts.append(skew(values[:, :, start : start + LANES], shift))
    return parts


def fill_columns(pad_ref, row, rows, cols):
    zero = jnp.zeros((rows, RADIUS, pad_ref.shape[2]), BF16)
    pad_ref[row : row + rows, 0:RADIUS] = zero
    pad_ref[row : row + rows, RADIUS + cols :] = zero


def fill_padded(pad_ref, row, block_ref):
    rows, cols = block_ref.shape[:2]
    fill_columns(pad_ref, row, rows, cols)
    pad_ref[row : row + rows, RADIUS : RADIUS + cols] = block_ref[...]


def window(pad_ref, row, rows, g):
    block = pad_ref[row : row + rows, g * GROUP : g * GROUP + WIN, :]
    return block.reshape(rows * WIN, block.shape[2])


def correlate_set(lhs, pad_ref, row, g, inv_root, out_ref, spot, lane):
    ys = lhs.shape[0] // GROUP
    scores = nt(lhs, window(pad_ref, row, 8, g)) * inv_root
    scores = scores.reshape(ys, GROUP, 8 * WIN)
    for i, part in enumerate(skew_wide(scores, LANES - GROUP + 1)):
        at = lane + i * LANES
        out_ref[spot, g, :, at : at + LANES] = part.astype(BF16)


def spread_weights(weight, wide_ref, tall_ref):
    kout = weight.shape[1]
    wides, talls = [], []
    for p in range(POS):
        row, _ = spread(p)
        table = spread_table(p, 0)
        part = weight[row : row + table.shape[0], :]
        wides.append(tn(part, table))
        talls.append(nn(spread_table(p, 1), part))
    base = jnp.concatenate(wides, axis=1)
    tall = jnp.concatenate(talls, axis=0).astype(BF16)[: SPAN * WIN]
    tall_rows = tall_ref.shape[1]
    for r in range(PER):
        wide_ref[r] = (base if r == 0 else pltpu.roll(base, r * WIN, 1)).astype(BF16)
        start = LANES + r * WIN
        tall_ref[r, :start] = jnp.zeros((start, kout), BF16)
        tall_ref[r, start : start + SPAN * WIN] = tall
        tall_ref[r, start + SPAN * WIN :] = jnp.zeros((tall_rows - start - SPAN * WIN, kout), BF16)


def inner_kernel(
    inv_root,
    source_hbm,
    edit_hbm,
    weight_hbm,
    source_ref,
    pad,
    turned_ref,
    corr_ref,
    wide_ref,
    tall_ref,
    own_ref,
    weight,
    sems,
):
    rows, groups, _, chan = source_ref.shape
    weight_copy = pltpu.make_async_copy(weight_hbm, weight, sems.at[2])
    weight_copy.start()
    copies = []
    cols = groups * GROUP
    edit_copy = pltpu.make_async_copy(edit_hbm, pad.at[:, RADIUS : RADIUS + cols], sems.at[0])
    source_copy = pltpu.make_async_copy(source_hbm, source_ref, sems.at[1])
    edit_copy.start()
    source_copy.start()
    fill_columns(pad, 0, rows, groups * GROUP)
    turn = mirror(rows * GROUP)
    weight_copy.wait()
    spread_weights(weight, wide_ref, tall_ref)
    source_copy.wait()
    edit_copy.wait()
    for g in range(groups):
        lhs = nn(turn, source_ref[:, g].reshape(rows * GROUP, chan)).astype(BF16)
        turned_ref[:, g] = lhs.reshape(rows, GROUP, chan)
        for s in range(rows // 8):
            correlate_set(lhs, pad, 8 * s, g, inv_root, corr_ref, slice(0, rows), 2 * s * LANES)
    cols = groups * GROUP
    for q in range(rows // PER):
        start = (3 - q) * LANES
        for r in range(PER):
            lhs = corr_ref[q * PER + r].reshape(cols, 4 * LANES)
            own_ref[q * PER + r] = nn(lhs, tall_ref[r, start : start + 4 * LANES])


def edge_spot(parts, kind):
    me = lax.axis_index("space")
    above = lax.rem(me, 2) ^ 1 if kind == 0 else lax.rem(me, 2)
    inside = jnp.where(above == 1, me != parts - 1, me != 0)
    return above, inside


def fill_halo(pad_ref, row, halo_ref, inside):
    cols = halo_ref.shape[1]
    pad_ref[pl.ds(row, 8), RADIUS : RADIUS + cols] = jnp.where(
        inside, halo_ref[...], jnp.zeros(halo_ref.shape, BF16)
    )


def rim_scores(inv_root, parts, kind, turned_ref, halo_ref, pad, rim_ref):
    rows, groups, _, chan = turned_ref.shape
    half = rows // 2
    above, inside = edge_spot(parts, kind)
    fill_columns(pad, 0, 8, groups * GROUP)
    fill_halo(pad, 0, halo_ref, inside)
    start = half * above
    for g in range(groups):
        lhs = turned_ref[pl.ds(start, half), g].reshape(half * GROUP, chan)
        correlate_set(lhs, pad, 0, g, inv_root, rim_ref, slice(0, half), 0)
    return above


def rim_values(rim_ref, tall_ref, above, out_ref):
    half, groups, _, lanes = rim_ref.shape
    for i in range(half):
        q, r = i // PER, i % PER
        start = pl.multiple_of((1 - q) * LANES + above * 4 * LANES, LANES)
        lhs = rim_ref[i].reshape(groups * GROUP, lanes)
        out_ref[i] = nn(lhs, tall_ref[r, pl.ds(start, lanes), :])


def across_kernel(
    inv_root, parts, turned_ref, halo_ref, tall_ref, rim_ref, extra_ref, pad
):
    above = rim_scores(inv_root, parts, 0, turned_ref, halo_ref, pad, rim_ref)
    rim_values(rim_ref, tall_ref, above, extra_ref)


def slice_kernel(edit_ref, across_ref, beyond_ref, sems):
    rows = edit_ref.shape[0]
    odd = lax.rem(lax.axis_index("space"), 2)
    copies = []
    count = sems.shape[0] // 2
    step = RADIUS // count
    for start, ref in ((odd, beyond_ref), (1 - odd, across_ref)):
        for i in range(count):
            block = edit_ref.at[pl.ds((rows - RADIUS) * start + i * step, step)]
            copies.append(
                pltpu.make_async_copy(
                    block, ref.at[i * step : (i + 1) * step], sems.at[len(copies)]
                )
            )
            copies[-1].start()
    for copy in copies:
        copy.wait()


def row_chunks(rims, corr_ref, r, rows):
    pieces = []
    half = rows // 2
    for q in range(rows // PER):
        y = q * PER + r
        parts = []
        for c in range(q, q + POS):
            if c < 2:
                part = rims[0, y, :, :, c * LANES : (c + 1) * LANES]
            elif c < 2 + rows // PER:
                part = corr_ref[y, :, :, (c - 2) * LANES : (c - 1) * LANES]
            else:
                at = c - 2 - rows // PER
                part = rims[1, y - half, :, :, at * LANES : (at + 1) * LANES]
            parts.append(part.reshape(part.shape[0] * part.shape[1], LANES))
        pieces.append(jnp.concatenate(parts, axis=1))
    return jnp.concatenate(pieces, axis=0)


def outer_kernel(
    inv_root,
    pixels,
    parts,
    turned_ref,
    corr_ref,
    rim_ref,
    extra_ref,
    own_ref,
    beyond_ref,
    tall_ref,
    bias_ref,
    head_ref,
    *rest,
):
    *out_refs, pad, rims, extra, stage = rest
    gate_ref, *piece_refs = out_refs
    rows, groups = turned_ref.shape[:2]
    above, _ = edge_spot(parts, 1)
    rims[1 - above] = rim_ref[...]
    extra[1 - above] = extra_ref[...]
    rim_scores(inv_root, parts, 1, turned_ref, beyond_ref, pad, rims.at[above])
    rim_values(rims.at[above], tall_ref, above, extra.at[above])
    bias, head = bias_ref[...], head_ref[...]
    kout = bias.shape[1]
    cols = groups * GROUP
    turn = mirror(cols)
    hidden = jnp.zeros((1, kout), F32)
    slopes = jnp.zeros((1, kout), F32)
    total = None
    for r in range(PER):
        corr = row_chunks(rims, corr_ref, r, rows)
        spots = [(q * PER + r, q // 2, q % 2 * PER + r) for q in range(rows // PER)]
        value = jnp.concatenate([own_ref[y] + extra[h, i] for y, h, i in spots], axis=0) + bias
        gating = jax.nn.sigmoid(value)
        act = value * gating
        slope = gating * (1.0 + value * (1.0 - gating))
        hidden = hidden + jnp.sum(act, axis=0, keepdims=True)
        slopes = slopes + jnp.sum(slope, axis=0, keepdims=True)
        pre = (slope * head).astype(BF16)
        for q in range(rows // PER):
            gate_ref[q * PER + r] = nn(turn, pre[q * cols : (q + 1) * cols]).astype(BF16)
        grad = tn(pre, corr)
        if r:
            grad = pltpu.roll(grad, POS * LANES - r * WIN, 1)
        total = grad if total is None else total + grad
    share = stage.shape[0] // parts
    stage[...] = jnp.zeros(stage.shape, F32)
    for p in range(POS):
        row, _ = spread(p)
        table = spread_table(p, 0)
        left = total[:, p * LANES : (p + 1) * LANES]
        packed = None
        for _ in range(3):
            term = left.astype(BF16)
            left = left - term.astype(F32)
            part = nt(table, term)
            packed = part if packed is None else packed + part
        stage[row : row + table.shape[0]] += packed
    scale = 1.0 / pixels
    stage[:STAT] = stage[:STAT] * scale
    stage[STAT : STAT + 1] = head * slopes * scale
    stage[STAT + 1 : STAT + 2] = hidden * scale
    score = jnp.sum(hidden * head, axis=1, keepdims=True) * scale
    me = lax.axis_index("space")
    for side, ref in enumerate(piece_refs):
        for i in range(ref.shape[0]):
            piece = i if parts == 1 else 2 * i + (lax.rem(me, 2) ^ side)
            start = pl.multiple_of(piece * share, 8)
            ref[i, :share] = stage[pl.ds(start, share), :]
            ref[i, share:] = jnp.broadcast_to(score, (8, kout))


def split_kernel(bit, keep_ref, came_ref, next_keep, next_send):
    mine = lax.rem(lax.axis_index("space") // bit, 2)
    for i in range(next_keep.shape[0]):
        for ref, at in ((next_keep, 2 * i + mine), (next_send, 2 * i + 1 - mine)):
            ref[i] = keep_ref[at] + came_ref[at]


def stack_kernel(first_ref, second_ref, out_ref):
    count = first_ref.shape[0]
    out_ref[:count] = first_ref[...]
    out_ref[count:] = second_ref[...]


def back_chunks(gate_ref, wide_ref, r, rows, groups):
    quarter = rows // PER
    lhs = jnp.concatenate([gate_ref[q * PER + r] for q in range(quarter)], axis=0)
    out = []
    for pos in range(POS):
        grad = nn(lhs, wide_ref[r, :, pos * LANES : (pos + 1) * LANES])
        grad = skew(grad.reshape(quarter * groups, GROUP, LANES), 0)
        out.append(grad.astype(BF16).reshape(quarter, groups, GROUP, LANES))
    return out


def rim_kernel(gate_ref, wide_ref, source_ref, across_ref, beyond_ref, band_lo, band_hi, sums):
    rows, groups, _, chan = source_ref.shape
    half = rows // 2
    quarter = rows // PER
    zero = jnp.zeros((groups, GROUP, LANES), BF16)
    for r in range(PER):
        for q in range(quarter):
            y = q * PER + r
            for c in (0, 1, 6, 7):
                pos = c - q
                band, row = (band_lo, y) if c < 2 else (band_hi, y - half)
                if not 0 <= row < half:
                    continue
                at = (c if c < 2 else c - 6) * LANES
                if 0 <= pos < POS:
                    grad = nn(gate_ref[y], wide_ref[r, :, pos * LANES : (pos + 1) * LANES])
                    part = skew(grad.reshape(groups, GROUP, LANES), 0).astype(BF16)
                else:
                    part = zero
                band[row, :, :, at : at + LANES] = part
    sums[...] = jnp.zeros(sums.shape, F32)

    def body(g, carry):
        start = g * GROUP
        for i, band in enumerate((band_lo, band_hi)):
            lhs = band[:, g].reshape(half * GROUP, 2 * LANES)
            rhs = source_ref[i * half : (i + 1) * half, g].reshape(half * GROUP, chan)
            grad = tn(lhs, rhs).reshape(8, WIN, chan)
            sums[8 * i : 8 * i + 8, start : start + WIN, :] += grad
        return carry

    for g in range(groups):
        body(g, 0)
    cols = groups * GROUP
    odd = lax.rem(lax.axis_index("space"), 2)
    low = pl.multiple_of(8 * odd, 8)
    high = pl.multiple_of(8 - 8 * odd, 8)
    across_ref[...] = sums[pl.ds(high, 8), RADIUS : RADIUS + cols].astype(BF16)
    beyond_ref[...] = sums[pl.ds(low, 8), RADIUS : RADIUS + cols].astype(BF16)


def edit_kernel(gate_ref, wide_ref, source_ref, band, edit_out, sums):
    rows, groups, _, chan = source_ref.shape
    quarter = rows // PER
    zero = jnp.zeros((PER, groups, GROUP, LANES), BF16)
    for q, c in ((1, 0), (3, 2), (0, 5), (2, 7)):
        band[q * PER : (q + 1) * PER, :, :, c * LANES : (c + 1) * LANES] = zero
    for r in range(PER):
        for pos, part in enumerate(back_chunks(gate_ref, wide_ref, r, rows, groups)):
            for q in range(quarter):
                at = (q + pos) * LANES
                band[q * PER + r, :, :, at : at + LANES] = part[q]
    sums[...] = jnp.zeros(sums.shape, F32)
    for g in range(groups):
        start = g * GROUP
        near = source_ref[:, g].reshape(rows * GROUP, chan)
        for s in range(rows // 8):
            at = (2 + 2 * s) * LANES
            lhs = band[:, g, :, at : at + 2 * LANES].reshape(rows * GROUP, 2 * LANES)
            grad = tn(lhs, near).reshape(8, WIN, chan)
            sums[8 * s : 8 * s + 8, start : start + WIN, :] += grad
    edit_out[...] = sums[:, RADIUS : RADIUS + groups * GROUP]


def source_kernel(parts, band, own_pad, across_ref, beyond_ref, source_out, pad):
    rows, groups, _, chan = source_out.shape
    half = rows // 2
    for kind, ref in ((0, across_ref), (1, beyond_ref)):
        above, inside = edge_spot(parts, kind)
        fill_halo(pad, 8 * above, ref, inside)
    fill_columns(pad, 0, 16, groups * GROUP)
    for g in range(groups):
        for i in range(2):
            at = i * 2 * LANES
            lhs = band[i * half : (i + 1) * half, g, :, at : at + 6 * LANES]
            spots = [window(pad, 8 * i, 8, g), window(own_pad, 0, rows, g)]
            rhs = jnp.concatenate(spots[::-1] if i else spots, axis=0)
            grad = nn(lhs.reshape(half * GROUP, 6 * LANES), rhs)
            source_out[i * half : (i + 1) * half, g] = grad.reshape(half, GROUP, chan)


def pieces_of(refs):
    return [ref.at[i] for ref in refs for i in range(ref.shape[0])]


def judge_kernel(pairs, first_ref, second_ref, win_ref, *rest):
    *came_refs, total_ref, grad_ref, loss_ref = rest
    share = total_ref.shape[1]
    me = lax.axis_index("pair")
    first, second, win = first_ref[...], second_ref[...], win_ref[...]
    hots, margin = [], jnp.zeros(first.shape, F32)
    pieces = pieces_of(came_refs)
    for k in range(pairs):
        pid = me ^ k
        hot = (first == pid).astype(F32) - (second == pid).astype(F32)
        score = pieces[k][share : share + 1, 0:1]
        margin = margin + hot * score
        hots.append(hot)
    sign = 2.0 * win.astype(F32) - 1.0
    loss = jnp.mean(jax.nn.softplus(-sign * margin), axis=1, keepdims=True)
    loss_ref[...] = jnp.broadcast_to(loss, loss_ref.shape)
    margin_grad = -sign * jax.nn.sigmoid(-sign * margin)
    total = jnp.zeros(total_ref.shape[1:], F32)
    for k in range(pairs):
        grad = jnp.sum(margin_grad * hots[k], axis=1, keepdims=True)
        if k == 0:
            grad_ref[...] = jnp.broadcast_to(grad, grad_ref.shape)
        total = total + grad * pieces[k][:share]
    total_ref[0] = total


def gather_kernel(order, *rest):
    *came_refs, loss_ref, conv_ref, bias_ref, head_ref, loss_out, stage = rest
    loss_out[...] = loss_ref[...]
    me = lax.axis_index("space")
    for flip, piece in zip(order, pieces_of(came_refs), strict=True):
        share = piece.shape[0]
        start = pl.multiple_of((me ^ flip) * share, 8)
        stage[pl.ds(start, share), :] = piece[...]
    conv_ref[...] = stage[: conv_ref.shape[0]]
    bias_ref[...] = stage[STAT : STAT + 1]
    head_ref[...] = stage[STAT + 1 : STAT + 2]


def finish_kernel(
    inv_root,
    parts,
    grad_ref,
    source_ref,
    edit_ref,
    across_ref,
    beyond_ref,
    source_hbm,
    edit_hbm,
    source_out,
    edit_out,
    sems,
):
    scale = grad_ref[0:1, 0:1].reshape(1, 1, 1) * inv_root
    rows = edit_ref.shape[0]
    copies = []

    def send(out, hbm, at):
        copies.append(pltpu.make_async_copy(out.at[at], hbm.at[at], sems.at[len(copies)]))
        copies[-1].start()

    for y in range(0, rows, 4):
        at = slice(y, y + 4)
        source_out[at] = (source_ref[at] * scale).astype(BF16)
        send(source_out, source_hbm, at)
    for kind, ref in ((0, across_ref), (1, beyond_ref)):
        above, inside = edge_spot(parts, kind)
        for y in (0, 4):
            at = pl.ds((rows - 8) * above + y, 4)
            extra = jnp.where(inside, ref[y : y + 4].astype(F32), 0.0)
            edit_out[at] = ((edit_ref[at] + extra) * scale).astype(BF16)
            send(edit_out, edit_hbm, at)
    for copy in copies:
        copy.wait()


def call(kernel, outs, scratch, flops, *args, far=(), far_out=False):
    nbytes = sum(a.size * a.dtype.itemsize for a in args)
    spaces = [pltpu.HBM if i in far else pltpu.VMEM for i in range(len(args))]
    return pl.pallas_call(
        kernel,
        out_shape=outs,
        in_specs=[pl.BlockSpec(memory_space=space) for space in spaces],
        **({"out_specs": [pl.BlockSpec(memory_space=pltpu.HBM)] * len(outs)} if far_out else {}),
        scratch_shapes=scratch,
        compiler_params=pltpu.CompilerParams(vmem_limit_bytes=VMEM_LIMIT),
        cost_estimate=pl.CostEstimate(flops=flops, bytes_accessed=nbytes, transcendentals=0),
    )(*map(pltpu.with_memory_space_constraint, args, spaces))


def result(dims, dtype=F32):
    return jax.ShapeDtypeStruct(dims, dtype)


def shape(dims, dtype=F32):
    return pltpu.VMEM(dims, dtype)


def place_bits(count):
    bits = [1 << i for i in range(count.bit_length() - 1)]
    assert count == 1 << len(bits)
    return bits


def swap(array, axis, bit):
    return lax.ppermute(array, axis, [(i, i ^ bit) for i in range(lax.axis_size(axis))])


def together(came, others):
    came, *others = lax.optimization_barrier((came, *others))
    return came, others


def collect(array, axis, bits, covers):
    order, done = [0], []
    stacks = [array]
    for i, bit in enumerate(bits):
        came = swap(array, axis, bit)
        cover = covers[i]() if i < len(covers) else ()
        came, cover = together(came, cover)
        done += cover
        order += [o ^ bit for o in order]
        stacks = [array, came]
        if i < len(bits) - 1:
            dims = (2 * array.shape[0], *array.shape[1:])
            (array,) = call(stack_kernel, (shape(dims),), [], 10**4, array, came)
    for cover in covers[len(bits) :]:
        done += cover()
    return stacks, order, done


def local(
    source_feats, edit_feats, conv_weight, conv_bias, head_weight, comp_first, comp_second, comp_win
):
    _, rows, columns, chan = source_feats.shape
    kout, disp = conv_weight.shape
    inv_root = chan ** (-0.5)
    space, pairs = lax.axis_size("space"), lax.axis_size("pair")
    pixels = rows * space * columns
    space_bits, pair_bits = place_bits(space), place_bits(pairs)
    groups = columns // GROUP
    wide_cols = columns + 2 * RADIUS
    share = -(-(disp + 2) // (8 * space)) * 8
    edit = edit_feats[0]
    source = source_feats.reshape(rows, groups, GROUP, chan)
    to_across = [(i, i ^ 1 if i ^ 1 < space else i) for i in range(space)]
    to_beyond = [(i, b if 0 <= (b := i + 1 - 2 * ((i + 1) % 2)) < space else i) for i in range(space)]
    across, beyond = call(
        slice_kernel,
        (shape((RADIUS, columns, chan), BF16),) * 2,
        [pltpu.SemaphoreType.DMA((2,))],
        10**4,
        edit,
        far=(0,),
    )
    across = lax.ppermute(across, "space", to_across)
    beyond = lax.ppermute(beyond, "space", to_beyond)
    near = (rows, groups, GROUP, chan)
    rim_shape = (rows // 2, groups, GROUP, 8 * WIN)
    held, own_pad, turned, corr, wide, tall, own = call(
        functools.partial(inner_kernel, inv_root),
        (
            shape(near, BF16),
            shape((rows, wide_cols, chan), BF16),
            shape(near, BF16),
            shape((rows, groups, GROUP, rows * WIN), BF16),
            shape((PER, kout, POS * LANES), BF16),
            shape((PER, (POS + 2) * LANES, kout), BF16),
            shape((rows, columns, kout)),
        ),
        [pltpu.VMEM((disp, kout), BF16), pltpu.SemaphoreType.DMA((3,))],
        2 * 10**9,
        source,
        edit,
        conv_weight.T,
        far=(0, 1, 2),
    )
    rim, extra = call(
        functools.partial(across_kernel, inv_root, space),
        (shape(rim_shape, BF16), shape((rows // 2, columns, kout))),
        [pltpu.VMEM((RADIUS, wide_cols, chan), BF16)],
        10**9,
        turned,
        across,
        tall,
    )
    half_pieces = max(space // 2, 1)
    gate, *pieces = call(
        functools.partial(outer_kernel, inv_root, pixels, space),
        (
            shape((rows, columns, kout), BF16),
            *(shape((half_pieces, share + 8, kout)),) * min(space, 2),
        ),
        [
            pltpu.VMEM((RADIUS, wide_cols, chan), BF16),
            pltpu.VMEM((2,) + rim_shape, BF16),
            pltpu.VMEM((2, rows // 2, columns, kout), F32),
            pltpu.VMEM((share * space, kout), F32),
        ],
        2 * 10**9,
        turned,
        corr,
        rim,
        extra,
        own,
        beyond,
        tall,
        conv_bias[None],
        head_weight[None],
    )
    came = [swap(pieces[1], "space", 1)] if space > 1 else []
    rims = call(
        rim_kernel,
        (shape((RADIUS, columns, chan), BF16),) * 2,
        [
            pltpu.VMEM(rim_shape, BF16),
            pltpu.VMEM(rim_shape, BF16),
            pltpu.VMEM((2 * RADIUS, wide_cols, chan), F32),
        ],
        10**9,
        gate,
        wide,
        held,
    )
    *came, rim_across, rim_beyond = lax.optimization_barrier((*came, *rims))
    from_beyond = lax.ppermute(rim_beyond, "space", to_beyond)
    from_across = lax.ppermute(rim_across, "space", to_across)
    keep = pieces[0]
    for bit in space_bits[1:]:
        dims = (keep.shape[0] // 2, *keep.shape[1:])
        keep, send = call(
            functools.partial(split_kernel, bit), (shape(dims),) * 2, [], 10**4, keep, *came
        )
        came = [swap(send, "space", bit)]
    quarter = keep + came[0] if came else keep

    def edit_cover():
        return call(
            edit_kernel,
            (
                shape((rows, groups, GROUP, (rows + 2 * RADIUS) * WIN), BF16),
                shape((rows, columns, chan)),
            ),
            [pltpu.VMEM((rows, wide_cols, chan), F32)],
            2 * 10**9,
            gate,
            wide,
            held,
        )

    edited = []

    def edit_first():
        edited.extend(edit_cover())
        return edited

    def source_cover():
        return call(
            functools.partial(source_kernel, space),
            (shape(near),),
            [pltpu.VMEM((2 * RADIUS, wide_cols, chan), BF16)],
            2 * 10**9,
            edited[0],
            own_pad,
            across,
            beyond,
        )

    stacks, _, (_, edit_sum, source_sum) = collect(
        quarter, "pair", pair_bits, (edit_first, source_cover)
    )
    total, score_grad, loss = call(
        functools.partial(judge_kernel, pairs),
        (shape((1, share, kout)), shape((8, LANES)), shape((1, LANES))),
        [],
        10**6,
        comp_first[None],
        comp_second[None],
        comp_win[None],
        *stacks,
    )

    def finish_cover():
        return call(
            functools.partial(finish_kernel, inv_root, space),
            (result((rows, columns, chan), BF16),) * 2,
            [
                pltpu.VMEM((rows, columns, chan), BF16),
                pltpu.VMEM((rows, columns, chan), BF16),
                pltpu.SemaphoreType.DMA((8,)),
            ],
            10**7,
            score_grad,
            source_sum.reshape(rows, columns, chan),
            edit_sum,
            from_across,
            from_beyond,
            far_out=True,
        )

    stacks, order, (source_grad, edit_grad) = collect(
        total, "space", space_bits[::-1], (finish_cover,)
    )
    conv_grad, bias_grad, head_grad, loss = call(
        functools.partial(gather_kernel, order),
        (result((disp, kout)), result((1, kout)), result((1, kout)), result((1, LANES))),
        [pltpu.VMEM((share * space, kout), F32)],
        10**6,
        *stacks,
        loss,
    )
    return (
        source_grad[None],
        edit_grad[None],
        conv_grad.T,
        bias_grad[0],
        head_grad[0],
        loss[0, :1],
    )


def solution(mesh):
    in_specs = (
        P(("groups", "pair"), "space", None, None),
        P(("groups", "pair"), "space", None, None),
        P(),
        P(),
        P(),
        P("groups"),
        P("groups"),
        P("groups"),
    )
    out_specs = (
        P(("groups", "pair"), "space", None, None),
        P(("groups", "pair"), "space", None, None),
        P("groups", None),
        P("groups"),
        P("groups"),
        P("groups"),
    )
    return jax.shard_map(local, mesh=mesh, in_specs=in_specs, out_specs=out_specs, check_vma=False)
```

```python
import functools

import jax
import jax.numpy as jnp
from jax import lax
from jax.experimental import pallas as pl
from jax.experimental.pallas import tpu as pltpu
from jax.sharding import PartitionSpec as P

RADIUS = 8
SPAN = 2 * RADIUS + 1
GROUP = 16
WIN = GROUP + 2 * RADIUS
LANES = 128
PER = LANES // WIN
POS = 5
STAT = SPAN * SPAN
F32 = jnp.float32
BF16 = jnp.bfloat16
VMEM_LIMIT = 24 * 1024 * 1024


def nt(a, b):
    return lax.dot_general(a, b, (((1,), (1,)), ((), ())), preferred_element_type=F32)


def nn(a, b):
    return lax.dot_general(a, b, (((1,), (0,)), ((), ())), preferred_element_type=F32)


def tn(a, b):
    return lax.dot_general(a, b, (((0,), (0,)), ((), ())), preferred_element_type=F32)


def iota(shape, dim):
    return lax.broadcasted_iota(jnp.int32, shape, dim)


def mirror(size):
    row, col = iota((size, size), 0), iota((size, size), 1)
    return (col == (row ^ (GROUP - 1))).astype(F32).astype(BF16)


def spread(p):
    first = p * PER * SPAN
    return first // 8 * 8, first % 8


def spread_table(p, dim):
    _, offset = spread(p)
    count = (PER if p < POS - 1 else 1) * SPAN
    dims = [LANES, LANES]
    dims[dim] = -(-(count + offset) // 8) * 8 if p < POS - 1 else count
    place, lane = iota(dims, dim), iota(dims, 1 - dim)
    dy, t = lane // WIN, lane % WIN
    hit = (place == dy * SPAN + t + offset) & (t < SPAN) & (dy * SPAN < count)
    return hit.astype(F32).astype(BF16)


def skew(values, shift):
    return pltpu.roll(values, shift, 2, stride=1, stride_axis=1)


def skew_wide(values, shift):
    parts = []
    for start in range(0, values.shape[-1], LANES):
        parts.append(skew(values[:, :, start : start + LANES], shift))
    return parts


def fill_columns(pad_ref, row, rows, cols):
    zero = jnp.zeros((rows, RADIUS, pad_ref.shape[2]), BF16)
    pad_ref[row : row + rows, 0:RADIUS] = zero
    pad_ref[row : row + rows, RADIUS + cols :] = zero


def fill_padded(pad_ref, row, block_ref):
    rows, cols = block_ref.shape[:2]
    fill_columns(pad_ref, row, rows, cols)
    pad_ref[row : row + rows, RADIUS : RADIUS + cols] = block_ref[...]


def window(pad_ref, row, rows, g):
    block = pad_ref[row : row + rows, g * GROUP : g * GROUP + WIN, :]
    return block.reshape(rows * WIN, block.shape[2])


def correlate_set(lhs, pad_ref, row, g, inv_root, out_ref, spot, lane):
    ys = lhs.shape[0] // GROUP
    scores = nt(lhs, window(pad_ref, row, 8, g)) * inv_root
    scores = scores.reshape(ys, GROUP, 8 * WIN)
    for i, part in enumerate(skew_wide(scores, LANES - GROUP + 1)):
        at = lane + i * LANES
        out_ref[spot, g, :, at : at + LANES] = part.astype(BF16)


def spread_weights(weight, wide_ref, tall_ref):
    kout = weight.shape[1]
    wides, talls = [], []
    for p in range(POS):
        row, _ = spread(p)
        table = spread_table(p, 0)
        part = weight[row : row + table.shape[0], :]
        wides.append(tn(part, table))
        talls.append(nn(spread_table(p, 1), part))
    base = jnp.concatenate(wides, axis=1)
    tall = jnp.concatenate(talls, axis=0).astype(BF16)[: SPAN * WIN]
    tall_rows = tall_ref.shape[1]
    for r in range(PER):
        wide_ref[r] = (base if r == 0 else pltpu.roll(base, r * WIN, 1)).astype(BF16)
        start = LANES + r * WIN
        tall_ref[r, :start] = jnp.zeros((start, kout), BF16)
        tall_ref[r, start : start + SPAN * WIN] = tall
        tall_ref[r, start + SPAN * WIN :] = jnp.zeros((tall_rows - start - SPAN * WIN, kout), BF16)


def inner_kernel(
    inv_root,
    source_hbm,
    edit_hbm,
    weight_hbm,
    source_ref,
    pad,
    turned_ref,
    corr_ref,
    wide_ref,
    tall_ref,
    own_ref,
    weight,
    sems,
):
    rows, groups, _, chan = source_ref.shape
    weight_copy = pltpu.make_async_copy(weight_hbm, weight, sems.at[2])
    weight_copy.start()
    copies = []
    cols = groups * GROUP
    edit_copy = pltpu.make_async_copy(edit_hbm, pad.at[:, RADIUS : RADIUS + cols], sems.at[0])
    source_copy = pltpu.make_async_copy(source_hbm, source_ref, sems.at[1])
    edit_copy.start()
    source_copy.start()
    fill_columns(pad, 0, rows, groups * GROUP)
    turn = mirror(rows * GROUP)
    weight_copy.wait()
    spread_weights(weight, wide_ref, tall_ref)
    source_copy.wait()
    edit_copy.wait()
    for g in range(groups):
        lhs = nn(turn, source_ref[:, g].reshape(rows * GROUP, chan)).astype(BF16)
        turned_ref[:, g] = lhs.reshape(rows, GROUP, chan)
        for s in range(rows // 8):
            correlate_set(lhs, pad, 8 * s, g, inv_root, corr_ref, slice(0, rows), 2 * s * LANES)
    cols = groups * GROUP
    for q in range(rows // PER):
        start = (3 - q) * LANES
        for r in range(PER):
            lhs = corr_ref[q * PER + r].reshape(cols, 4 * LANES)
            own_ref[q * PER + r] = nn(lhs, tall_ref[r, start : start + 4 * LANES])


def edge_spot(parts, kind):
    me = lax.axis_index("space")
    above = lax.rem(me, 2) ^ 1 if kind == 0 else lax.rem(me, 2)
    inside = jnp.where(above == 1, me != parts - 1, me != 0)
    return above, inside


def fill_halo(pad_ref, row, halo_ref, inside):
    cols = halo_ref.shape[1]
    pad_ref[pl.ds(row, 8), RADIUS : RADIUS + cols] = jnp.where(
        inside, halo_ref[...], jnp.zeros(halo_ref.shape, BF16)
    )


def rim_scores(inv_root, parts, kind, turned_ref, halo_ref, pad, rim_ref):
    rows, groups, _, chan = turned_ref.shape
    half = rows // 2
    above, inside = edge_spot(parts, kind)
    fill_columns(pad, 0, 8, groups * GROUP)
    fill_halo(pad, 0, halo_ref, inside)
    start = half * above
    for g in range(groups):
        lhs = turned_ref[pl.ds(start, half), g].reshape(half * GROUP, chan)
        correlate_set(lhs, pad, 0, g, inv_root, rim_ref, slice(0, half), 0)
    return above


def rim_values(rim_ref, tall_ref, above, out_ref):
    half, groups, _, lanes = rim_ref.shape
    for i in range(half):
        q, r = i // PER, i % PER
        start = pl.multiple_of((1 - q) * LANES + above * 4 * LANES, LANES)
        lhs = rim_ref[i].reshape(groups * GROUP, lanes)
        out_ref[i] = nn(lhs, tall_ref[r, pl.ds(start, lanes), :])


def across_kernel(
    inv_root, parts, turned_ref, halo_ref, tall_ref, rim_ref, extra_ref, pad
):
    above = rim_scores(inv_root, parts, 0, turned_ref, halo_ref, pad, rim_ref)
    rim_values(rim_ref, tall_ref, above, extra_ref)


def slice_kernel(edit_ref, across_ref, beyond_ref, sems):
    rows = edit_ref.shape[0]
    odd = lax.rem(lax.axis_index("space"), 2)
    copies = []
    count = sems.shape[0] // 2
    step = RADIUS // count
    for start, ref in ((odd, beyond_ref), (1 - odd, across_ref)):
        for i in range(count):
            block = edit_ref.at[pl.ds((rows - RADIUS) * start + i * step, step)]
            copies.append(
                pltpu.make_async_copy(
                    block, ref.at[i * step : (i + 1) * step], sems.at[len(copies)]
                )
            )
            copies[-1].start()
    for copy in copies:
        copy.wait()


def row_chunks(rims, corr_ref, r, rows):
    pieces = []
    half = rows // 2
    for q in range(rows // PER):
        y = q * PER + r
        parts = []
        for c in range(q, q + POS):
            if c < 2:
                part = rims[0, y, :, :, c * LANES : (c + 1) * LANES]
            elif c < 2 + rows // PER:
                part = corr_ref[y, :, :, (c - 2) * LANES : (c - 1) * LANES]
            else:
                at = c - 2 - rows // PER
                part = rims[1, y - half, :, :, at * LANES : (at + 1) * LANES]
            parts.append(part.reshape(part.shape[0] * part.shape[1], LANES))
        pieces.append(jnp.concatenate(parts, axis=1))
    return jnp.concatenate(pieces, axis=0)


def outer_kernel(
    inv_root,
    pixels,
    parts,
    turned_ref,
    corr_ref,
    rim_ref,
    extra_ref,
    own_ref,
    beyond_ref,
    tall_ref,
    bias_ref,
    head_ref,
    *rest,
):
    gate_ref = rest[0]
    piece_refs = rest[1 : 1 + parts]
    pad, rims, extra, stage = rest[1 + parts :]
    rows, groups = turned_ref.shape[:2]
    above, _ = edge_spot(parts, 1)
    rims[1 - above] = rim_ref[...]
    extra[1 - above] = extra_ref[...]
    rim_scores(inv_root, parts, 1, turned_ref, beyond_ref, pad, rims.at[above])
    rim_values(rims.at[above], tall_ref, above, extra.at[above])
    bias, head = bias_ref[...], head_ref[...]
    kout = bias.shape[1]
    cols = groups * GROUP
    turn = mirror(cols)
    hidden = jnp.zeros((1, kout), F32)
    slopes = jnp.zeros((1, kout), F32)
    total = None
    for r in range(PER):
        corr = row_chunks(rims, corr_ref, r, rows)
        spots = [(q * PER + r, q // 2, q % 2 * PER + r) for q in range(rows // PER)]
        value = jnp.concatenate([own_ref[y] + extra[h, i] for y, h, i in spots], axis=0) + bias
        gating = jax.nn.sigmoid(value)
        act = value * gating
        slope = gating * (1.0 + value * (1.0 - gating))
        hidden = hidden + jnp.sum(act, axis=0, keepdims=True)
        slopes = slopes + jnp.sum(slope, axis=0, keepdims=True)
        pre = (slope * head).astype(BF16)
        for q in range(rows // PER):
            gate_ref[q * PER + r] = nn(turn, pre[q * cols : (q + 1) * cols]).astype(BF16)
        grad = tn(pre, corr)
        if r:
            grad = pltpu.roll(grad, POS * LANES - r * WIN, 1)
        total = grad if total is None else total + grad
    share = stage.shape[0] // parts
    stage[...] = jnp.zeros(stage.shape, F32)
    for p in range(POS):
        row, _ = spread(p)
        table = spread_table(p, 0)
        left = total[:, p * LANES : (p + 1) * LANES]
        packed = None
        for _ in range(3):
            term = left.astype(BF16)
            left = left - term.astype(F32)
            part = nt(table, term)
            packed = part if packed is None else packed + part
        stage[row : row + table.shape[0]] += packed
    scale = 1.0 / pixels
    stage[:STAT] = stage[:STAT] * scale
    stage[STAT : STAT + 1] = head * slopes * scale
    stage[STAT + 1 : STAT + 2] = hidden * scale
    score = jnp.sum(hidden * head, axis=1, keepdims=True) * scale
    me = lax.axis_index("space")
    for k in range(parts):
        start = pl.multiple_of(partner(me, k, parts) * share, 8)
        piece_refs[k][:share] = stage[pl.ds(start, share), :]
        piece_refs[k][share:] = jnp.broadcast_to(score, (8, kout))


def back_chunks(gate_ref, wide_ref, r, rows, groups):
    quarter = rows // PER
    lhs = jnp.concatenate([gate_ref[q * PER + r] for q in range(quarter)], axis=0)
    out = []
    for pos in range(POS):
        grad = nn(lhs, wide_ref[r, :, pos * LANES : (pos + 1) * LANES])
        grad = skew(grad.reshape(quarter * groups, GROUP, LANES), 0)
        out.append(grad.astype(BF16).reshape(quarter, groups, GROUP, LANES))
    return out


def rim_kernel(gate_ref, wide_ref, source_ref, across_ref, beyond_ref, band_lo, band_hi, sums):
    rows, groups, _, chan = source_ref.shape
    half = rows // 2
    quarter = rows // PER
    zero = jnp.zeros((groups, GROUP, LANES), BF16)
    for r in range(PER):
        for q in range(quarter):
            y = q * PER + r
            for c in (0, 1, 6, 7):
                pos = c - q
                band, row = (band_lo, y) if c < 2 else (band_hi, y - half)
                if not 0 <= row < half:
                    continue
                at = (c if c < 2 else c - 6) * LANES
                if 0 <= pos < POS:
                    grad = nn(gate_ref[y], wide_ref[r, :, pos * LANES : (pos + 1) * LANES])
                    part = skew(grad.reshape(groups, GROUP, LANES), 0).astype(BF16)
                else:
                    part = zero
                band[row, :, :, at : at + LANES] = part
    sums[...] = jnp.zeros(sums.shape, F32)

    def body(g, carry):
        start = g * GROUP
        for i, band in enumerate((band_lo, band_hi)):
            lhs = band[:, g].reshape(half * GROUP, 2 * LANES)
            rhs = source_ref[i * half : (i + 1) * half, g].reshape(half * GROUP, chan)
            grad = tn(lhs, rhs).reshape(8, WIN, chan)
            sums[8 * i : 8 * i + 8, start : start + WIN, :] += grad
        return carry

    for g in range(groups):
        body(g, 0)
    cols = groups * GROUP
    odd = lax.rem(lax.axis_index("space"), 2)
    low = pl.multiple_of(8 * odd, 8)
    high = pl.multiple_of(8 - 8 * odd, 8)
    across_ref[...] = sums[pl.ds(high, 8), RADIUS : RADIUS + cols].astype(BF16)
    beyond_ref[...] = sums[pl.ds(low, 8), RADIUS : RADIUS + cols].astype(BF16)


def back_kernel(
    parts,
    gate_ref,
    wide_ref,
    source_ref,
    own_pad,
    across_ref,
    beyond_ref,
    source_out,
    edit_out,
    pad,
    band,
    sums,
):
    rows, groups, _, chan = source_ref.shape
    half = rows // 2
    quarter = rows // PER
    for kind, ref in ((0, across_ref), (1, beyond_ref)):
        above, inside = edge_spot(parts, kind)
        fill_halo(pad, 8 * above, ref, inside)
    fill_columns(pad, 0, 16, groups * GROUP)
    zero = jnp.zeros((PER, groups, GROUP, LANES), BF16)
    for q, c in ((1, 0), (3, 2), (0, 5), (2, 7)):
        band[q * PER : (q + 1) * PER, :, :, c * LANES : (c + 1) * LANES] = zero
    for r in range(PER):
        for pos, part in enumerate(back_chunks(gate_ref, wide_ref, r, rows, groups)):
            for q in range(quarter):
                at = (q + pos) * LANES
                band[q * PER + r, :, :, at : at + LANES] = part[q]
    sums[...] = jnp.zeros(sums.shape, F32)

    def body(g, carry):
        start = g * GROUP
        near = source_ref[:, g].reshape(rows * GROUP, chan)
        for s in range(rows // 8):
            at = (2 + 2 * s) * LANES
            lhs = band[:, g, :, at : at + 2 * LANES].reshape(rows * GROUP, 2 * LANES)
            grad = tn(lhs, near).reshape(8, WIN, chan)
            sums[8 * s : 8 * s + 8, start : start + WIN, :] += grad
        for i in range(2):
            at = i * 2 * LANES
            lhs = band[i * half : (i + 1) * half, g, :, at : at + 6 * LANES]
            spots = [window(pad, 8 * i, 8, g), window(own_pad, 0, rows, g)]
            rhs = jnp.concatenate(spots[::-1] if i else spots, axis=0)
            grad = nn(lhs.reshape(half * GROUP, 6 * LANES), rhs)
            source_out[i * half : (i + 1) * half, g] = grad.reshape(half, GROUP, chan)
        return carry

    for g in range(groups):
        body(g, 0)
    cols = groups * GROUP
    edit_out[...] = sums[:, RADIUS : RADIUS + cols]


def partner(me, step, count):
    if count & (count - 1):
        return (me + step + count) % count
    return me ^ abs(step)


def judge_kernel(pairs, first_ref, second_ref, win_ref, *rest):
    piece_refs = rest[:pairs]
    total_ref, grad_ref, loss_ref = rest[pairs:]
    share = total_ref.shape[0]
    me = lax.axis_index("pair")
    first, second, win = first_ref[...], second_ref[...], win_ref[...]
    hots, margin = [], jnp.zeros(first.shape, F32)
    for k in range(pairs):
        pid = partner(me, -k, pairs)
        hot = (first == pid).astype(F32) - (second == pid).astype(F32)
        score = piece_refs[k][share : share + 1, 0:1]
        margin = margin + hot * score
        hots.append(hot)
    sign = 2.0 * win.astype(F32) - 1.0
    loss = jnp.mean(jax.nn.softplus(-sign * margin), axis=1, keepdims=True)
    loss_ref[...] = jnp.broadcast_to(loss, loss_ref.shape)
    margin_grad = -sign * jax.nn.sigmoid(-sign * margin)
    total = jnp.zeros(total_ref.shape, F32)
    for k in range(pairs):
        grad = jnp.sum(margin_grad * hots[k], axis=1, keepdims=True)
        if k == 0:
            grad_ref[...] = jnp.broadcast_to(grad, grad_ref.shape)
        total = total + grad * piece_refs[k][:share]
    total_ref[...] = total


def gather_kernel(parts, *rest):
    piece_refs = rest[:parts]
    loss_ref, conv_ref, bias_ref, head_ref, loss_out, stage = rest[parts:]
    loss_out[...] = loss_ref[...]
    share = piece_refs[0].shape[0]
    me = lax.axis_index("space")
    for k in range(parts):
        start = pl.multiple_of(partner(me, -k, parts) * share, 8)
        stage[pl.ds(start, share), :] = piece_refs[k][...]
    conv_ref[...] = stage[: conv_ref.shape[0]]
    bias_ref[...] = stage[STAT : STAT + 1]
    head_ref[...] = stage[STAT + 1 : STAT + 2]


def finish_kernel(
    inv_root,
    parts,
    grad_ref,
    source_ref,
    edit_ref,
    across_ref,
    beyond_ref,
    source_hbm,
    edit_hbm,
    source_out,
    edit_out,
    sems,
):
    scale = grad_ref[0:1, 0:1].reshape(1, 1, 1) * inv_root
    rows = edit_ref.shape[0]
    copies = []

    def send(out, hbm, at):
        copies.append(pltpu.make_async_copy(out.at[at], hbm.at[at], sems.at[len(copies)]))
        copies[-1].start()

    for y in range(0, rows, 4):
        at = slice(y, y + 4)
        source_out[at] = (source_ref[at] * scale).astype(BF16)
        send(source_out, source_hbm, at)
    for kind, ref in ((0, across_ref), (1, beyond_ref)):
        above, inside = edge_spot(parts, kind)
        for y in (0, 4):
            at = pl.ds((rows - 8) * above + y, 4)
            extra = jnp.where(inside, ref[y : y + 4].astype(F32), 0.0)
            edit_out[at] = ((edit_ref[at] + extra) * scale).astype(BF16)
            send(edit_out, edit_hbm, at)
    for copy in copies:
        copy.wait()


def call(kernel, outs, scratch, flops, *args, far=(), far_out=False):
    nbytes = sum(a.size * a.dtype.itemsize for a in args)
    spaces = [pltpu.HBM if i in far else pltpu.VMEM for i in range(len(args))]
    return pl.pallas_call(
        kernel,
        out_shape=outs,
        in_specs=[pl.BlockSpec(memory_space=space) for space in spaces],
        **({"out_specs": [pl.BlockSpec(memory_space=pltpu.HBM)] * len(outs)} if far_out else {}),
        scratch_shapes=scratch,
        compiler_params=pltpu.CompilerParams(vmem_limit_bytes=VMEM_LIMIT),
        cost_estimate=pl.CostEstimate(flops=flops, bytes_accessed=nbytes, transcendentals=0),
    )(*map(pltpu.with_memory_space_constraint, args, spaces))


def result(dims, dtype=F32):
    return jax.ShapeDtypeStruct(dims, dtype)


def shape(dims, dtype=F32):
    return pltpu.VMEM(dims, dtype)


def around(axis, step):
    count = lax.axis_size(axis)
    return [(i, partner(i, step, count)) for i in range(count)]


def beyond_pairs(space, pairs):
    table = []
    for i in range(space):
        other = i + 1 if i % 2 else i - 1
        for p in range(pairs):
            if 0 <= other < space:
                to = other * pairs + p
            else:
                to = i * pairs + (p ^ 1 if p ^ 1 < pairs else p)
            table.append((i * pairs + p, to))
    return table


def local(
    source_feats, edit_feats, conv_weight, conv_bias, head_weight, comp_first, comp_second, comp_win
):
    _, rows, columns, chan = source_feats.shape
    kout, disp = conv_weight.shape
    inv_root = chan ** (-0.5)
    space, pairs = lax.axis_size("space"), lax.axis_size("pair")
    pixels = rows * space * columns
    groups = columns // GROUP
    wide_cols = columns + 2 * RADIUS
    share = -(-(disp + 2) // (8 * space)) * 8
    edit = edit_feats[0]
    source = source_feats.reshape(rows, groups, GROUP, chan)
    to_across = [(i, i ^ 1 if i ^ 1 < space else i) for i in range(space)]
    to_beyond = beyond_pairs(space, pairs)
    across, beyond = call(
        slice_kernel,
        (shape((RADIUS, columns, chan), BF16),) * 2,
        [pltpu.SemaphoreType.DMA((2,))],
        10**4,
        edit,
        far=(0,),
    )
    across = lax.ppermute(across, "space", to_across)
    beyond = lax.ppermute(beyond, ("space", "pair"), to_beyond)
    near = (rows, groups, GROUP, chan)
    rim_shape = (rows // 2, groups, GROUP, 8 * WIN)
    held, own_pad, turned, corr, wide, tall, own = call(
        functools.partial(inner_kernel, inv_root),
        (
            shape(near, BF16),
            shape((rows, wide_cols, chan), BF16),
            shape(near, BF16),
            shape((rows, groups, GROUP, rows * WIN), BF16),
            shape((PER, kout, POS * LANES), BF16),
            shape((PER, (POS + 2) * LANES, kout), BF16),
            shape((rows, columns, kout)),
        ),
        [pltpu.VMEM((disp, kout), BF16), pltpu.SemaphoreType.DMA((3,))],
        2 * 10**9,
        source,
        edit,
        conv_weight.T,
        far=(0, 1, 2),
    )
    rim, extra = call(
        functools.partial(across_kernel, inv_root, space),
        (shape(rim_shape, BF16), shape((rows // 2, columns, kout))),
        [pltpu.VMEM((RADIUS, wide_cols, chan), BF16)],
        10**9,
        turned,
        across,
        tall,
    )
    gate, *pieces = call(
        functools.partial(outer_kernel, inv_root, pixels, space),
        (shape((rows, columns, kout), BF16),) + (shape((share + 8, kout)),) * space,
        [
            pltpu.VMEM((RADIUS, wide_cols, chan), BF16),
            pltpu.VMEM((2,) + rim_shape, BF16),
            pltpu.VMEM((2, rows // 2, columns, kout), F32),
            pltpu.VMEM((share * space, kout), F32),
        ],
        2 * 10**9,
        turned,
        corr,
        rim,
        extra,
        own,
        beyond,
        tall,
        conv_bias[None],
        head_weight[None],
    )
    quarter = pieces[0]
    for k in range(1, space):
        quarter = quarter + lax.ppermute(pieces[k], "space", around("space", k))
    rim_across, rim_beyond = call(
        rim_kernel,
        (shape((RADIUS, columns, chan), BF16),) * 2,
        [
            pltpu.VMEM((rows // 2, groups, GROUP, 8 * WIN), BF16),
            pltpu.VMEM((rows // 2, groups, GROUP, 8 * WIN), BF16),
            pltpu.VMEM((2 * RADIUS, wide_cols, chan), F32),
        ],
        10**9,
        gate,
        wide,
        held,
    )
    from_across = lax.ppermute(rim_across, "space", to_across)
    from_beyond = lax.ppermute(rim_beyond, ("space", "pair"), to_beyond)
    source_sum, edit_sum = call(
        functools.partial(back_kernel, space),
        (shape((rows, groups, GROUP, chan)), shape((rows, columns, chan))),
        [
            pltpu.VMEM((2 * RADIUS, wide_cols, chan), BF16),
            pltpu.VMEM((rows, groups, GROUP, (rows + 2 * RADIUS) * WIN), BF16),
            pltpu.VMEM((rows, wide_cols, chan), F32),
        ],
        4 * 10**9,
        gate,
        wide,
        held,
        own_pad,
        across,
        beyond,
    )
    others = [quarter] + [lax.ppermute(quarter, "pair", around("pair", k)) for k in range(1, pairs)]
    *others, source_sum, edit_sum = lax.optimization_barrier((*others, source_sum, edit_sum))
    total, score_grad, loss = call(
        functools.partial(judge_kernel, pairs),
        (shape((share, kout)), shape((8, LANES)), shape((1, LANES))),
        [],
        10**6,
        comp_first[None],
        comp_second[None],
        comp_win[None],
        *others,
    )
    gathered = [total] + [lax.ppermute(total, "space", around("space", k)) for k in range(1, space)]
    source_grad, edit_grad = call(
        functools.partial(finish_kernel, inv_root, space),
        (result((rows, columns, chan), BF16),) * 2,
        [
            pltpu.VMEM((rows, columns, chan), BF16),
            pltpu.VMEM((rows, columns, chan), BF16),
            pltpu.SemaphoreType.DMA((8,)),
        ],
        10**7,
        score_grad,
        source_sum.reshape(rows, columns, chan),
        edit_sum,
        from_across,
        from_beyond,
        far_out=True,
    )
    *gathered, source_grad, edit_grad = lax.optimization_barrier((*gathered, source_grad, edit_grad))
    conv_grad, bias_grad, head_grad, loss = call(
        functools.partial(gather_kernel, space),
        (result((disp, kout)), result((1, kout)), result((1, kout)), result((1, LANES))),
        [pltpu.VMEM((share * space, kout), F32)],
        10**6,
        *gathered,
        loss,
    )
    return (
        source_grad[None],
        edit_grad[None],
        conv_grad.T,
        bias_grad[0],
        head_grad[0],
        loss[0, :1],
    )


def solution(mesh):
    in_specs = (
        P(("groups", "pair"), "space", None, None),
        P(("groups", "pair"), "space", None, None),
        P(),
        P(),
        P(),
        P("groups"),
        P("groups"),
        P("groups"),
    )
    out_specs = (
        P(("groups", "pair"), "space", None, None),
        P(("groups", "pair"), "space", None, None),
        P("groups", None),
        P("groups"),
        P("groups"),
        P("groups"),
    )
    return jax.shard_map(local, mesh=mesh, in_specs=in_specs, out_specs=out_specs, check_vma=False)
```

```python
import functools

import jax
import jax.numpy as jnp
from jax import lax
from jax.experimental import pallas as pl
from jax.experimental.pallas import tpu as pltpu
from jax.sharding import PartitionSpec as P

RADIUS = 8
SPAN = 2 * RADIUS + 1
GROUP = 16
WIN = GROUP + 2 * RADIUS
LANES = 128
PER = LANES // WIN
POS = 5
STAT = SPAN * SPAN
F32 = jnp.float32
BF16 = jnp.bfloat16
VMEM_LIMIT = 24 * 1024 * 1024


def nt(a, b):
    return lax.dot_general(a, b, (((1,), (1,)), ((), ())), preferred_element_type=F32)


def nn(a, b):
    return lax.dot_general(a, b, (((1,), (0,)), ((), ())), preferred_element_type=F32)


def tn(a, b):
    return lax.dot_general(a, b, (((0,), (0,)), ((), ())), preferred_element_type=F32)


def iota(shape, dim):
    return lax.broadcasted_iota(jnp.int32, shape, dim)


def mirror(size):
    row, col = iota((size, size), 0), iota((size, size), 1)
    return (col == (row ^ (GROUP - 1))).astype(F32).astype(BF16)


def spread(p):
    first = p * PER * SPAN
    return first // 8 * 8, first % 8


def spread_table(p, dim):
    _, offset = spread(p)
    count = (PER if p < POS - 1 else 1) * SPAN
    dims = [LANES, LANES]
    dims[dim] = -(-(count + offset) // 8) * 8 if p < POS - 1 else count
    place, lane = iota(dims, dim), iota(dims, 1 - dim)
    dy, t = lane // WIN, lane % WIN
    hit = (place == dy * SPAN + t + offset) & (t < SPAN) & (dy * SPAN < count)
    return hit.astype(F32).astype(BF16)


def skew(values, shift):
    return pltpu.roll(values, shift, 2, stride=1, stride_axis=1)


def skew_wide(values, shift):
    parts = []
    for start in range(0, values.shape[-1], LANES):
        parts.append(skew(values[:, :, start : start + LANES], shift))
    return parts


def fill_columns(pad_ref, row, rows, cols):
    zero = jnp.zeros((rows, RADIUS, pad_ref.shape[2]), BF16)
    pad_ref[row : row + rows, 0:RADIUS] = zero
    pad_ref[row : row + rows, RADIUS + cols :] = zero


def fill_padded(pad_ref, row, block_ref):
    rows, cols = block_ref.shape[:2]
    fill_columns(pad_ref, row, rows, cols)
    pad_ref[row : row + rows, RADIUS : RADIUS + cols] = block_ref[...]


def window(pad_ref, row, rows, g):
    block = pad_ref[row : row + rows, g * GROUP : g * GROUP + WIN, :]
    return block.reshape(rows * WIN, block.shape[2])


def correlate_set(lhs, pad_ref, row, g, inv_root, out_ref, spot, lane):
    ys = lhs.shape[0] // GROUP
    scores = nt(lhs, window(pad_ref, row, 8, g)) * inv_root
    scores = scores.reshape(ys, GROUP, 8 * WIN)
    for i, part in enumerate(skew_wide(scores, LANES - GROUP + 1)):
        at = lane + i * LANES
        out_ref[spot, g, :, at : at + LANES] = part.astype(BF16)


def spread_weights(weight, wide_ref, tall_ref):
    kout = weight.shape[1]
    wides, talls = [], []
    for p in range(POS):
        row, _ = spread(p)
        table = spread_table(p, 0)
        part = weight[row : row + table.shape[0], :]
        wides.append(tn(part, table))
        talls.append(nn(spread_table(p, 1), part))
    base = jnp.concatenate(wides, axis=1)
    tall = jnp.concatenate(talls, axis=0).astype(BF16)[: SPAN * WIN]
    tall_rows = tall_ref.shape[1]
    for r in range(PER):
        wide_ref[r] = (base if r == 0 else pltpu.roll(base, r * WIN, 1)).astype(BF16)
        start = LANES + r * WIN
        tall_ref[r, :start] = jnp.zeros((start, kout), BF16)
        tall_ref[r, start : start + SPAN * WIN] = tall
        tall_ref[r, start + SPAN * WIN :] = jnp.zeros((tall_rows - start - SPAN * WIN, kout), BF16)


def inner_kernel(
    inv_root,
    source_hbm,
    edit_hbm,
    weight_hbm,
    source_ref,
    pad,
    turned_ref,
    corr_ref,
    wide_ref,
    tall_ref,
    own_ref,
    weight,
    sems,
):
    rows, groups, _, chan = source_ref.shape
    weight_copy = pltpu.make_async_copy(weight_hbm, weight, sems.at[2])
    weight_copy.start()
    copies = []
    cols = groups * GROUP
    edit_copy = pltpu.make_async_copy(edit_hbm, pad.at[:, RADIUS : RADIUS + cols], sems.at[0])
    source_copy = pltpu.make_async_copy(source_hbm, source_ref, sems.at[1])
    edit_copy.start()
    source_copy.start()
    fill_columns(pad, 0, rows, groups * GROUP)
    turn = mirror(rows * GROUP)
    weight_copy.wait()
    spread_weights(weight, wide_ref, tall_ref)
    source_copy.wait()
    edit_copy.wait()
    for g in range(groups):
        lhs = nn(turn, source_ref[:, g].reshape(rows * GROUP, chan)).astype(BF16)
        turned_ref[:, g] = lhs.reshape(rows, GROUP, chan)
        for s in range(rows // 8):
            correlate_set(lhs, pad, 8 * s, g, inv_root, corr_ref, slice(0, rows), 2 * s * LANES)
    cols = groups * GROUP
    for q in range(rows // PER):
        start = (3 - q) * LANES
        for r in range(PER):
            lhs = corr_ref[q * PER + r].reshape(cols, 4 * LANES)
            own_ref[q * PER + r] = nn(lhs, tall_ref[r, start : start + 4 * LANES])


def edge_spot(parts, kind):
    me = lax.axis_index("space")
    above = lax.rem(me, 2) ^ 1 if kind == 0 else lax.rem(me, 2)
    inside = jnp.where(above == 1, me != parts - 1, me != 0)
    return above, inside


def fill_halo(pad_ref, row, halo_ref, inside):
    cols = halo_ref.shape[1]
    pad_ref[pl.ds(row, 8), RADIUS : RADIUS + cols] = jnp.where(
        inside, halo_ref[...], jnp.zeros(halo_ref.shape, BF16)
    )


def rim_scores(inv_root, parts, kind, turned_ref, halo_ref, pad, rim_ref):
    rows, groups, _, chan = turned_ref.shape
    half = rows // 2
    above, inside = edge_spot(parts, kind)
    fill_columns(pad, 0, 8, groups * GROUP)
    fill_halo(pad, 0, halo_ref, inside)
    start = half * above
    for g in range(groups):
        lhs = turned_ref[pl.ds(start, half), g].reshape(half * GROUP, chan)
        correlate_set(lhs, pad, 0, g, inv_root, rim_ref, slice(0, half), 0)
    return above


def rim_values(rim_ref, tall_ref, above, out_ref):
    half, groups, _, lanes = rim_ref.shape
    for i in range(half):
        q, r = i // PER, i % PER
        start = pl.multiple_of((1 - q) * LANES + above * 4 * LANES, LANES)
        lhs = rim_ref[i].reshape(groups * GROUP, lanes)
        out_ref[i] = nn(lhs, tall_ref[r, pl.ds(start, lanes), :])


def across_kernel(
    inv_root, parts, turned_ref, halo_ref, tall_ref, rim_ref, extra_ref, pad
):
    above = rim_scores(inv_root, parts, 0, turned_ref, halo_ref, pad, rim_ref)
    rim_values(rim_ref, tall_ref, above, extra_ref)


def slice_kernel(edit_ref, across_ref, beyond_ref, sems):
    rows = edit_ref.shape[0]
    odd = lax.rem(lax.axis_index("space"), 2)
    copies = []
    count = sems.shape[0] // 2
    step = RADIUS // count
    for start, ref in ((odd, beyond_ref), (1 - odd, across_ref)):
        for i in range(count):
            block = edit_ref.at[pl.ds((rows - RADIUS) * start + i * step, step)]
            copies.append(
                pltpu.make_async_copy(
                    block, ref.at[i * step : (i + 1) * step], sems.at[len(copies)]
                )
            )
            copies[-1].start()
    for copy in copies:
        copy.wait()


def row_chunks(rims, corr_ref, r, rows):
    pieces = []
    half = rows // 2
    for q in range(rows // PER):
        y = q * PER + r
        parts = []
        for c in range(q, q + POS):
            if c < 2:
                part = rims[0, y, :, :, c * LANES : (c + 1) * LANES]
            elif c < 2 + rows // PER:
                part = corr_ref[y, :, :, (c - 2) * LANES : (c - 1) * LANES]
            else:
                at = c - 2 - rows // PER
                part = rims[1, y - half, :, :, at * LANES : (at + 1) * LANES]
            parts.append(part.reshape(part.shape[0] * part.shape[1], LANES))
        pieces.append(jnp.concatenate(parts, axis=1))
    return jnp.concatenate(pieces, axis=0)


def outer_kernel(
    inv_root,
    pixels,
    parts,
    turned_ref,
    corr_ref,
    rim_ref,
    extra_ref,
    own_ref,
    beyond_ref,
    tall_ref,
    bias_ref,
    head_ref,
    *rest,
):
    gate_ref = rest[0]
    piece_refs = rest[1 : 1 + parts]
    pad, rims, extra, stage = rest[1 + parts :]
    rows, groups = turned_ref.shape[:2]
    above, _ = edge_spot(parts, 1)
    rims[1 - above] = rim_ref[...]
    extra[1 - above] = extra_ref[...]
    rim_scores(inv_root, parts, 1, turned_ref, beyond_ref, pad, rims.at[above])
    rim_values(rims.at[above], tall_ref, above, extra.at[above])
    bias, head = bias_ref[...], head_ref[...]
    kout = bias.shape[1]
    cols = groups * GROUP
    turn = mirror(cols)
    hidden = jnp.zeros((1, kout), F32)
    slopes = jnp.zeros((1, kout), F32)
    total = None
    for r in range(PER):
        corr = row_chunks(rims, corr_ref, r, rows)
        spots = [(q * PER + r, q // 2, q % 2 * PER + r) for q in range(rows // PER)]
        value = jnp.concatenate([own_ref[y] + extra[h, i] for y, h, i in spots], axis=0) + bias
        gating = jax.nn.sigmoid(value)
        act = value * gating
        slope = gating * (1.0 + value * (1.0 - gating))
        hidden = hidden + jnp.sum(act, axis=0, keepdims=True)
        slopes = slopes + jnp.sum(slope, axis=0, keepdims=True)
        pre = (slope * head).astype(BF16)
        for q in range(rows // PER):
            gate_ref[q * PER + r] = nn(turn, pre[q * cols : (q + 1) * cols]).astype(BF16)
        grad = tn(pre, corr)
        if r:
            grad = pltpu.roll(grad, POS * LANES - r * WIN, 1)
        total = grad if total is None else total + grad
    share = stage.shape[0] // parts
    stage[...] = jnp.zeros(stage.shape, F32)
    for p in range(POS):
        row, _ = spread(p)
        table = spread_table(p, 0)
        left = total[:, p * LANES : (p + 1) * LANES]
        packed = None
        for _ in range(3):
            term = left.astype(BF16)
            left = left - term.astype(F32)
            part = nt(table, term)
            packed = part if packed is None else packed + part
        stage[row : row + table.shape[0]] += packed
    scale = 1.0 / pixels
    stage[:STAT] = stage[:STAT] * scale
    stage[STAT : STAT + 1] = head * slopes * scale
    stage[STAT + 1 : STAT + 2] = hidden * scale
    score = jnp.sum(hidden * head, axis=1, keepdims=True) * scale
    me = lax.axis_index("space")
    for k in range(parts):
        start = pl.multiple_of(partner(me, k, parts) * share, 8)
        piece_refs[k][:share] = stage[pl.ds(start, share), :]
        piece_refs[k][share:] = jnp.broadcast_to(score, (8, kout))


def back_chunks(gate_ref, wide_ref, r, rows, groups):
    quarter = rows // PER
    lhs = jnp.concatenate([gate_ref[q * PER + r] for q in range(quarter)], axis=0)
    out = []
    for pos in range(POS):
        grad = nn(lhs, wide_ref[r, :, pos * LANES : (pos + 1) * LANES])
        grad = skew(grad.reshape(quarter * groups, GROUP, LANES), 0)
        out.append(grad.astype(BF16).reshape(quarter, groups, GROUP, LANES))
    return out


def rim_kernel(gate_ref, wide_ref, source_ref, across_ref, beyond_ref, band_lo, band_hi, sums):
    rows, groups, _, chan = source_ref.shape
    half = rows // 2
    quarter = rows // PER
    zero = jnp.zeros((groups, GROUP, LANES), BF16)
    for r in range(PER):
        for q in range(quarter):
            y = q * PER + r
            for c in (0, 1, 6, 7):
                pos = c - q
                band, row = (band_lo, y) if c < 2 else (band_hi, y - half)
                if not 0 <= row < half:
                    continue
                at = (c if c < 2 else c - 6) * LANES
                if 0 <= pos < POS:
                    grad = nn(gate_ref[y], wide_ref[r, :, pos * LANES : (pos + 1) * LANES])
                    part = skew(grad.reshape(groups, GROUP, LANES), 0).astype(BF16)
                else:
                    part = zero
                band[row, :, :, at : at + LANES] = part
    sums[...] = jnp.zeros(sums.shape, F32)

    def body(g, carry):
        start = g * GROUP
        for i, band in enumerate((band_lo, band_hi)):
            lhs = band[:, g].reshape(half * GROUP, 2 * LANES)
            rhs = source_ref[i * half : (i + 1) * half, g].reshape(half * GROUP, chan)
            grad = tn(lhs, rhs).reshape(8, WIN, chan)
            sums[8 * i : 8 * i + 8, start : start + WIN, :] += grad
        return carry

    for g in range(groups):
        body(g, 0)
    cols = groups * GROUP
    odd = lax.rem(lax.axis_index("space"), 2)
    low = pl.multiple_of(8 * odd, 8)
    high = pl.multiple_of(8 - 8 * odd, 8)
    across_ref[...] = sums[pl.ds(high, 8), RADIUS : RADIUS + cols].astype(BF16)
    beyond_ref[...] = sums[pl.ds(low, 8), RADIUS : RADIUS + cols].astype(BF16)


def back_kernel(
    parts,
    gate_ref,
    wide_ref,
    source_ref,
    own_pad,
    across_ref,
    beyond_ref,
    source_out,
    edit_out,
    pad,
    band,
    sums,
):
    rows, groups, _, chan = source_ref.shape
    half = rows // 2
    quarter = rows // PER
    for kind, ref in ((0, across_ref), (1, beyond_ref)):
        above, inside = edge_spot(parts, kind)
        fill_halo(pad, 8 * above, ref, inside)
    fill_columns(pad, 0, 16, groups * GROUP)
    zero = jnp.zeros((PER, groups, GROUP, LANES), BF16)
    for q, c in ((1, 0), (3, 2), (0, 5), (2, 7)):
        band[q * PER : (q + 1) * PER, :, :, c * LANES : (c + 1) * LANES] = zero
    for r in range(PER):
        for pos, part in enumerate(back_chunks(gate_ref, wide_ref, r, rows, groups)):
            for q in range(quarter):
                at = (q + pos) * LANES
                band[q * PER + r, :, :, at : at + LANES] = part[q]
    sums[...] = jnp.zeros(sums.shape, F32)

    def body(g, carry):
        start = g * GROUP
        near = source_ref[:, g].reshape(rows * GROUP, chan)
        for s in range(rows // 8):
            at = (2 + 2 * s) * LANES
            lhs = band[:, g, :, at : at + 2 * LANES].reshape(rows * GROUP, 2 * LANES)
            grad = tn(lhs, near).reshape(8, WIN, chan)
            sums[8 * s : 8 * s + 8, start : start + WIN, :] += grad
        for i in range(2):
            at = i * 2 * LANES
            lhs = band[i * half : (i + 1) * half, g, :, at : at + 6 * LANES]
            spots = [window(pad, 8 * i, 8, g), window(own_pad, 0, rows, g)]
            rhs = jnp.concatenate(spots[::-1] if i else spots, axis=0)
            grad = nn(lhs.reshape(half * GROUP, 6 * LANES), rhs)
            source_out[i * half : (i + 1) * half, g] = grad.reshape(half, GROUP, chan)
        return carry

    for g in range(groups):
        body(g, 0)
    cols = groups * GROUP
    edit_out[...] = sums[:, RADIUS : RADIUS + cols]


def partner(me, step, count):
    if count & (count - 1):
        return (me + step + count) % count
    return me ^ abs(step)


def judge_kernel(pairs, first_ref, second_ref, win_ref, *rest):
    piece_refs = rest[:pairs]
    total_ref, grad_ref, loss_ref = rest[pairs:]
    share = total_ref.shape[0]
    me = lax.axis_index("pair")
    first, second, win = first_ref[...], second_ref[...], win_ref[...]
    hots, margin = [], jnp.zeros(first.shape, F32)
    for k in range(pairs):
        pid = partner(me, -k, pairs)
        hot = (first == pid).astype(F32) - (second == pid).astype(F32)
        score = piece_refs[k][share : share + 1, 0:1]
        margin = margin + hot * score
        hots.append(hot)
    sign = 2.0 * win.astype(F32) - 1.0
    loss = jnp.mean(jax.nn.softplus(-sign * margin), axis=1, keepdims=True)
    loss_ref[...] = jnp.broadcast_to(loss, loss_ref.shape)
    margin_grad = -sign * jax.nn.sigmoid(-sign * margin)
    total = jnp.zeros(total_ref.shape, F32)
    for k in range(pairs):
        grad = jnp.sum(margin_grad * hots[k], axis=1, keepdims=True)
        if k == 0:
            grad_ref[...] = jnp.broadcast_to(grad, grad_ref.shape)
        total = total + grad * piece_refs[k][:share]
    total_ref[...] = total


def gather_kernel(parts, *rest):
    piece_refs = rest[:parts]
    loss_ref, conv_ref, bias_ref, head_ref, loss_out, stage = rest[parts:]
    loss_out[...] = loss_ref[...]
    share = piece_refs[0].shape[0]
    me = lax.axis_index("space")
    for k in range(parts):
        start = pl.multiple_of(partner(me, -k, parts) * share, 8)
        stage[pl.ds(start, share), :] = piece_refs[k][...]
    conv_ref[...] = stage[: conv_ref.shape[0]]
    bias_ref[...] = stage[STAT : STAT + 1]
    head_ref[...] = stage[STAT + 1 : STAT + 2]


def finish_kernel(
    inv_root,
    parts,
    grad_ref,
    source_ref,
    edit_ref,
    across_ref,
    beyond_ref,
    source_hbm,
    edit_hbm,
    source_out,
    edit_out,
    sems,
):
    scale = grad_ref[0:1, 0:1].reshape(1, 1, 1) * inv_root
    rows = edit_ref.shape[0]
    copies = []

    def send(out, hbm, at):
        copies.append(pltpu.make_async_copy(out.at[at], hbm.at[at], sems.at[len(copies)]))
        copies[-1].start()

    for y in range(0, rows, 4):
        at = slice(y, y + 4)
        source_out[at] = (source_ref[at] * scale).astype(BF16)
        send(source_out, source_hbm, at)
    for kind, ref in ((0, across_ref), (1, beyond_ref)):
        above, inside = edge_spot(parts, kind)
        for y in (0, 4):
            at = pl.ds((rows - 8) * above + y, 4)
            extra = jnp.where(inside, ref[y : y + 4].astype(F32), 0.0)
            edit_out[at] = ((edit_ref[at] + extra) * scale).astype(BF16)
            send(edit_out, edit_hbm, at)
    for copy in copies:
        copy.wait()


def call(kernel, outs, scratch, flops, *args, far=(), far_out=False):
    nbytes = sum(a.size * a.dtype.itemsize for a in args)
    spaces = [pltpu.HBM if i in far else pltpu.VMEM for i in range(len(args))]
    return pl.pallas_call(
        kernel,
        out_shape=outs,
        in_specs=[pl.BlockSpec(memory_space=space) for space in spaces],
        **({"out_specs": [pl.BlockSpec(memory_space=pltpu.HBM)] * len(outs)} if far_out else {}),
        scratch_shapes=scratch,
        compiler_params=pltpu.CompilerParams(vmem_limit_bytes=VMEM_LIMIT),
        cost_estimate=pl.CostEstimate(flops=flops, bytes_accessed=nbytes, transcendentals=0),
    )(*map(pltpu.with_memory_space_constraint, args, spaces))


def result(dims, dtype=F32):
    return jax.ShapeDtypeStruct(dims, dtype)


def shape(dims, dtype=F32):
    return pltpu.VMEM(dims, dtype)


def around(axis, step):
    count = lax.axis_size(axis)
    return [(i, partner(i, step, count)) for i in range(count)]


def beyond_pairs(teams, space):
    table = []
    for team in range(teams):
        for i in range(space):
            other = i + 1 if i % 2 else i - 1
            to = (team, other) if 0 <= other < space else (team ^ 1 if team ^ 1 < teams else team, i)
            table.append((team * space + i, to[0] * space + to[1]))
    return table


def local(
    source_feats, edit_feats, conv_weight, conv_bias, head_weight, comp_first, comp_second, comp_win
):
    _, rows, columns, chan = source_feats.shape
    kout, disp = conv_weight.shape
    inv_root = chan ** (-0.5)
    space, pairs = lax.axis_size("space"), lax.axis_size("pair")
    pixels = rows * space * columns
    groups = columns // GROUP
    wide_cols = columns + 2 * RADIUS
    share = -(-(disp + 2) // (8 * space)) * 8
    edit = edit_feats[0]
    source = source_feats.reshape(rows, groups, GROUP, chan)
    to_across = [(i, i ^ 1 if i ^ 1 < space else i) for i in range(space)]
    to_beyond = beyond_pairs(lax.axis_size("groups"), space)
    across, beyond = call(
        slice_kernel,
        (shape((RADIUS, columns, chan), BF16),) * 2,
        [pltpu.SemaphoreType.DMA((2,))],
        10**4,
        edit,
        far=(0,),
    )
    across = lax.ppermute(across, "space", to_across)
    beyond = lax.ppermute(beyond, ("groups", "space"), to_beyond)
    near = (rows, groups, GROUP, chan)
    rim_shape = (rows // 2, groups, GROUP, 8 * WIN)
    held, own_pad, turned, corr, wide, tall, own = call(
        functools.partial(inner_kernel, inv_root),
        (
            shape(near, BF16),
            shape((rows, wide_cols, chan), BF16),
            shape(near, BF16),
            shape((rows, groups, GROUP, rows * WIN), BF16),
            shape((PER, kout, POS * LANES), BF16),
            shape((PER, (POS + 2) * LANES, kout), BF16),
            shape((rows, columns, kout)),
        ),
        [pltpu.VMEM((disp, kout), BF16), pltpu.SemaphoreType.DMA((3,))],
        2 * 10**9,
        source,
        edit,
        conv_weight.T,
        far=(0, 1, 2),
    )
    rim, extra = call(
        functools.partial(across_kernel, inv_root, space),
        (shape(rim_shape, BF16), shape((rows // 2, columns, kout))),
        [pltpu.VMEM((RADIUS, wide_cols, chan), BF16)],
        10**9,
        turned,
        across,
        tall,
    )
    gate, *pieces = call(
        functools.partial(outer_kernel, inv_root, pixels, space),
        (shape((rows, columns, kout), BF16),) + (shape((share + 8, kout)),) * space,
        [
            pltpu.VMEM((RADIUS, wide_cols, chan), BF16),
            pltpu.VMEM((2,) + rim_shape, BF16),
            pltpu.VMEM((2, rows // 2, columns, kout), F32),
            pltpu.VMEM((share * space, kout), F32),
        ],
        2 * 10**9,
        turned,
        corr,
        rim,
        extra,
        own,
        beyond,
        tall,
        conv_bias[None],
        head_weight[None],
    )
    quarter = pieces[0]
    for k in range(1, space):
        quarter = quarter + lax.ppermute(pieces[k], "space", around("space", k))
    rim_across, rim_beyond = call(
        rim_kernel,
        (shape((RADIUS, columns, chan), BF16),) * 2,
        [
            pltpu.VMEM((rows // 2, groups, GROUP, 8 * WIN), BF16),
            pltpu.VMEM((rows // 2, groups, GROUP, 8 * WIN), BF16),
            pltpu.VMEM((2 * RADIUS, wide_cols, chan), F32),
        ],
        10**9,
        gate,
        wide,
        held,
    )
    from_across = lax.ppermute(rim_across, "space", to_across)
    from_beyond = lax.ppermute(rim_beyond, ("groups", "space"), to_beyond)
    source_sum, edit_sum = call(
        functools.partial(back_kernel, space),
        (shape((rows, groups, GROUP, chan)), shape((rows, columns, chan))),
        [
            pltpu.VMEM((2 * RADIUS, wide_cols, chan), BF16),
            pltpu.VMEM((rows, groups, GROUP, (rows + 2 * RADIUS) * WIN), BF16),
            pltpu.VMEM((rows, wide_cols, chan), F32),
        ],
        4 * 10**9,
        gate,
        wide,
        held,
        own_pad,
        across,
        beyond,
    )
    others = [quarter] + [lax.ppermute(quarter, "pair", around("pair", k)) for k in range(1, pairs)]
    *others, source_sum, edit_sum = lax.optimization_barrier((*others, source_sum, edit_sum))
    total, score_grad, loss = call(
        functools.partial(judge_kernel, pairs),
        (shape((share, kout)), shape((8, LANES)), shape((1, LANES))),
        [],
        10**6,
        comp_first[None],
        comp_second[None],
        comp_win[None],
        *others,
    )
    gathered = [total] + [lax.ppermute(total, "space", around("space", k)) for k in range(1, space)]
    source_grad, edit_grad = call(
        functools.partial(finish_kernel, inv_root, space),
        (result((rows, columns, chan), BF16),) * 2,
        [
            pltpu.VMEM((rows, columns, chan), BF16),
            pltpu.VMEM((rows, columns, chan), BF16),
            pltpu.SemaphoreType.DMA((8,)),
        ],
        10**7,
        score_grad,
        source_sum.reshape(rows, columns, chan),
        edit_sum,
        from_across,
        from_beyond,
        far_out=True,
    )
    *gathered, source_grad, edit_grad = lax.optimization_barrier((*gathered, source_grad, edit_grad))
    conv_grad, bias_grad, head_grad, loss = call(
        functools.partial(gather_kernel, space),
        (result((disp, kout)), result((1, kout)), result((1, kout)), result((1, LANES))),
        [pltpu.VMEM((share * space, kout), F32)],
        10**6,
        *gathered,
        loss,
    )
    return (
        source_grad[None],
        edit_grad[None],
        conv_grad.T,
        bias_grad[0],
        head_grad[0],
        loss[0, :1],
    )


def solution(mesh):
    in_specs = (
        P(("groups", "pair"), "space", None, None),
        P(("groups", "pair"), "space", None, None),
        P(),
        P(),
        P(),
        P("groups"),
        P("groups"),
        P("groups"),
    )
    out_specs = (
        P(("groups", "pair"), "space", None, None),
        P(("groups", "pair"), "space", None, None),
        P("groups", None),
        P("groups"),
        P("groups"),
        P("groups"),
    )
    return jax.shard_map(local, mesh=mesh, in_specs=in_specs, out_specs=out_specs, check_vma=False)
```

```python
import functools

import jax
import jax.numpy as jnp
from jax import lax
from jax.experimental import pallas as pl
from jax.experimental.pallas import tpu as pltpu
from jax.sharding import PartitionSpec as P

RADIUS = 8
SPAN = 2 * RADIUS + 1
GROUP = 16
WIN = GROUP + 2 * RADIUS
LANES = 128
PER = LANES // WIN
POS = 5
STAT = SPAN * SPAN
F32 = jnp.float32
BF16 = jnp.bfloat16
VMEM_LIMIT = 24 * 1024 * 1024


def nt(a, b):
    return lax.dot_general(a, b, (((1,), (1,)), ((), ())), preferred_element_type=F32)


def nn(a, b):
    return lax.dot_general(a, b, (((1,), (0,)), ((), ())), preferred_element_type=F32)


def tn(a, b):
    return lax.dot_general(a, b, (((0,), (0,)), ((), ())), preferred_element_type=F32)


def iota(shape, dim):
    return lax.broadcasted_iota(jnp.int32, shape, dim)


def mirror(size):
    row, col = iota((size, size), 0), iota((size, size), 1)
    return (col == (row ^ (GROUP - 1))).astype(F32).astype(BF16)


def spread(p):
    first = p * PER * SPAN
    return first // 8 * 8, first % 8


def spread_table(p, dim):
    _, offset = spread(p)
    count = (PER if p < POS - 1 else 1) * SPAN
    dims = [LANES, LANES]
    dims[dim] = -(-(count + offset) // 8) * 8 if p < POS - 1 else count
    place, lane = iota(dims, dim), iota(dims, 1 - dim)
    dy, t = lane // WIN, lane % WIN
    hit = (place == dy * SPAN + t + offset) & (t < SPAN) & (dy * SPAN < count)
    return hit.astype(F32).astype(BF16)


def skew(values, shift):
    return pltpu.roll(values, shift, 2, stride=1, stride_axis=1)


def skew_wide(values, shift):
    parts = []
    for start in range(0, values.shape[-1], LANES):
        parts.append(skew(values[:, :, start : start + LANES], shift))
    return parts


def fill_columns(pad_ref, row, rows, cols):
    zero = jnp.zeros((rows, RADIUS, pad_ref.shape[2]), BF16)
    pad_ref[row : row + rows, 0:RADIUS] = zero
    pad_ref[row : row + rows, RADIUS + cols :] = zero


def fill_padded(pad_ref, row, block_ref):
    rows, cols = block_ref.shape[:2]
    fill_columns(pad_ref, row, rows, cols)
    pad_ref[row : row + rows, RADIUS : RADIUS + cols] = block_ref[...]


def window(pad_ref, row, rows, g):
    block = pad_ref[row : row + rows, g * GROUP : g * GROUP + WIN, :]
    return block.reshape(rows * WIN, block.shape[2])


def correlate_set(lhs, pad_ref, row, g, inv_root, out_ref, spot, lane):
    ys = lhs.shape[0] // GROUP
    scores = nt(lhs, window(pad_ref, row, 8, g)) * inv_root
    scores = scores.reshape(ys, GROUP, 8 * WIN)
    for i, part in enumerate(skew_wide(scores, LANES - GROUP + 1)):
        at = lane + i * LANES
        out_ref[spot, g, :, at : at + LANES] = part.astype(BF16)


def spread_weights(weight, wide_ref, tall_ref):
    kout = weight.shape[1]
    wides, talls = [], []
    for p in range(POS):
        row, _ = spread(p)
        table = spread_table(p, 0)
        part = weight[row : row + table.shape[0], :]
        wides.append(tn(part, table))
        talls.append(nn(spread_table(p, 1), part))
    base = jnp.concatenate(wides, axis=1)
    tall = jnp.concatenate(talls, axis=0).astype(BF16)[: SPAN * WIN]
    tall_rows = tall_ref.shape[1]
    for r in range(PER):
        edge = jnp.zeros((kout, LANES), BF16)
        moved = base if r == 0 else pltpu.roll(base, r * WIN, 1)
        wide_ref[r] = jnp.concatenate([edge, moved.astype(BF16), edge], axis=1)
        start = LANES + r * WIN
        tall_ref[r, :start] = jnp.zeros((start, kout), BF16)
        tall_ref[r, start : start + SPAN * WIN] = tall
        tall_ref[r, start + SPAN * WIN :] = jnp.zeros((tall_rows - start - SPAN * WIN, kout), BF16)


def load_kernel(
    source_hbm,
    edit_hbm,
    weight_hbm,
    source_ref,
    pad,
    turned_ref,
    wide_ref,
    tall_ref,
    weight,
    sems,
):
    rows, groups, _, chan = source_ref.shape
    cols = groups * GROUP
    weight_copy = pltpu.make_async_copy(weight_hbm, weight, sems.at[2])
    source_copy = pltpu.make_async_copy(source_hbm, source_ref, sems.at[1])
    edit_copy = pltpu.make_async_copy(edit_hbm, pad.at[:, RADIUS : RADIUS + cols], sems.at[0])
    weight_copy.start()
    source_copy.start()
    edit_copy.start()
    fill_columns(pad, 0, rows, cols)
    turn = mirror(rows * GROUP)
    weight_copy.wait()
    spread_weights(weight, wide_ref, tall_ref)
    source_copy.wait()
    for g in range(groups):
        lhs = nn(turn, source_ref[:, g].reshape(rows * GROUP, chan)).astype(BF16)
        turned_ref[:, g] = lhs.reshape(rows, GROUP, chan)
    edit_copy.wait()


def inner_kernel(inv_root, turned_ref, pad, tall_ref, corr_ref, own_ref):
    rows, groups, _, chan = turned_ref.shape
    for g in range(groups):
        lhs = turned_ref[:, g].reshape(rows * GROUP, chan)
        for s in range(rows // 8):
            correlate_set(lhs, pad, 8 * s, g, inv_root, corr_ref, slice(0, rows), 2 * s * LANES)
    cols = groups * GROUP
    for q in range(rows // PER):
        start = (3 - q) * LANES
        for r in range(PER):
            lhs = corr_ref[q * PER + r].reshape(cols, 4 * LANES)
            own_ref[q * PER + r] = nn(lhs, tall_ref[r, start : start + 4 * LANES])


def edge_spot(parts, kind):
    me = lax.axis_index("space")
    above = lax.rem(me, 2) ^ 1 if kind == 0 else lax.rem(me, 2)
    inside = jnp.where(above == 1, me != parts - 1, me != 0)
    return above, inside


def fill_halo(pad_ref, row, halo_ref, inside):
    cols = halo_ref.shape[1]
    pad_ref[pl.ds(row, 8), RADIUS : RADIUS + cols] = jnp.where(
        inside, halo_ref[...], jnp.zeros(halo_ref.shape, BF16)
    )


def rim_scores(inv_root, parts, kind, turned_ref, halo_ref, pad, rim_ref):
    rows, groups, _, chan = turned_ref.shape
    half = rows // 2
    above, inside = edge_spot(parts, kind)
    fill_columns(pad, 0, 8, groups * GROUP)
    fill_halo(pad, 0, halo_ref, inside)
    start = half * above
    for g in range(groups):
        lhs = turned_ref[pl.ds(start, half), g].reshape(half * GROUP, chan)
        correlate_set(lhs, pad, 0, g, inv_root, rim_ref, slice(0, half), 0)
    return above


def rim_values(rim_ref, tall_ref, above, out_ref):
    half, groups, _, lanes = rim_ref.shape
    for i in range(half):
        q, r = i // PER, i % PER
        start = pl.multiple_of((1 - q) * LANES + above * 4 * LANES, LANES)
        lhs = rim_ref[i].reshape(groups * GROUP, lanes)
        out_ref[i] = nn(lhs, tall_ref[r, pl.ds(start, lanes), :])


def half_rows(above, own_ref, extra, corr_ref, rim, strip, bias_ref, head_ref, gate_ref, gate_at):
    half, groups = rim.shape[:2]
    cols = groups * GROUP
    rim_lanes, own_lanes = rim.shape[3], corr_ref.shape[3]

    @pl.when(above == 0)
    def _():
        strip[:, :, :, :rim_lanes] = rim[...]
        strip[:, :, :, rim_lanes:] = corr_ref[:half]

    @pl.when(above == 1)
    def _():
        strip[:, :, :, :own_lanes] = corr_ref[half:]
        strip[:, :, :, own_lanes:] = rim[...]

    bias, head = bias_ref[...], head_ref[...]
    kout = bias.shape[1]
    turn = mirror(cols)
    hidden = jnp.zeros((1, kout), F32)
    slopes = jnp.zeros((1, kout), F32)
    total = None
    for r in range(PER):
        rows = [q * PER + r for q in range(half // PER)]
        value = jnp.concatenate([own_ref[half * above + i] + extra[i] for i in rows], axis=0) + bias
        gating = jax.nn.sigmoid(value)
        act = value * gating
        slope = gating * (1.0 + value * (1.0 - gating))
        hidden = hidden + jnp.sum(act, axis=0, keepdims=True)
        slopes = slopes + jnp.sum(slope, axis=0, keepdims=True)
        pre = (slope * head).astype(BF16)
        for q, i in enumerate(rows):
            gate_ref[gate_at + i] = nn(turn, pre[q * cols : (q + 1) * cols]).astype(BF16)
        corr = [strip[i, :, :, i // PER * LANES : (i // PER + POS) * LANES] for i in rows]
        corr = jnp.concatenate([c.reshape(cols, POS * LANES) for c in corr], axis=0)
        grad = tn(pre, corr)
        if r:
            grad = pltpu.roll(grad, POS * LANES - r * WIN, 1)
        total = grad if total is None else total + grad
    return hidden, slopes, total


def across_kernel(
    inv_root,
    parts,
    turned_ref,
    corr_ref,
    own_ref,
    halo_ref,
    tall_ref,
    bias_ref,
    head_ref,
    gate_ref,
    sums_ref,
    total_ref,
    pad,
    rim,
    extra,
    strip,
):
    above = rim_scores(inv_root, parts, 0, turned_ref, halo_ref, pad, rim)
    rim_values(rim, tall_ref, above, extra)
    hidden, slopes, total_ref[...] = half_rows(
        above, own_ref, extra, corr_ref, rim, strip, bias_ref, head_ref, gate_ref, 0
    )
    sums_ref[0:1] = hidden
    sums_ref[1:2] = slopes


def slice_kernel(edit_ref, across_ref, beyond_ref, sems):
    rows = edit_ref.shape[0]
    odd = lax.rem(lax.axis_index("space"), 2)
    copies = []
    count = sems.shape[0] // 2
    step = RADIUS // count
    for start, ref in ((odd, beyond_ref), (1 - odd, across_ref)):
        for i in range(count):
            block = edit_ref.at[pl.ds((rows - RADIUS) * start + i * step, step)]
            copies.append(
                pltpu.make_async_copy(
                    block, ref.at[i * step : (i + 1) * step], sems.at[len(copies)]
                )
            )
            copies[-1].start()
    for copy in copies:
        copy.wait()


def put_rows(stage, share, row, values):
    done = 0
    while done < values.shape[0]:
        piece, at = divmod(row + done, share - 1)
        count = min(values.shape[0] - done, share - 1 - at)
        start = piece * share + at
        stage[start : start + count] = values[done : done + count]
        done += count


def outer_kernel(
    inv_root,
    pixels,
    parts,
    turned_ref,
    corr_ref,
    own_ref,
    halo_ref,
    tall_ref,
    bias_ref,
    head_ref,
    near_gate_ref,
    near_sums_ref,
    near_total_ref,
    *rest,
):
    gate_ref, *piece_refs, pad, rim, extra, strip, stage = rest
    half = rim.shape[0]
    above = rim_scores(inv_root, parts, 1, turned_ref, halo_ref, pad, rim)
    rim_values(rim, tall_ref, above, extra)
    gate_ref[pl.ds(half * (1 - above), half)] = near_gate_ref[...]
    hidden, slopes, total = half_rows(
        above, own_ref, extra, corr_ref, rim, strip, bias_ref, head_ref, gate_ref, half * above
    )
    hidden = hidden + near_sums_ref[0:1]
    slopes = slopes + near_sums_ref[1:2]
    total = total + near_total_ref[...]
    head = head_ref[...]
    kout = head.shape[1]
    share = stage.shape[0] // parts
    stage[...] = jnp.zeros(stage.shape, F32)
    scale = 1.0 / pixels
    turned = jnp.transpose(total) * scale
    for dy in range(SPAN):
        put_rows(stage, share, dy * SPAN, turned[dy * WIN : dy * WIN + SPAN])
    put_rows(stage, share, STAT, jnp.concatenate([head * slopes, hidden], axis=0) * scale)
    score = jnp.sum(hidden * head, axis=1, keepdims=True) * scale
    me = lax.axis_index("space")
    for k in range(parts):
        start = pl.multiple_of(partner(me, k, parts) * share, 8)
        piece_refs[k][...] = stage[pl.ds(start, share), :]
        piece_refs[k][share - 1 :] = jnp.broadcast_to(score, (1, kout))


def back_chunks(gate_ref, wide_ref, r, rows, groups):
    quarter = rows // PER
    lhs = jnp.concatenate([gate_ref[q * PER + r] for q in range(quarter)], axis=0)
    out = []
    for pos in range(POS):
        grad = nn(lhs, wide_ref[r, :, (pos + 1) * LANES : (pos + 2) * LANES])
        grad = skew(grad.reshape(quarter * groups, GROUP, LANES), 0)
        out.append(grad.astype(BF16).reshape(quarter, groups, GROUP, LANES))
    return out


def rim_kernel(kind, parts, gate_ref, wide_ref, source_ref, out_ref, band, sums):
    rows, groups, _, chan = source_ref.shape
    half = rows // 2
    above, _ = edge_spot(parts, kind)
    first = 0 if gate_ref.shape[0] == half else half * above
    for i in range(half):
        q, r = i // PER, i % PER
        start = pl.multiple_of((1 - q) * LANES + above * 4 * LANES, LANES)
        grad = nn(gate_ref[first + i], wide_ref[r, :, pl.ds(start, 2 * LANES)])
        parts_of = skew_wide(grad.reshape(groups, GROUP, 2 * LANES), 0)
        band[i] = jnp.concatenate(parts_of, axis=2).astype(BF16)
    sums[...] = jnp.zeros(sums.shape, F32)
    for g in range(groups):
        lhs = band[:, g].reshape(half * GROUP, 2 * LANES)
        rhs = source_ref[pl.ds(half * above, half), g].reshape(half * GROUP, chan)
        sums[:, g * GROUP : g * GROUP + WIN, :] += tn(lhs, rhs).reshape(8, WIN, chan)
    out_ref[...] = sums[:, RADIUS : RADIUS + groups * GROUP].astype(BF16)


def back_kernel(
    parts,
    gate_ref,
    wide_ref,
    source_ref,
    own_pad,
    across_ref,
    beyond_ref,
    source_out,
    edit_out,
    pad,
    band,
    sums,
):
    rows, groups, _, chan = source_ref.shape
    half = rows // 2
    quarter = rows // PER
    for kind, ref in ((0, across_ref), (1, beyond_ref)):
        above, inside = edge_spot(parts, kind)
        fill_halo(pad, 8 * above, ref, inside)
    fill_columns(pad, 0, 16, groups * GROUP)
    zero = jnp.zeros((PER, groups, GROUP, LANES), BF16)
    for q, c in ((1, 0), (3, 2), (0, 5), (2, 7)):
        band[q * PER : (q + 1) * PER, :, :, c * LANES : (c + 1) * LANES] = zero
    for r in range(PER):
        for pos, part in enumerate(back_chunks(gate_ref, wide_ref, r, rows, groups)):
            for q in range(quarter):
                at = (q + pos) * LANES
                band[q * PER + r, :, :, at : at + LANES] = part[q]
    sums[...] = jnp.zeros(sums.shape, F32)

    def body(g, carry):
        start = g * GROUP
        near = source_ref[:, g].reshape(rows * GROUP, chan)
        for s in range(rows // 8):
            at = (2 + 2 * s) * LANES
            lhs = band[:, g, :, at : at + 2 * LANES].reshape(rows * GROUP, 2 * LANES)
            grad = tn(lhs, near).reshape(8, WIN, chan)
            sums[8 * s : 8 * s + 8, start : start + WIN, :] += grad
        for i in range(2):
            at = i * 2 * LANES
            lhs = band[i * half : (i + 1) * half, g, :, at : at + 6 * LANES]
            spots = [window(pad, 8 * i, 8, g), window(own_pad, 0, rows, g)]
            rhs = jnp.concatenate(spots[::-1] if i else spots, axis=0)
            grad = nn(lhs.reshape(half * GROUP, 6 * LANES), rhs)
            source_out[i * half : (i + 1) * half, g] = grad.reshape(half, GROUP, chan)
        return carry

    for g in range(groups):
        body(g, 0)
    cols = groups * GROUP
    edit_out[...] = sums[:, RADIUS : RADIUS + cols]


def partner(me, step, count):
    if count & (count - 1):
        return (me + step + count) % count
    return me ^ abs(step)


def judge_kernel(pairs, first_ref, second_ref, win_ref, *rest):
    piece_refs = rest[:pairs]
    total_ref, grad_ref, loss_ref = rest[pairs:]
    share = total_ref.shape[0]
    me = lax.axis_index("pair")
    first, second, win = first_ref[...], second_ref[...], win_ref[...]
    hots, margin = [], jnp.zeros(first.shape, F32)
    for k in range(pairs):
        pid = partner(me, -k, pairs)
        hot = (first == pid).astype(F32) - (second == pid).astype(F32)
        score = piece_refs[k][share - 1 : share, 0:1]
        margin = margin + hot * score
        hots.append(hot)
    sign = 2.0 * win.astype(F32) - 1.0
    loss = jnp.mean(jax.nn.softplus(-sign * margin), axis=1, keepdims=True)
    loss_ref[...] = jnp.broadcast_to(loss, loss_ref.shape)
    margin_grad = -sign * jax.nn.sigmoid(-sign * margin)
    total = jnp.zeros(total_ref.shape, F32)
    for k in range(pairs):
        grad = jnp.sum(margin_grad * hots[k], axis=1, keepdims=True)
        if k == 0:
            grad_ref[...] = jnp.broadcast_to(grad, grad_ref.shape)
        total = total + grad * piece_refs[k][...]
    total_ref[...] = total


def gather_kernel(parts, *rest):
    piece_refs = rest[:parts]
    loss_ref, conv_ref, bias_ref, head_ref, loss_out, stage = rest[parts:]
    loss_out[...] = loss_ref[...]
    share = piece_refs[0].shape[0]
    me = lax.axis_index("space")
    for k in range(parts):
        start = pl.multiple_of(partner(me, -k, parts) * share, 8)
        stage[pl.ds(start, share), :] = piece_refs[k][...]
    rows = conv_ref.shape[0]
    for piece in range(-(-rows // (share - 1))):
        row = piece * (share - 1)
        count = min(share - 1, rows - row)
        conv_ref[row : row + count] = stage[piece * share : piece * share + count]
    for i, ref in enumerate((bias_ref, head_ref)):
        piece, at = divmod(STAT + i, share - 1)
        ref[...] = stage[piece * share + at : piece * share + at + 1]


def finish_kernel(
    inv_root,
    parts,
    grad_ref,
    source_ref,
    edit_ref,
    across_ref,
    beyond_ref,
    source_hbm,
    edit_hbm,
    source_out,
    edit_out,
    sems,
):
    scale = grad_ref[0:1, 0:1].reshape(1, 1, 1) * inv_root
    rows = edit_ref.shape[0]
    copies = []

    def send(out, hbm, at):
        copies.append(pltpu.make_async_copy(out.at[at], hbm.at[at], sems.at[len(copies)]))
        copies[-1].start()

    for y in range(0, rows, 4):
        at = slice(y, y + 4)
        source_out[at] = (source_ref[at] * scale).astype(BF16)
        send(source_out, source_hbm, at)
    for kind, ref in ((0, across_ref), (1, beyond_ref)):
        above, inside = edge_spot(parts, kind)
        for y in (0, 4):
            at = pl.ds((rows - 8) * above + y, 4)
            extra = jnp.where(inside, ref[y : y + 4].astype(F32), 0.0)
            edit_out[at] = ((edit_ref[at] + extra) * scale).astype(BF16)
            send(edit_out, edit_hbm, at)
    for copy in copies:
        copy.wait()


def call(kernel, outs, scratch, flops, *args, far=(), far_out=False):
    nbytes = sum(a.size * a.dtype.itemsize for a in args)
    spaces = [pltpu.HBM if i in far else pltpu.VMEM for i in range(len(args))]
    return pl.pallas_call(
        kernel,
        out_shape=outs,
        in_specs=[pl.BlockSpec(memory_space=space) for space in spaces],
        **({"out_specs": [pl.BlockSpec(memory_space=pltpu.HBM)] * len(outs)} if far_out else {}),
        scratch_shapes=scratch,
        compiler_params=pltpu.CompilerParams(vmem_limit_bytes=VMEM_LIMIT),
        cost_estimate=pl.CostEstimate(flops=flops, bytes_accessed=nbytes, transcendentals=0),
    )(*map(pltpu.with_memory_space_constraint, args, spaces))


def result(dims, dtype=F32):
    return jax.ShapeDtypeStruct(dims, dtype)


def shape(dims, dtype=F32):
    return pltpu.VMEM(dims, dtype)


def around(axis, step):
    count = lax.axis_size(axis)
    return [(i, partner(i, step, count)) for i in range(count)]


def beyond_pairs(teams, space):
    table = []
    for team in range(teams):
        for i in range(space):
            other = i + 1 if i % 2 else i - 1
            to = (team, other) if 0 <= other < space else (team ^ 1 if team ^ 1 < teams else team, i)
            table.append((team * space + i, to[0] * space + to[1]))
    return table


def swap(array, axis, bit):
    return lax.ppermute(array, axis, [(i, i ^ bit) for i in range(lax.axis_size(axis))])


def local(
    source_feats, edit_feats, conv_weight, conv_bias, head_weight, comp_first, comp_second, comp_win
):
    _, rows, columns, chan = source_feats.shape
    kout, disp = conv_weight.shape
    inv_root = chan ** (-0.5)
    space, pairs = lax.axis_size("space"), lax.axis_size("pair")
    pixels = rows * space * columns
    assert space & (space - 1) == 0
    groups = columns // GROUP
    wide_cols = columns + 2 * RADIUS
    share = 8
    while (share - 1) * space < disp + 2:
        share += 8
    edit = edit_feats[0]
    source = source_feats.reshape(rows, groups, GROUP, chan)
    to_across = [(i, i ^ 1 if i ^ 1 < space else i) for i in range(space)]
    to_beyond = beyond_pairs(lax.axis_size("groups"), space)
    across, beyond = call(
        slice_kernel,
        (shape((RADIUS, columns, chan), BF16),) * 2,
        [pltpu.SemaphoreType.DMA((2,))],
        10**4,
        edit,
        far=(0,),
    )
    across = lax.ppermute(across, "space", to_across)
    beyond = lax.ppermute(beyond, ("groups", "space"), to_beyond)
    near = (rows, groups, GROUP, chan)
    rim_shape = (rows // 2, groups, GROUP, 8 * WIN)
    held, own_pad, turned, wide, tall = call(
        load_kernel,
        (
            shape(near, BF16),
            shape((rows, wide_cols, chan), BF16),
            shape(near, BF16),
            shape((PER, kout, (POS + 2) * LANES), BF16),
            shape((PER, (POS + 2) * LANES, kout), BF16),
        ),
        [pltpu.VMEM((disp, kout), BF16), pltpu.SemaphoreType.DMA((3,))],
        10**4,
        source,
        edit,
        conv_weight.T,
        far=(0, 1, 2),
    )
    corr, own = call(
        functools.partial(inner_kernel, inv_root),
        (shape((rows, groups, GROUP, rows * WIN), BF16), shape((rows, columns, kout))),
        [],
        2 * 10**9,
        turned,
        own_pad,
        tall,
    )
    work = [
        pltpu.VMEM((RADIUS, wide_cols, chan), BF16),
        pltpu.VMEM(rim_shape, BF16),
        pltpu.VMEM((rows // 2, columns, kout), F32),
        pltpu.VMEM((rows // 2, groups, GROUP, (rows + RADIUS) * WIN), BF16),
    ]
    near_gate, near_sums, near_total = call(
        functools.partial(across_kernel, inv_root, space),
        (
            shape((rows // 2, columns, kout), BF16),
            shape((2, kout)),
            shape((kout, POS * LANES)),
        ),
        work,
        10**9,
        turned,
        corr,
        own,
        across,
        tall,
        conv_bias[None],
        head_weight[None],
    )

    def rim_terms(kind, gates):
        (terms,) = call(
            functools.partial(rim_kernel, kind, space),
            (shape((RADIUS, columns, chan), BF16),),
            [pltpu.VMEM(rim_shape, BF16), pltpu.VMEM((RADIUS, wide_cols, chan), F32)],
            10**9,
            gates,
            wide,
            held,
        )
        return terms

    terms, far = lax.optimization_barrier((rim_terms(0, near_gate), beyond))
    from_across = lax.ppermute(terms, "space", to_across)
    gate, *pieces = call(
        functools.partial(outer_kernel, inv_root, pixels, space),
        (shape((rows, columns, kout), BF16),) + (shape((share, kout)),) * space,
        work + [pltpu.VMEM((share * space, kout), F32)],
        2 * 10**9,
        turned,
        corr,
        own,
        far,
        tall,
        conv_bias[None],
        head_weight[None],
        near_gate,
        near_sums,
        near_total,
    )
    crossings = range(2, space, 2)
    far_terms = rim_terms(1, gate)
    came = {k: swap(pieces[k + 1], "space", 1) for k in (*crossings, 0) if k + 1 < space}
    paired = dict(enumerate(pieces))
    if crossings:
        used = [came[k] for k in crossings]
        far_terms, *used = lax.optimization_barrier((far_terms, *used))
        for k, other in zip(crossings, used):
            paired[k] = pieces[k] + other
    crossed = [swap(paired[k], "space", k) for k in crossings]
    from_beyond = lax.ppermute(far_terms, ("groups", "space"), to_beyond)
    quarter = pieces[0]
    for other in (*(came[k] for k in (0,) if space > 1), *crossed):
        quarter = quarter + other
    source_sum, edit_sum = call(
        functools.partial(back_kernel, space),
        (shape((rows, groups, GROUP, chan)), shape((rows, columns, chan))),
        [
            pltpu.VMEM((2 * RADIUS, wide_cols, chan), BF16),
            pltpu.VMEM((rows, groups, GROUP, (rows + 2 * RADIUS) * WIN), BF16),
            pltpu.VMEM((rows, wide_cols, chan), F32),
        ],
        4 * 10**9,
        gate,
        wide,
        held,
        own_pad,
        across,
        beyond,
    )
    others = [quarter] + [lax.ppermute(quarter, "pair", around("pair", k)) for k in range(1, pairs)]
    *others, source_sum, edit_sum = lax.optimization_barrier((*others, source_sum, edit_sum))
    total, score_grad, loss = call(
        functools.partial(judge_kernel, pairs),
        (shape((share, kout)), shape((8, LANES)), shape((1, LANES))),
        [],
        10**6,
        comp_first[None],
        comp_second[None],
        comp_win[None],
        *others,
    )
    gathered = {0: total}
    for k in crossings:
        gathered[k] = swap(total, "space", k)
    if space > 1:
        gathered[1] = swap(total, "space", 1)
    source_grad, edit_grad = call(
        functools.partial(finish_kernel, inv_root, space),
        (result((rows, columns, chan), BF16),) * 2,
        [
            pltpu.VMEM((rows, columns, chan), BF16),
            pltpu.VMEM((rows, columns, chan), BF16),
            pltpu.SemaphoreType.DMA((8,)),
        ],
        10**7,
        score_grad,
        source_sum.reshape(rows, columns, chan),
        edit_sum,
        from_across,
        from_beyond,
        far_out=True,
    )
    if crossings:
        used = [gathered[k] for k in crossings]
        source_grad, edit_grad, *used = lax.optimization_barrier((source_grad, edit_grad, *used))
        for k, other in zip(crossings, used):
            gathered[k], gathered[k + 1] = other, swap(other, "space", 1)
    gathered = [gathered[k] for k in range(space)]
    conv_grad, bias_grad, head_grad, loss = call(
        functools.partial(gather_kernel, space),
        (result((disp, kout)), result((1, kout)), result((1, kout)), result((1, LANES))),
        [pltpu.VMEM((share * space, kout), F32)],
        10**6,
        *gathered,
        loss,
    )
    return (
        source_grad[None],
        edit_grad[None],
        conv_grad.T,
        bias_grad[0],
        head_grad[0],
        loss[0, :1],
    )


def solution(mesh):
    in_specs = (
        P(("groups", "pair"), "space", None, None),
        P(("groups", "pair"), "space", None, None),
        P(),
        P(),
        P(),
        P("groups"),
        P("groups"),
        P("groups"),
    )
    out_specs = (
        P(("groups", "pair"), "space", None, None),
        P(("groups", "pair"), "space", None, None),
        P("groups", None),
        P("groups"),
        P("groups"),
        P("groups"),
    )
    return jax.shard_map(local, mesh=mesh, in_specs=in_specs, out_specs=out_specs, check_vma=False)
```

```python
import functools

import jax
import jax.numpy as jnp
from jax import lax
from jax.experimental import pallas as pl
from jax.experimental.pallas import tpu as pltpu
from jax.sharding import PartitionSpec as P

RADIUS = 8
SPAN = 2 * RADIUS + 1
GROUP = 16
WIN = GROUP + 2 * RADIUS
LANES = 128
PER = LANES // WIN
POS = 5
STAT = SPAN * SPAN
F32 = jnp.float32
BF16 = jnp.bfloat16
VMEM_LIMIT = 24 * 1024 * 1024


def nt(a, b):
    return lax.dot_general(a, b, (((1,), (1,)), ((), ())), preferred_element_type=F32)


def nn(a, b):
    return lax.dot_general(a, b, (((1,), (0,)), ((), ())), preferred_element_type=F32)


def tn(a, b):
    return lax.dot_general(a, b, (((0,), (0,)), ((), ())), preferred_element_type=F32)


def iota(shape, dim):
    return lax.broadcasted_iota(jnp.int32, shape, dim)


def mirror(size):
    row, col = iota((size, size), 0), iota((size, size), 1)
    return (col == (row ^ (GROUP - 1))).astype(F32).astype(BF16)


def spread(p):
    first = p * PER * SPAN
    return first // 8 * 8, first % 8


def spread_table(p, dim):
    _, offset = spread(p)
    count = (PER if p < POS - 1 else 1) * SPAN
    dims = [LANES, LANES]
    dims[dim] = -(-(count + offset) // 8) * 8 if p < POS - 1 else count
    place, lane = iota(dims, dim), iota(dims, 1 - dim)
    dy, t = lane // WIN, lane % WIN
    hit = (place == dy * SPAN + t + offset) & (t < SPAN) & (dy * SPAN < count)
    return hit.astype(F32).astype(BF16)


def skew(values, shift):
    return pltpu.roll(values, shift, 2, stride=1, stride_axis=1)


def skew_wide(values, shift):
    parts = []
    for start in range(0, values.shape[-1], LANES):
        parts.append(skew(values[:, :, start : start + LANES], shift))
    return parts


def fill_columns(pad_ref, row, rows, cols):
    zero = jnp.zeros((rows, RADIUS, pad_ref.shape[2]), BF16)
    pad_ref[row : row + rows, 0:RADIUS] = zero
    pad_ref[row : row + rows, RADIUS + cols :] = zero


def fill_padded(pad_ref, row, block_ref):
    rows, cols = block_ref.shape[:2]
    fill_columns(pad_ref, row, rows, cols)
    pad_ref[row : row + rows, RADIUS : RADIUS + cols] = block_ref[...]


def window(pad_ref, row, rows, g):
    block = pad_ref[row : row + rows, g * GROUP : g * GROUP + WIN, :]
    return block.reshape(rows * WIN, block.shape[2])


def correlate_set(lhs, pad_ref, row, g, inv_root, out_ref, spot, lane):
    ys = lhs.shape[0] // GROUP
    scores = nt(lhs, window(pad_ref, row, 8, g)) * inv_root
    scores = scores.reshape(ys, GROUP, 8 * WIN)
    for i, part in enumerate(skew_wide(scores, LANES - GROUP + 1)):
        at = lane + i * LANES
        out_ref[spot, g, :, at : at + LANES] = part.astype(BF16)


def spread_weights(weight, wide_ref, tall_ref):
    kout = weight.shape[1]
    wides, talls = [], []
    for p in range(POS):
        row, _ = spread(p)
        table = spread_table(p, 0)
        part = weight[row : row + table.shape[0], :]
        wides.append(tn(part, table))
        talls.append(nn(spread_table(p, 1), part))
    base = jnp.concatenate(wides, axis=1)
    tall = jnp.concatenate(talls, axis=0).astype(BF16)[: SPAN * WIN]
    tall_rows = tall_ref.shape[1]
    for r in range(PER):
        edge = jnp.zeros((kout, LANES), BF16)
        moved = base if r == 0 else pltpu.roll(base, r * WIN, 1)
        wide_ref[r] = jnp.concatenate([edge, moved.astype(BF16), edge], axis=1)
        start = LANES + r * WIN
        tall_ref[r, :start] = jnp.zeros((start, kout), BF16)
        tall_ref[r, start : start + SPAN * WIN] = tall
        tall_ref[r, start + SPAN * WIN :] = jnp.zeros((tall_rows - start - SPAN * WIN, kout), BF16)


def load_kernel(
    source_hbm,
    edit_hbm,
    weight_hbm,
    source_ref,
    pad,
    turned_ref,
    wide_ref,
    tall_ref,
    weight,
    sems,
):
    rows, groups, _, chan = source_ref.shape
    cols = groups * GROUP
    weight_copy = pltpu.make_async_copy(weight_hbm, weight, sems.at[2])
    source_copy = pltpu.make_async_copy(source_hbm, source_ref, sems.at[1])
    edit_copy = pltpu.make_async_copy(edit_hbm, pad.at[:, RADIUS : RADIUS + cols], sems.at[0])
    weight_copy.start()
    source_copy.start()
    edit_copy.start()
    fill_columns(pad, 0, rows, cols)
    turn = mirror(rows * GROUP)
    weight_copy.wait()
    spread_weights(weight, wide_ref, tall_ref)
    source_copy.wait()
    for g in range(groups):
        lhs = nn(turn, source_ref[:, g].reshape(rows * GROUP, chan)).astype(BF16)
        turned_ref[:, g] = lhs.reshape(rows, GROUP, chan)
    edit_copy.wait()


def inner_kernel(inv_root, turned_ref, pad, tall_ref, corr_ref, own_ref):
    rows, groups, _, chan = turned_ref.shape
    for g in range(groups):
        lhs = turned_ref[:, g].reshape(rows * GROUP, chan)
        for s in range(rows // 8):
            correlate_set(lhs, pad, 8 * s, g, inv_root, corr_ref, slice(0, rows), 2 * s * LANES)
    cols = groups * GROUP
    for q in range(rows // PER):
        start = (3 - q) * LANES
        for r in range(PER):
            lhs = corr_ref[q * PER + r].reshape(cols, 4 * LANES)
            own_ref[q * PER + r] = nn(lhs, tall_ref[r, start : start + 4 * LANES])


def edge_spot(parts, kind):
    me = lax.axis_index("space")
    above = lax.rem(me, 2) ^ 1 if kind == 0 else lax.rem(me, 2)
    inside = jnp.where(above == 1, me != parts - 1, me != 0)
    return above, inside


def fill_halo(pad_ref, row, halo_ref, inside):
    cols = halo_ref.shape[1]
    pad_ref[pl.ds(row, 8), RADIUS : RADIUS + cols] = jnp.where(
        inside, halo_ref[...], jnp.zeros(halo_ref.shape, BF16)
    )


def rim_scores(inv_root, parts, kind, turned_ref, halo_ref, pad, rim_ref):
    rows, groups, _, chan = turned_ref.shape
    half = rows // 2
    above, inside = edge_spot(parts, kind)
    fill_columns(pad, 0, 8, groups * GROUP)
    fill_halo(pad, 0, halo_ref, inside)
    start = half * above
    for g in range(groups):
        lhs = turned_ref[pl.ds(start, half), g].reshape(half * GROUP, chan)
        correlate_set(lhs, pad, 0, g, inv_root, rim_ref, slice(0, half), 0)
    return above


def rim_values(rim_ref, tall_ref, above, out_ref):
    half, groups, _, lanes = rim_ref.shape
    for i in range(half):
        q, r = i // PER, i % PER
        start = pl.multiple_of((1 - q) * LANES + above * 4 * LANES, LANES)
        lhs = rim_ref[i].reshape(groups * GROUP, lanes)
        out_ref[i] = nn(lhs, tall_ref[r, pl.ds(start, lanes), :])


def half_rows(above, own_ref, extra, corr_ref, rim, strip, bias_ref, head_ref, gate_ref, gate_at):
    half, groups = rim.shape[:2]
    cols = groups * GROUP
    rim_lanes, own_lanes = rim.shape[3], corr_ref.shape[3]

    @pl.when(above == 0)
    def _():
        strip[:, :, :, :rim_lanes] = rim[...]
        strip[:, :, :, rim_lanes:] = corr_ref[:half]

    @pl.when(above == 1)
    def _():
        strip[:, :, :, :own_lanes] = corr_ref[half:]
        strip[:, :, :, own_lanes:] = rim[...]

    bias, head = bias_ref[...], head_ref[...]
    kout = bias.shape[1]
    turn = mirror(cols)
    hidden = jnp.zeros((1, kout), F32)
    slopes = jnp.zeros((1, kout), F32)
    total = None
    for r in range(PER):
        rows = [q * PER + r for q in range(half // PER)]
        value = jnp.concatenate([own_ref[half * above + i] + extra[i] for i in rows], axis=0) + bias
        gating = jax.nn.sigmoid(value)
        act = value * gating
        slope = gating * (1.0 + value * (1.0 - gating))
        hidden = hidden + jnp.sum(act, axis=0, keepdims=True)
        slopes = slopes + jnp.sum(slope, axis=0, keepdims=True)
        pre = (slope * head).astype(BF16)
        for q, i in enumerate(rows):
            gate_ref[gate_at + i] = nn(turn, pre[q * cols : (q + 1) * cols]).astype(BF16)
        corr = [strip[i, :, :, i // PER * LANES : (i // PER + POS) * LANES] for i in rows]
        corr = jnp.concatenate([c.reshape(cols, POS * LANES) for c in corr], axis=0)
        grad = tn(pre, corr)
        if r:
            grad = pltpu.roll(grad, POS * LANES - r * WIN, 1)
        total = grad if total is None else total + grad
    return hidden, slopes, total


def across_kernel(
    inv_root,
    parts,
    turned_ref,
    corr_ref,
    own_ref,
    halo_ref,
    tall_ref,
    bias_ref,
    head_ref,
    gate_ref,
    sums_ref,
    total_ref,
    pad,
    rim,
    extra,
    strip,
):
    above = rim_scores(inv_root, parts, 0, turned_ref, halo_ref, pad, rim)
    rim_values(rim, tall_ref, above, extra)
    hidden, slopes, total_ref[...] = half_rows(
        above, own_ref, extra, corr_ref, rim, strip, bias_ref, head_ref, gate_ref, 0
    )
    sums_ref[0:1] = hidden
    sums_ref[1:2] = slopes


def slice_kernel(edit_ref, across_ref, beyond_ref, sems):
    rows = edit_ref.shape[0]
    odd = lax.rem(lax.axis_index("space"), 2)
    copies = []
    count = sems.shape[0] // 2
    step = RADIUS // count
    for start, ref in ((odd, beyond_ref), (1 - odd, across_ref)):
        for i in range(count):
            block = edit_ref.at[pl.ds((rows - RADIUS) * start + i * step, step)]
            copies.append(
                pltpu.make_async_copy(
                    block, ref.at[i * step : (i + 1) * step], sems.at[len(copies)]
                )
            )
            copies[-1].start()
    for copy in copies:
        copy.wait()


def put_rows(stage, share, row, values):
    done = 0
    while done < values.shape[0]:
        piece, at = divmod(row + done, share - 1)
        count = min(values.shape[0] - done, share - 1 - at)
        start = piece * share + at
        stage[start : start + count] = values[done : done + count]
        done += count


def outer_kernel(
    inv_root,
    pixels,
    parts,
    turned_ref,
    corr_ref,
    own_ref,
    halo_ref,
    tall_ref,
    bias_ref,
    head_ref,
    near_gate_ref,
    near_sums_ref,
    near_total_ref,
    *rest,
):
    gate_ref, *piece_refs, pad, rim, extra, strip, stage = rest
    half = rim.shape[0]
    above = rim_scores(inv_root, parts, 1, turned_ref, halo_ref, pad, rim)
    rim_values(rim, tall_ref, above, extra)
    gate_ref[pl.ds(half * (1 - above), half)] = near_gate_ref[...]
    hidden, slopes, total = half_rows(
        above, own_ref, extra, corr_ref, rim, strip, bias_ref, head_ref, gate_ref, half * above
    )
    hidden = hidden + near_sums_ref[0:1]
    slopes = slopes + near_sums_ref[1:2]
    total = total + near_total_ref[...]
    head = head_ref[...]
    kout = head.shape[1]
    share = stage.shape[0] // parts
    stage[...] = jnp.zeros(stage.shape, F32)
    scale = 1.0 / pixels
    turned = jnp.transpose(total) * scale
    for dy in range(SPAN):
        put_rows(stage, share, dy * SPAN, turned[dy * WIN : dy * WIN + SPAN])
    put_rows(stage, share, STAT, jnp.concatenate([head * slopes, hidden], axis=0) * scale)
    score = jnp.sum(hidden * head, axis=1, keepdims=True) * scale
    me = lax.axis_index("space")
    for k in range(parts):
        start = pl.multiple_of(partner(me, k, parts) * share, 8)
        piece_refs[k][...] = stage[pl.ds(start, share), :]
        piece_refs[k][share - 1 :] = jnp.broadcast_to(score, (1, kout))


def back_chunks(gate_ref, wide_ref, r, rows, groups):
    quarter = rows // PER
    lhs = jnp.concatenate([gate_ref[q * PER + r] for q in range(quarter)], axis=0)
    out = []
    for pos in range(POS):
        grad = nn(lhs, wide_ref[r, :, (pos + 1) * LANES : (pos + 2) * LANES])
        grad = skew(grad.reshape(quarter * groups, GROUP, LANES), 0)
        out.append(grad.astype(BF16).reshape(quarter, groups, GROUP, LANES))
    return out


def rim_kernel(kind, parts, gate_ref, wide_ref, source_ref, out_ref, band, sums):
    rows, groups, _, chan = source_ref.shape
    half = rows // 2
    above, _ = edge_spot(parts, kind)
    first = 0 if gate_ref.shape[0] == half else half * above
    for i in range(half):
        q, r = i // PER, i % PER
        start = pl.multiple_of((1 - q) * LANES + above * 4 * LANES, LANES)
        grad = nn(gate_ref[first + i], wide_ref[r, :, pl.ds(start, 2 * LANES)])
        parts_of = skew_wide(grad.reshape(groups, GROUP, 2 * LANES), 0)
        band[i] = jnp.concatenate(parts_of, axis=2).astype(BF16)
    sums[...] = jnp.zeros(sums.shape, F32)
    for g in range(groups):
        lhs = band[:, g].reshape(half * GROUP, 2 * LANES)
        rhs = source_ref[pl.ds(half * above, half), g].reshape(half * GROUP, chan)
        sums[:, g * GROUP : g * GROUP + WIN, :] += tn(lhs, rhs).reshape(8, WIN, chan)
    out_ref[...] = sums[:, RADIUS : RADIUS + groups * GROUP].astype(BF16)


def back_kernel(
    parts,
    gate_ref,
    wide_ref,
    source_ref,
    own_pad,
    across_ref,
    beyond_ref,
    source_out,
    edit_out,
    pad,
    band,
    sums,
):
    rows, groups, _, chan = source_ref.shape
    half = rows // 2
    quarter = rows // PER
    for kind, ref in ((0, across_ref), (1, beyond_ref)):
        above, inside = edge_spot(parts, kind)
        fill_halo(pad, 8 * above, ref, inside)
    fill_columns(pad, 0, 16, groups * GROUP)
    zero = jnp.zeros((PER, groups, GROUP, LANES), BF16)
    for q, c in ((1, 0), (3, 2), (0, 5), (2, 7)):
        band[q * PER : (q + 1) * PER, :, :, c * LANES : (c + 1) * LANES] = zero
    for r in range(PER):
        for pos, part in enumerate(back_chunks(gate_ref, wide_ref, r, rows, groups)):
            for q in range(quarter):
                at = (q + pos) * LANES
                band[q * PER + r, :, :, at : at + LANES] = part[q]
    sums[...] = jnp.zeros(sums.shape, F32)

    def body(g, carry):
        start = g * GROUP
        near = source_ref[:, g].reshape(rows * GROUP, chan)
        for s in range(rows // 8):
            at = (2 + 2 * s) * LANES
            lhs = band[:, g, :, at : at + 2 * LANES].reshape(rows * GROUP, 2 * LANES)
            grad = tn(lhs, near).reshape(8, WIN, chan)
            sums[8 * s : 8 * s + 8, start : start + WIN, :] += grad
        for i in range(2):
            at = i * 2 * LANES
            lhs = band[i * half : (i + 1) * half, g, :, at : at + 6 * LANES]
            spots = [window(pad, 8 * i, 8, g), window(own_pad, 0, rows, g)]
            rhs = jnp.concatenate(spots[::-1] if i else spots, axis=0)
            grad = nn(lhs.reshape(half * GROUP, 6 * LANES), rhs)
            source_out[i * half : (i + 1) * half, g] = grad.reshape(half, GROUP, chan)
        return carry

    for g in range(groups):
        body(g, 0)
    cols = groups * GROUP
    edit_out[...] = sums[:, RADIUS : RADIUS + cols]


def partner(me, step, count):
    if count & (count - 1):
        return (me + step + count) % count
    return me ^ abs(step)


def judge_kernel(pairs, first_ref, second_ref, win_ref, *rest):
    piece_refs = rest[:pairs]
    total_ref, grad_ref, loss_ref = rest[pairs:]
    share = total_ref.shape[0]
    me = lax.axis_index("pair")
    first, second, win = first_ref[...], second_ref[...], win_ref[...]
    hots, margin = [], jnp.zeros(first.shape, F32)
    for k in range(pairs):
        pid = partner(me, -k, pairs)
        hot = (first == pid).astype(F32) - (second == pid).astype(F32)
        score = piece_refs[k][share - 1 : share, 0:1]
        margin = margin + hot * score
        hots.append(hot)
    sign = 2.0 * win.astype(F32) - 1.0
    loss = jnp.mean(jax.nn.softplus(-sign * margin), axis=1, keepdims=True)
    loss_ref[...] = jnp.broadcast_to(loss, loss_ref.shape)
    margin_grad = -sign * jax.nn.sigmoid(-sign * margin)
    total = jnp.zeros(total_ref.shape, F32)
    for k in range(pairs):
        grad = jnp.sum(margin_grad * hots[k], axis=1, keepdims=True)
        if k == 0:
            grad_ref[...] = jnp.broadcast_to(grad, grad_ref.shape)
        total = total + grad * piece_refs[k][...]
    total_ref[...] = total.astype(total_ref.dtype)


def gather_kernel(parts, *rest):
    piece_refs = rest[:parts]
    loss_ref, conv_ref, bias_ref, head_ref, loss_out, stage = rest[parts:]
    loss_out[...] = loss_ref[...]
    share = piece_refs[0].shape[0]
    me = lax.axis_index("space")
    for k in range(parts):
        start = pl.multiple_of(partner(me, -k, parts) * share, 8)
        stage[pl.ds(start, share), :] = piece_refs[k][...].astype(F32)
    rows = conv_ref.shape[0]
    for piece in range(-(-rows // (share - 1))):
        row = piece * (share - 1)
        count = min(share - 1, rows - row)
        conv_ref[row : row + count] = stage[piece * share : piece * share + count]
    for i, ref in enumerate((bias_ref, head_ref)):
        piece, at = divmod(STAT + i, share - 1)
        ref[...] = stage[piece * share + at : piece * share + at + 1]


def finish_kernel(
    inv_root,
    parts,
    grad_ref,
    source_ref,
    edit_ref,
    across_ref,
    beyond_ref,
    source_hbm,
    edit_hbm,
    source_out,
    edit_out,
    sems,
):
    scale = grad_ref[0:1, 0:1].reshape(1, 1, 1) * inv_root
    rows = edit_ref.shape[0]
    copies = []

    def send(out, hbm, at):
        copies.append(pltpu.make_async_copy(out.at[at], hbm.at[at], sems.at[len(copies)]))
        copies[-1].start()

    for y in range(0, rows, 4):
        at = slice(y, y + 4)
        source_out[at] = (source_ref[at] * scale).astype(BF16)
        send(source_out, source_hbm, at)
    for kind, ref in ((0, across_ref), (1, beyond_ref)):
        above, inside = edge_spot(parts, kind)
        for y in (0, 4):
            at = pl.ds((rows - 8) * above + y, 4)
            extra = jnp.where(inside, ref[y : y + 4].astype(F32), 0.0)
            edit_out[at] = ((edit_ref[at] + extra) * scale).astype(BF16)
            send(edit_out, edit_hbm, at)
    for copy in copies:
        copy.wait()


def call(kernel, outs, scratch, flops, *args, far=(), far_out=False):
    nbytes = sum(a.size * a.dtype.itemsize for a in args)
    spaces = [pltpu.HBM if i in far else pltpu.VMEM for i in range(len(args))]
    return pl.pallas_call(
        kernel,
        out_shape=outs,
        in_specs=[pl.BlockSpec(memory_space=space) for space in spaces],
        **({"out_specs": [pl.BlockSpec(memory_space=pltpu.HBM)] * len(outs)} if far_out else {}),
        scratch_shapes=scratch,
        compiler_params=pltpu.CompilerParams(vmem_limit_bytes=VMEM_LIMIT),
        cost_estimate=pl.CostEstimate(flops=flops, bytes_accessed=nbytes, transcendentals=0),
    )(*map(pltpu.with_memory_space_constraint, args, spaces))


def result(dims, dtype=F32):
    return jax.ShapeDtypeStruct(dims, dtype)


def shape(dims, dtype=F32):
    return pltpu.VMEM(dims, dtype)


def around(axis, step):
    count = lax.axis_size(axis)
    return [(i, partner(i, step, count)) for i in range(count)]


def beyond_pairs(teams, space):
    table = []
    for team in range(teams):
        for i in range(space):
            other = i + 1 if i % 2 else i - 1
            to = (team, other) if 0 <= other < space else (team ^ 1 if team ^ 1 < teams else team, i)
            table.append((team * space + i, to[0] * space + to[1]))
    return table


def local(
    source_feats, edit_feats, conv_weight, conv_bias, head_weight, comp_first, comp_second, comp_win
):
    _, rows, columns, chan = source_feats.shape
    kout, disp = conv_weight.shape
    inv_root = chan ** (-0.5)
    space, pairs = lax.axis_size("space"), lax.axis_size("pair")
    pixels = rows * space * columns
    groups = columns // GROUP
    wide_cols = columns + 2 * RADIUS
    share = 8
    while (share - 1) * space < disp + 2:
        share += 8
    edit = edit_feats[0]
    source = source_feats.reshape(rows, groups, GROUP, chan)
    to_across = [(i, i ^ 1 if i ^ 1 < space else i) for i in range(space)]
    to_beyond = beyond_pairs(lax.axis_size("groups"), space)
    across, beyond = call(
        slice_kernel,
        (shape((RADIUS, columns, chan), BF16),) * 2,
        [pltpu.SemaphoreType.DMA((2,))],
        10**4,
        edit,
        far=(0,),
    )
    across = lax.ppermute(across, "space", to_across)
    beyond = lax.ppermute(beyond, ("groups", "space"), to_beyond)
    near = (rows, groups, GROUP, chan)
    rim_shape = (rows // 2, groups, GROUP, 8 * WIN)
    held, own_pad, turned, wide, tall = call(
        load_kernel,
        (
            shape(near, BF16),
            shape((rows, wide_cols, chan), BF16),
            shape(near, BF16),
            shape((PER, kout, (POS + 2) * LANES), BF16),
            shape((PER, (POS + 2) * LANES, kout), BF16),
        ),
        [pltpu.VMEM((disp, kout), BF16), pltpu.SemaphoreType.DMA((3,))],
        10**4,
        source,
        edit,
        conv_weight.T,
        far=(0, 1, 2),
    )
    corr, own = call(
        functools.partial(inner_kernel, inv_root),
        (shape((rows, groups, GROUP, rows * WIN), BF16), shape((rows, columns, kout))),
        [],
        2 * 10**9,
        turned,
        own_pad,
        tall,
    )
    work = [
        pltpu.VMEM((RADIUS, wide_cols, chan), BF16),
        pltpu.VMEM(rim_shape, BF16),
        pltpu.VMEM((rows // 2, columns, kout), F32),
        pltpu.VMEM((rows // 2, groups, GROUP, (rows + RADIUS) * WIN), BF16),
    ]
    near_gate, near_sums, near_total = call(
        functools.partial(across_kernel, inv_root, space),
        (
            shape((rows // 2, columns, kout), BF16),
            shape((2, kout)),
            shape((kout, POS * LANES)),
        ),
        work,
        10**9,
        turned,
        corr,
        own,
        across,
        tall,
        conv_bias[None],
        head_weight[None],
    )

    def rim_terms(kind, gates):
        (terms,) = call(
            functools.partial(rim_kernel, kind, space),
            (shape((RADIUS, columns, chan), BF16),),
            [pltpu.VMEM(rim_shape, BF16), pltpu.VMEM((RADIUS, wide_cols, chan), F32)],
            10**9,
            gates,
            wide,
            held,
        )
        return terms

    terms, far = lax.optimization_barrier((rim_terms(0, near_gate), beyond))
    from_across = lax.ppermute(terms, "space", to_across)
    gate, *pieces = call(
        functools.partial(outer_kernel, inv_root, pixels, space),
        (shape((rows, columns, kout), BF16),) + (shape((share, kout)),) * space,
        work + [pltpu.VMEM((share * space, kout), F32)],
        2 * 10**9,
        turned,
        corr,
        own,
        far,
        tall,
        conv_bias[None],
        head_weight[None],
        near_gate,
        near_sums,
        near_total,
    )
    from_beyond = lax.ppermute(rim_terms(1, gate), ("groups", "space"), to_beyond)
    quarter = pieces[0]
    for k in reversed(range(1, space)):
        quarter = quarter + lax.ppermute(pieces[k], "space", around("space", k))
    source_sum, edit_sum = call(
        functools.partial(back_kernel, space),
        (shape((rows, groups, GROUP, chan)), shape((rows, columns, chan))),
        [
            pltpu.VMEM((2 * RADIUS, wide_cols, chan), BF16),
            pltpu.VMEM((rows, groups, GROUP, (rows + 2 * RADIUS) * WIN), BF16),
            pltpu.VMEM((rows, wide_cols, chan), F32),
        ],
        4 * 10**9,
        gate,
        wide,
        held,
        own_pad,
        across,
        beyond,
    )
    others = [quarter] + [lax.ppermute(quarter, "pair", around("pair", k)) for k in range(1, pairs)]
    *others, source_sum, edit_sum = lax.optimization_barrier((*others, source_sum, edit_sum))
    total, score_grad, loss = call(
        functools.partial(judge_kernel, pairs),
        (shape((share, kout), BF16), shape((8, LANES)), shape((1, LANES))),
        [],
        10**6,
        comp_first[None],
        comp_second[None],
        comp_win[None],
        *others,
    )
    gathered = [total] + [lax.ppermute(total, "space", around("space", k)) for k in range(1, space)]
    source_grad, edit_grad = call(
        functools.partial(finish_kernel, inv_root, space),
        (result((rows, columns, chan), BF16),) * 2,
        [
            pltpu.VMEM((rows, columns, chan), BF16),
            pltpu.VMEM((rows, columns, chan), BF16),
            pltpu.SemaphoreType.DMA((8,)),
        ],
        10**7,
        score_grad,
        source_sum.reshape(rows, columns, chan),
        edit_sum,
        from_across,
        from_beyond,
        far_out=True,
    )
    *gathered, source_grad, edit_grad = lax.optimization_barrier((*gathered, source_grad, edit_grad))
    conv_grad, bias_grad, head_grad, loss = call(
        functools.partial(gather_kernel, space),
        (result((disp, kout)), result((1, kout)), result((1, kout)), result((1, LANES))),
        [pltpu.VMEM((share * space, kout), F32)],
        10**6,
        *gathered,
        loss,
    )
    return (
        source_grad[None],
        edit_grad[None],
        conv_grad.T,
        bias_grad[0],
        head_grad[0],
        loss[0, :1],
    )


def solution(mesh):
    in_specs = (
        P(("groups", "pair"), "space", None, None),
        P(("groups", "pair"), "space", None, None),
        P(),
        P(),
        P(),
        P("groups"),
        P("groups"),
        P("groups"),
    )
    out_specs = (
        P(("groups", "pair"), "space", None, None),
        P(("groups", "pair"), "space", None, None),
        P("groups", None),
        P("groups"),
        P("groups"),
        P("groups"),
    )
    return jax.shard_map(local, mesh=mesh, in_specs=in_specs, out_specs=out_specs, check_vma=False)
```

```python
import functools

import jax
import jax.numpy as jnp
from jax import lax
from jax.experimental import pallas as pl
from jax.experimental.pallas import tpu as pltpu
from jax.sharding import PartitionSpec as P

RADIUS = 8
SPAN = 2 * RADIUS + 1
GROUP = 16
WIN = GROUP + 2 * RADIUS
LANES = 128
PER = LANES // WIN
POS = 5
STAT = SPAN * SPAN
F32 = jnp.float32
BF16 = jnp.bfloat16
VMEM_LIMIT = 24 * 1024 * 1024


def nt(a, b):
    return lax.dot_general(a, b, (((1,), (1,)), ((), ())), preferred_element_type=F32)


def nn(a, b):
    return lax.dot_general(a, b, (((1,), (0,)), ((), ())), preferred_element_type=F32)


def tn(a, b):
    return lax.dot_general(a, b, (((0,), (0,)), ((), ())), preferred_element_type=F32)


def iota(shape, dim):
    return lax.broadcasted_iota(jnp.int32, shape, dim)


def mirror(size):
    row, col = iota((size, size), 0), iota((size, size), 1)
    return (col == (row ^ (GROUP - 1))).astype(F32).astype(BF16)


def spread(p):
    first = p * PER * SPAN
    return first // 8 * 8, first % 8


def spread_table(p, dim):
    _, offset = spread(p)
    count = (PER if p < POS - 1 else 1) * SPAN
    dims = [LANES, LANES]
    dims[dim] = -(-(count + offset) // 8) * 8 if p < POS - 1 else count
    place, lane = iota(dims, dim), iota(dims, 1 - dim)
    dy, t = lane // WIN, lane % WIN
    hit = (place == dy * SPAN + t + offset) & (t < SPAN) & (dy * SPAN < count)
    return hit.astype(F32).astype(BF16)


def skew(values, shift):
    return pltpu.roll(values, shift, 2, stride=1, stride_axis=1)


def skew_wide(values, shift):
    parts = []
    for start in range(0, values.shape[-1], LANES):
        parts.append(skew(values[:, :, start : start + LANES], shift))
    return parts


def fill_columns(pad_ref, row, rows, cols):
    zero = jnp.zeros((rows, RADIUS, pad_ref.shape[2]), BF16)
    pad_ref[row : row + rows, 0:RADIUS] = zero
    pad_ref[row : row + rows, RADIUS + cols :] = zero


def fill_padded(pad_ref, row, block_ref):
    rows, cols = block_ref.shape[:2]
    fill_columns(pad_ref, row, rows, cols)
    pad_ref[row : row + rows, RADIUS : RADIUS + cols] = block_ref[...]


def window(pad_ref, row, rows, g):
    block = pad_ref[row : row + rows, g * GROUP : g * GROUP + WIN, :]
    return block.reshape(rows * WIN, block.shape[2])


def correlate_set(lhs, pad_ref, row, g, inv_root, out_ref, spot, lane):
    ys = lhs.shape[0] // GROUP
    scores = nt(lhs, window(pad_ref, row, 8, g)) * inv_root
    scores = scores.reshape(ys, GROUP, 8 * WIN)
    for i, part in enumerate(skew_wide(scores, LANES - GROUP + 1)):
        at = lane + i * LANES
        out_ref[spot, g, :, at : at + LANES] = part.astype(BF16)


def spread_weights(weight, wide_ref, tall_ref):
    kout = weight.shape[1]
    wides, talls = [], []
    for p in range(POS):
        row, _ = spread(p)
        table = spread_table(p, 0)
        part = weight[row : row + table.shape[0], :]
        wides.append(tn(part, table))
        talls.append(nn(spread_table(p, 1), part))
    base = jnp.concatenate(wides, axis=1)
    tall = jnp.concatenate(talls, axis=0).astype(BF16)[: SPAN * WIN]
    tall_rows = tall_ref.shape[1]
    for r in range(PER):
        edge = jnp.zeros((kout, LANES), BF16)
        moved = base if r == 0 else pltpu.roll(base, r * WIN, 1)
        wide_ref[r] = jnp.concatenate([edge, moved.astype(BF16), edge], axis=1)
        start = LANES + r * WIN
        tall_ref[r, :start] = jnp.zeros((start, kout), BF16)
        tall_ref[r, start : start + SPAN * WIN] = tall
        tall_ref[r, start + SPAN * WIN :] = jnp.zeros((tall_rows - start - SPAN * WIN, kout), BF16)


def load_kernel(
    source_hbm,
    edit_hbm,
    weight_hbm,
    source_ref,
    pad,
    turned_ref,
    wide_ref,
    tall_ref,
    weight,
    sems,
):
    rows, groups, _, chan = source_ref.shape
    cols = groups * GROUP
    weight_copy = pltpu.make_async_copy(weight_hbm, weight, sems.at[2])
    source_copy = pltpu.make_async_copy(source_hbm, source_ref, sems.at[1])
    edit_copy = pltpu.make_async_copy(edit_hbm, pad.at[:, RADIUS : RADIUS + cols], sems.at[0])
    weight_copy.start()
    source_copy.start()
    edit_copy.start()
    fill_columns(pad, 0, rows, cols)
    turn = mirror(rows * GROUP)
    weight_copy.wait()
    spread_weights(weight, wide_ref, tall_ref)
    source_copy.wait()
    for g in range(groups):
        lhs = nn(turn, source_ref[:, g].reshape(rows * GROUP, chan)).astype(BF16)
        turned_ref[:, g] = lhs.reshape(rows, GROUP, chan)
    edit_copy.wait()


def inner_kernel(inv_root, turned_ref, pad, tall_ref, corr_ref, own_ref):
    rows, groups, _, chan = turned_ref.shape
    for g in range(groups):
        lhs = turned_ref[:, g].reshape(rows * GROUP, chan)
        for s in range(rows // 8):
            correlate_set(lhs, pad, 8 * s, g, inv_root, corr_ref, slice(0, rows), 2 * s * LANES)
    cols = groups * GROUP
    for q in range(rows // PER):
        start = (3 - q) * LANES
        for r in range(PER):
            lhs = corr_ref[q * PER + r].reshape(cols, 4 * LANES)
            own_ref[q * PER + r] = nn(lhs, tall_ref[r, start : start + 4 * LANES])


def edge_spot(parts, kind):
    me = lax.axis_index("space")
    above = lax.rem(me, 2) ^ 1 if kind == 0 else lax.rem(me, 2)
    inside = jnp.where(above == 1, me != parts - 1, me != 0)
    return above, inside


def fill_halo(pad_ref, row, halo_ref, inside):
    cols = halo_ref.shape[1]
    pad_ref[pl.ds(row, 8), RADIUS : RADIUS + cols] = jnp.where(
        inside, halo_ref[...], jnp.zeros(halo_ref.shape, BF16)
    )


def rim_scores(inv_root, parts, kind, turned_ref, halo_ref, pad, rim_ref):
    rows, groups, _, chan = turned_ref.shape
    half = rows // 2
    above, inside = edge_spot(parts, kind)
    fill_columns(pad, 0, 8, groups * GROUP)
    fill_halo(pad, 0, halo_ref, inside)
    start = half * above
    for g in range(groups):
        lhs = turned_ref[pl.ds(start, half), g].reshape(half * GROUP, chan)
        correlate_set(lhs, pad, 0, g, inv_root, rim_ref, slice(0, half), 0)
    return above


def rim_values(rim_ref, tall_ref, above, out_ref):
    half, groups, _, lanes = rim_ref.shape
    for i in range(half):
        q, r = i // PER, i % PER
        start = pl.multiple_of((1 - q) * LANES + above * 4 * LANES, LANES)
        lhs = rim_ref[i].reshape(groups * GROUP, lanes)
        out_ref[i] = nn(lhs, tall_ref[r, pl.ds(start, lanes), :])


def half_rows(above, own_ref, extra, corr_ref, rim, strip, bias_ref, head_ref, gate_ref, gate_at):
    half, groups = rim.shape[:2]
    cols = groups * GROUP
    rim_lanes, own_lanes = rim.shape[3], corr_ref.shape[3]

    @pl.when(above == 0)
    def _():
        strip[:, :, :, :rim_lanes] = rim[...]
        strip[:, :, :, rim_lanes:] = corr_ref[:half]

    @pl.when(above == 1)
    def _():
        strip[:, :, :, :own_lanes] = corr_ref[half:]
        strip[:, :, :, own_lanes:] = rim[...]

    bias, head = bias_ref[...], head_ref[...]
    kout = bias.shape[1]
    turn = mirror(cols)
    hidden = jnp.zeros((1, kout), F32)
    slopes = jnp.zeros((1, kout), F32)
    total = None
    for r in range(PER):
        rows = [q * PER + r for q in range(half // PER)]
        value = jnp.concatenate([own_ref[half * above + i] + extra[i] for i in rows], axis=0) + bias
        gating = jax.nn.sigmoid(value)
        act = value * gating
        slope = gating * (1.0 + value * (1.0 - gating))
        hidden = hidden + jnp.sum(act, axis=0, keepdims=True)
        slopes = slopes + jnp.sum(slope, axis=0, keepdims=True)
        pre = (slope * head).astype(BF16)
        for q, i in enumerate(rows):
            gate_ref[gate_at + i] = nn(turn, pre[q * cols : (q + 1) * cols]).astype(BF16)
        corr = [strip[i, :, :, i // PER * LANES : (i // PER + POS) * LANES] for i in rows]
        corr = jnp.concatenate([c.reshape(cols, POS * LANES) for c in corr], axis=0)
        level = jnp.where(jnp.abs(slope - 1.0) < 2.0**-9, 1.0, 0.0).astype(BF16)
        grad = tn(jnp.concatenate([pre, level], axis=1), corr)
        if r:
            grad = pltpu.roll(grad, POS * LANES - r * WIN, 1)
        total = grad if total is None else total + grad
    return hidden, slopes, total


def across_kernel(
    inv_root,
    parts,
    turned_ref,
    corr_ref,
    own_ref,
    halo_ref,
    tall_ref,
    bias_ref,
    head_ref,
    gate_ref,
    sums_ref,
    total_ref,
    pad,
    rim,
    extra,
    strip,
):
    above = rim_scores(inv_root, parts, 0, turned_ref, halo_ref, pad, rim)
    rim_values(rim, tall_ref, above, extra)
    hidden, slopes, total_ref[...] = half_rows(
        above, own_ref, extra, corr_ref, rim, strip, bias_ref, head_ref, gate_ref, 0
    )
    sums_ref[0:1] = hidden
    sums_ref[1:2] = slopes


def slice_kernel(edit_ref, across_ref, beyond_ref, sems):
    rows = edit_ref.shape[0]
    odd = lax.rem(lax.axis_index("space"), 2)
    copies = []
    count = sems.shape[0] // 2
    step = RADIUS // count
    for start, ref in ((odd, beyond_ref), (1 - odd, across_ref)):
        for i in range(count):
            block = edit_ref.at[pl.ds((rows - RADIUS) * start + i * step, step)]
            copies.append(
                pltpu.make_async_copy(
                    block, ref.at[i * step : (i + 1) * step], sems.at[len(copies)]
                )
            )
            copies[-1].start()
    for copy in copies:
        copy.wait()


def put_rows(stage, share, row, values):
    done = 0
    while done < values.shape[0]:
        piece, at = divmod(row + done, share - 1)
        count = min(values.shape[0] - done, share - 1 - at)
        start = piece * share + at
        stage[start : start + count] = values[done : done + count]
        done += count


def outer_kernel(
    inv_root,
    pixels,
    parts,
    turned_ref,
    corr_ref,
    own_ref,
    halo_ref,
    tall_ref,
    bias_ref,
    head_ref,
    near_gate_ref,
    near_sums_ref,
    near_total_ref,
    *rest,
):
    gate_ref, *piece_refs, pad, rim, extra, strip, stage = rest
    half = rim.shape[0]
    above = rim_scores(inv_root, parts, 1, turned_ref, halo_ref, pad, rim)
    rim_values(rim, tall_ref, above, extra)
    gate_ref[pl.ds(half * (1 - above), half)] = near_gate_ref[...]
    hidden, slopes, total = half_rows(
        above, own_ref, extra, corr_ref, rim, strip, bias_ref, head_ref, gate_ref, half * above
    )
    hidden = hidden + near_sums_ref[0:1]
    slopes = slopes + near_sums_ref[1:2]
    total = total + near_total_ref[...]
    head = head_ref[...]
    kout = head.shape[1]
    share = stage.shape[1] // parts
    stage[...] = jnp.zeros(stage.shape, F32)
    scale = 1.0 / pixels
    turned = jnp.transpose(total) * scale
    for dy in range(SPAN):
        for i in range(2):
            block = turned[dy * WIN : dy * WIN + SPAN, i * kout : (i + 1) * kout]
            put_rows(stage.at[i], share, dy * SPAN, block)
    put_rows(stage.at[0], share, STAT, jnp.concatenate([head * slopes, hidden], axis=0) * scale)
    score = jnp.sum(hidden * head, axis=1, keepdims=True) * scale
    for p in range(parts):
        stage[0, (p + 1) * share - 1 : (p + 1) * share] = jnp.broadcast_to(score, (1, kout))
    me = lax.axis_index("space")
    for k in range(parts):
        at = pl.ds(pl.multiple_of(partner(me, k, parts) * share, 8), share)
        encode(piece_refs[k], stage[0, at], stage[1, at])


def encode(ref, value, level):
    first = value.astype(BF16)
    left = value - first.astype(F32)
    second = left.astype(BF16)
    third = left - second.astype(F32)
    ref[0] = first
    ref[1] = second
    last = iota(value.shape, 0) == value.shape[0] - 1
    ref[2] = jnp.where(last, third, level).astype(BF16)


def decode(ref):
    third = ref[2].astype(F32)
    last = iota(third.shape, 0) == third.shape[0] - 1
    value = ref[0].astype(F32) + ref[1].astype(F32) + jnp.where(last, third, 0.0)
    return value, jnp.where(last, 0.0, third)


def merge_kernel(*refs):
    *came_refs, out_ref = refs
    value, level = decode(came_refs[0])
    for ref in came_refs[1:]:
        more, flat = decode(ref)
        value, level = value + more, level + flat
    encode(out_ref, value, level)


def back_chunks(gate_ref, wide_ref, r, rows, groups):
    quarter = rows // PER
    lhs = jnp.concatenate([gate_ref[q * PER + r] for q in range(quarter)], axis=0)
    out = []
    for pos in range(POS):
        grad = nn(lhs, wide_ref[r, :, (pos + 1) * LANES : (pos + 2) * LANES])
        grad = skew(grad.reshape(quarter * groups, GROUP, LANES), 0)
        out.append(grad.astype(BF16).reshape(quarter, groups, GROUP, LANES))
    return out


def rim_kernel(kind, parts, gate_ref, wide_ref, source_ref, out_ref, band, sums):
    rows, groups, _, chan = source_ref.shape
    half = rows // 2
    above, _ = edge_spot(parts, kind)
    first = 0 if gate_ref.shape[0] == half else half * above
    for i in range(half):
        q, r = i // PER, i % PER
        start = pl.multiple_of((1 - q) * LANES + above * 4 * LANES, LANES)
        grad = nn(gate_ref[first + i], wide_ref[r, :, pl.ds(start, 2 * LANES)])
        parts_of = skew_wide(grad.reshape(groups, GROUP, 2 * LANES), 0)
        band[i] = jnp.concatenate(parts_of, axis=2).astype(BF16)
    sums[...] = jnp.zeros(sums.shape, F32)
    for g in range(groups):
        lhs = band[:, g].reshape(half * GROUP, 2 * LANES)
        rhs = source_ref[pl.ds(half * above, half), g].reshape(half * GROUP, chan)
        sums[:, g * GROUP : g * GROUP + WIN, :] += tn(lhs, rhs).reshape(8, WIN, chan)
    out_ref[...] = sums[:, RADIUS : RADIUS + groups * GROUP].astype(BF16)


def back_kernel(
    parts,
    gate_ref,
    wide_ref,
    source_ref,
    own_pad,
    across_ref,
    beyond_ref,
    source_out,
    edit_out,
    pad,
    band,
    sums,
):
    rows, groups, _, chan = source_ref.shape
    half = rows // 2
    quarter = rows // PER
    for kind, ref in ((0, across_ref), (1, beyond_ref)):
        above, inside = edge_spot(parts, kind)
        fill_halo(pad, 8 * above, ref, inside)
    fill_columns(pad, 0, 16, groups * GROUP)
    zero = jnp.zeros((PER, groups, GROUP, LANES), BF16)
    for q, c in ((1, 0), (3, 2), (0, 5), (2, 7)):
        band[q * PER : (q + 1) * PER, :, :, c * LANES : (c + 1) * LANES] = zero
    for r in range(PER):
        for pos, part in enumerate(back_chunks(gate_ref, wide_ref, r, rows, groups)):
            for q in range(quarter):
                at = (q + pos) * LANES
                band[q * PER + r, :, :, at : at + LANES] = part[q]
    sums[...] = jnp.zeros(sums.shape, F32)

    def body(g, carry):
        start = g * GROUP
        near = source_ref[:, g].reshape(rows * GROUP, chan)
        for s in range(rows // 8):
            at = (2 + 2 * s) * LANES
            lhs = band[:, g, :, at : at + 2 * LANES].reshape(rows * GROUP, 2 * LANES)
            grad = tn(lhs, near).reshape(8, WIN, chan)
            sums[8 * s : 8 * s + 8, start : start + WIN, :] += grad
        for i in range(2):
            at = i * 2 * LANES
            lhs = band[i * half : (i + 1) * half, g, :, at : at + 6 * LANES]
            spots = [window(pad, 8 * i, 8, g), window(own_pad, 0, rows, g)]
            rhs = jnp.concatenate(spots[::-1] if i else spots, axis=0)
            grad = nn(lhs.reshape(half * GROUP, 6 * LANES), rhs)
            source_out[i * half : (i + 1) * half, g] = grad.reshape(half, GROUP, chan)
        return carry

    for g in range(groups):
        body(g, 0)
    cols = groups * GROUP
    edit_out[...] = sums[:, RADIUS : RADIUS + cols]


def partner(me, step, count):
    if count & (count - 1):
        return (me + step + count) % count
    return me ^ abs(step)


def judge_kernel(pairs, first_ref, second_ref, win_ref, head_ref, *rest):
    piece_refs = rest[:pairs]
    total_ref, grad_ref, loss_ref = rest[pairs:]
    share = total_ref.shape[0]
    me = lax.axis_index("pair")
    first, second, win = first_ref[...], second_ref[...], win_ref[...]
    hots, margin = [], jnp.zeros(first.shape, F32)
    planes = [decode(ref) for ref in piece_refs]
    head = head_ref[...]
    held = head.astype(BF16).astype(F32)
    for k in range(pairs):
        pid = partner(me, -k, pairs)
        hot = (first == pid).astype(F32) - (second == pid).astype(F32)
        score = planes[k][0][share - 1 : share, 0:1]
        margin = margin + hot * score
        hots.append(hot)
    sign = 2.0 * win.astype(F32) - 1.0
    loss = jnp.mean(jax.nn.softplus(-sign * margin), axis=1, keepdims=True)
    loss_ref[...] = jnp.broadcast_to(loss, loss_ref.shape)
    margin_grad = -sign * jax.nn.sigmoid(-sign * margin)
    total = jnp.zeros(total_ref.shape, F32)
    for k in range(pairs):
        grad = jnp.sum(margin_grad * hots[k], axis=1, keepdims=True)
        if k == 0:
            grad_ref[...] = jnp.broadcast_to(grad, grad_ref.shape)
        extra = (grad * head).astype(BF16).astype(F32) - grad * held
        total = total + grad * planes[k][0] + extra * planes[k][1]
    total_ref[...] = total.astype(total_ref.dtype)


def gather_kernel(parts, *rest):
    piece_refs = rest[:parts]
    loss_ref, conv_ref, bias_ref, head_ref, loss_out, stage = rest[parts:]
    loss_out[...] = loss_ref[...]
    share = piece_refs[0].shape[0]
    me = lax.axis_index("space")
    for k in range(parts):
        start = pl.multiple_of(partner(me, -k, parts) * share, 8)
        stage[pl.ds(start, share), :] = piece_refs[k][...].astype(F32)
    rows = conv_ref.shape[0]
    for piece in range(-(-rows // (share - 1))):
        row = piece * (share - 1)
        count = min(share - 1, rows - row)
        conv_ref[row : row + count] = stage[piece * share : piece * share + count]
    for i, ref in enumerate((bias_ref, head_ref)):
        piece, at = divmod(STAT + i, share - 1)
        ref[...] = stage[piece * share + at : piece * share + at + 1]


def finish_kernel(
    inv_root,
    parts,
    grad_ref,
    source_ref,
    edit_ref,
    across_ref,
    beyond_ref,
    source_hbm,
    edit_hbm,
    source_out,
    edit_out,
    sems,
):
    scale = grad_ref[0:1, 0:1].reshape(1, 1, 1) * inv_root
    rows = edit_ref.shape[0]
    copies = []

    def send(out, hbm, at):
        copies.append(pltpu.make_async_copy(out.at[at], hbm.at[at], sems.at[len(copies)]))
        copies[-1].start()

    for y in range(0, rows, 4):
        at = slice(y, y + 4)
        source_out[at] = (source_ref[at] * scale).astype(BF16)
        send(source_out, source_hbm, at)
    for kind, ref in ((0, across_ref), (1, beyond_ref)):
        above, inside = edge_spot(parts, kind)
        for y in (0, 4):
            at = pl.ds((rows - 8) * above + y, 4)
            extra = jnp.where(inside, ref[y : y + 4].astype(F32), 0.0)
            edit_out[at] = ((edit_ref[at] + extra) * scale).astype(BF16)
            send(edit_out, edit_hbm, at)
    for copy in copies:
        copy.wait()


def call(kernel, outs, scratch, flops, *args, far=(), far_out=False):
    nbytes = sum(a.size * a.dtype.itemsize for a in args)
    spaces = [pltpu.HBM if i in far else pltpu.VMEM for i in range(len(args))]
    return pl.pallas_call(
        kernel,
        out_shape=outs,
        in_specs=[pl.BlockSpec(memory_space=space) for space in spaces],
        **({"out_specs": [pl.BlockSpec(memory_space=pltpu.HBM)] * len(outs)} if far_out else {}),
        scratch_shapes=scratch,
        compiler_params=pltpu.CompilerParams(vmem_limit_bytes=VMEM_LIMIT),
        cost_estimate=pl.CostEstimate(flops=flops, bytes_accessed=nbytes, transcendentals=0),
    )(*map(pltpu.with_memory_space_constraint, args, spaces))


def result(dims, dtype=F32):
    return jax.ShapeDtypeStruct(dims, dtype)


def shape(dims, dtype=F32):
    return pltpu.VMEM(dims, dtype)


def around(axis, step):
    count = lax.axis_size(axis)
    return [(i, partner(i, step, count)) for i in range(count)]


def beyond_pairs(teams, space):
    table = []
    for team in range(teams):
        for i in range(space):
            other = i + 1 if i % 2 else i - 1
            to = (team, other) if 0 <= other < space else (team ^ 1 if team ^ 1 < teams else team, i)
            table.append((team * space + i, to[0] * space + to[1]))
    return table


def local(
    source_feats, edit_feats, conv_weight, conv_bias, head_weight, comp_first, comp_second, comp_win
):
    _, rows, columns, chan = source_feats.shape
    kout, disp = conv_weight.shape
    inv_root = chan ** (-0.5)
    space, pairs = lax.axis_size("space"), lax.axis_size("pair")
    pixels = rows * space * columns
    groups = columns // GROUP
    wide_cols = columns + 2 * RADIUS
    share = 8
    while (share - 1) * space < disp + 2:
        share += 8
    edit = edit_feats[0]
    source = source_feats.reshape(rows, groups, GROUP, chan)
    to_across = [(i, i ^ 1 if i ^ 1 < space else i) for i in range(space)]
    to_beyond = beyond_pairs(lax.axis_size("groups"), space)
    across, beyond = call(
        slice_kernel,
        (shape((RADIUS, columns, chan), BF16),) * 2,
        [pltpu.SemaphoreType.DMA((2,))],
        10**4,
        edit,
        far=(0,),
    )
    across = lax.ppermute(across, "space", to_across)
    beyond = lax.ppermute(beyond, ("groups", "space"), to_beyond)
    near = (rows, groups, GROUP, chan)
    rim_shape = (rows // 2, groups, GROUP, 8 * WIN)
    held, own_pad, turned, wide, tall = call(
        load_kernel,
        (
            shape(near, BF16),
            shape((rows, wide_cols, chan), BF16),
            shape(near, BF16),
            shape((PER, kout, (POS + 2) * LANES), BF16),
            shape((PER, (POS + 2) * LANES, kout), BF16),
        ),
        [pltpu.VMEM((disp, kout), BF16), pltpu.SemaphoreType.DMA((3,))],
        10**4,
        source,
        edit,
        conv_weight.T,
        far=(0, 1, 2),
    )
    corr, own = call(
        functools.partial(inner_kernel, inv_root),
        (shape((rows, groups, GROUP, rows * WIN), BF16), shape((rows, columns, kout))),
        [],
        2 * 10**9,
        turned,
        own_pad,
        tall,
    )
    work = [
        pltpu.VMEM((RADIUS, wide_cols, chan), BF16),
        pltpu.VMEM(rim_shape, BF16),
        pltpu.VMEM((rows // 2, columns, kout), F32),
        pltpu.VMEM((rows // 2, groups, GROUP, (rows + RADIUS) * WIN), BF16),
    ]
    near_gate, near_sums, near_total = call(
        functools.partial(across_kernel, inv_root, space),
        (
            shape((rows // 2, columns, kout), BF16),
            shape((2, kout)),
            shape((2 * kout, POS * LANES)),
        ),
        work,
        10**9,
        turned,
        corr,
        own,
        across,
        tall,
        conv_bias[None],
        head_weight[None],
    )

    def rim_terms(kind, gates):
        (terms,) = call(
            functools.partial(rim_kernel, kind, space),
            (shape((RADIUS, columns, chan), BF16),),
            [pltpu.VMEM(rim_shape, BF16), pltpu.VMEM((RADIUS, wide_cols, chan), F32)],
            10**9,
            gates,
            wide,
            held,
        )
        return terms

    terms, far = lax.optimization_barrier((rim_terms(0, near_gate), beyond))
    from_across = lax.ppermute(terms, "space", to_across)
    gate, *pieces = call(
        functools.partial(outer_kernel, inv_root, pixels, space),
        (shape((rows, columns, kout), BF16),) + (shape((3, share, kout), BF16),) * space,
        work + [pltpu.VMEM((2, share * space, kout), F32)],
        2 * 10**9,
        turned,
        corr,
        own,
        far,
        tall,
        conv_bias[None],
        head_weight[None],
        near_gate,
        near_sums,
        near_total,
    )
    from_beyond = lax.ppermute(rim_terms(1, gate), ("groups", "space"), to_beyond)
    came = [lax.ppermute(pieces[k], "space", around("space", k)) for k in reversed(range(1, space))]
    (quarter,) = call(
        merge_kernel, (shape((3, share, kout), BF16),), [], 10**4, pieces[0], *came
    )
    source_sum, edit_sum = call(
        functools.partial(back_kernel, space),
        (shape((rows, groups, GROUP, chan)), shape((rows, columns, chan))),
        [
            pltpu.VMEM((2 * RADIUS, wide_cols, chan), BF16),
            pltpu.VMEM((rows, groups, GROUP, (rows + 2 * RADIUS) * WIN), BF16),
            pltpu.VMEM((rows, wide_cols, chan), F32),
        ],
        4 * 10**9,
        gate,
        wide,
        held,
        own_pad,
        across,
        beyond,
    )
    others = [quarter] + [lax.ppermute(quarter, "pair", around("pair", k)) for k in range(1, pairs)]
    *others, source_sum, edit_sum = lax.optimization_barrier((*others, source_sum, edit_sum))
    total, score_grad, loss = call(
        functools.partial(judge_kernel, pairs),
        (shape((share, kout), BF16), shape((8, LANES)), shape((1, LANES))),
        [],
        10**6,
        comp_first[None],
        comp_second[None],
        comp_win[None],
        head_weight[None],
        *others,
    )
    gathered = [total] + [lax.ppermute(total, "space", around("space", k)) for k in range(1, space)]
    source_grad, edit_grad = call(
        functools.partial(finish_kernel, inv_root, space),
        (result((rows, columns, chan), BF16),) * 2,
        [
            pltpu.VMEM((rows, columns, chan), BF16),
            pltpu.VMEM((rows, columns, chan), BF16),
            pltpu.SemaphoreType.DMA((8,)),
        ],
        10**7,
        score_grad,
        source_sum.reshape(rows, columns, chan),
        edit_sum,
        from_across,
        from_beyond,
        far_out=True,
    )
    *gathered, source_grad, edit_grad = lax.optimization_barrier((*gathered, source_grad, edit_grad))
    conv_grad, bias_grad, head_grad, loss = call(
        functools.partial(gather_kernel, space),
        (result((disp, kout)), result((1, kout)), result((1, kout)), result((1, LANES))),
        [pltpu.VMEM((share * space, kout), F32)],
        10**6,
        *gathered,
        loss,
    )
    return (
        source_grad[None],
        edit_grad[None],
        conv_grad.T,
        bias_grad[0],
        head_grad[0],
        loss[0, :1],
    )


def solution(mesh):
    in_specs = (
        P(("groups", "pair"), "space", None, None),
        P(("groups", "pair"), "space", None, None),
        P(),
        P(),
        P(),
        P("groups"),
        P("groups"),
        P("groups"),
    )
    out_specs = (
        P(("groups", "pair"), "space", None, None),
        P(("groups", "pair"), "space", None, None),
        P("groups", None),
        P("groups"),
        P("groups"),
        P("groups"),
    )
    return jax.shard_map(local, mesh=mesh, in_specs=in_specs, out_specs=out_specs, check_vma=False)
```

```python
import functools

import jax
import jax.numpy as jnp
from jax import lax
from jax.experimental import pallas as pl
from jax.experimental.pallas import tpu as pltpu
from jax.sharding import PartitionSpec as P

RADIUS = 8
SPAN = 2 * RADIUS + 1
GROUP = 16
WIN = GROUP + 2 * RADIUS
LANES = 128
PER = LANES // WIN
POS = 5
STAT = SPAN * SPAN
F32 = jnp.float32
BF16 = jnp.bfloat16
VMEM_LIMIT = 24 * 1024 * 1024


def nt(a, b):
    return lax.dot_general(a, b, (((1,), (1,)), ((), ())), preferred_element_type=F32)


def nn(a, b):
    return lax.dot_general(a, b, (((1,), (0,)), ((), ())), preferred_element_type=F32)


def tn(a, b):
    return lax.dot_general(a, b, (((0,), (0,)), ((), ())), preferred_element_type=F32)


def iota(shape, dim):
    return lax.broadcasted_iota(jnp.int32, shape, dim)


def mirror(size):
    row, col = iota((size, size), 0), iota((size, size), 1)
    return (col == (row ^ (GROUP - 1))).astype(F32).astype(BF16)


def spread(p):
    first = p * PER * SPAN
    return first // 8 * 8, first % 8


def spread_table(p, dim):
    _, offset = spread(p)
    count = (PER if p < POS - 1 else 1) * SPAN
    dims = [LANES, LANES]
    dims[dim] = -(-(count + offset) // 8) * 8 if p < POS - 1 else count
    place, lane = iota(dims, dim), iota(dims, 1 - dim)
    dy, t = lane // WIN, lane % WIN
    hit = (place == dy * SPAN + t + offset) & (t < SPAN) & (dy * SPAN < count)
    return hit.astype(F32).astype(BF16)


def skew(values, shift):
    return pltpu.roll(values, shift, 2, stride=1, stride_axis=1)


def skew_wide(values, shift):
    parts = []
    for start in range(0, values.shape[-1], LANES):
        parts.append(skew(values[:, :, start : start + LANES], shift))
    return parts


def fill_columns(pad_ref, row, rows, cols):
    zero = jnp.zeros((rows, RADIUS, pad_ref.shape[2]), BF16)
    pad_ref[row : row + rows, 0:RADIUS] = zero
    pad_ref[row : row + rows, RADIUS + cols :] = zero


def fill_padded(pad_ref, row, block_ref):
    rows, cols = block_ref.shape[:2]
    fill_columns(pad_ref, row, rows, cols)
    pad_ref[row : row + rows, RADIUS : RADIUS + cols] = block_ref[...]


def window(pad_ref, row, rows, g):
    block = pad_ref[row : row + rows, g * GROUP : g * GROUP + WIN, :]
    return block.reshape(rows * WIN, block.shape[2])


def correlate_set(lhs, pad_ref, row, g, inv_root, out_ref, spot, lane):
    ys = lhs.shape[0] // GROUP
    scores = nt(lhs, window(pad_ref, row, 8, g)) * inv_root
    scores = scores.reshape(ys, GROUP, 8 * WIN)
    for i, part in enumerate(skew_wide(scores, LANES - GROUP + 1)):
        at = lane + i * LANES
        out_ref[spot, g, :, at : at + LANES] = part.astype(BF16)


def spread_weights(weight, wide_ref, tall_ref):
    kout = weight.shape[1]
    wides, talls = [], []
    for p in range(POS):
        row, _ = spread(p)
        table = spread_table(p, 0)
        part = weight[row : row + table.shape[0], :]
        wides.append(tn(part, table))
        talls.append(nn(spread_table(p, 1), part))
    base = jnp.concatenate(wides, axis=1)
    tall = jnp.concatenate(talls, axis=0).astype(BF16)[: SPAN * WIN]
    tall_rows = tall_ref.shape[1]
    for r in range(PER):
        edge = jnp.zeros((kout, LANES), BF16)
        moved = base if r == 0 else pltpu.roll(base, r * WIN, 1)
        wide_ref[r] = jnp.concatenate([edge, moved.astype(BF16), edge], axis=1)
        start = LANES + r * WIN
        tall_ref[r, :start] = jnp.zeros((start, kout), BF16)
        tall_ref[r, start : start + SPAN * WIN] = tall
        tall_ref[r, start + SPAN * WIN :] = jnp.zeros((tall_rows - start - SPAN * WIN, kout), BF16)


def load_kernel(
    source_hbm,
    edit_hbm,
    weight_hbm,
    source_ref,
    pad,
    turned_ref,
    wide_ref,
    tall_ref,
    weight,
    sems,
):
    rows, groups, _, chan = source_ref.shape
    cols = groups * GROUP
    weight_copy = pltpu.make_async_copy(weight_hbm, weight, sems.at[2])
    source_copy = pltpu.make_async_copy(source_hbm, source_ref, sems.at[1])
    edit_copy = pltpu.make_async_copy(edit_hbm, pad.at[:, RADIUS : RADIUS + cols], sems.at[0])
    weight_copy.start()
    source_copy.start()
    edit_copy.start()
    fill_columns(pad, 0, rows, cols)
    turn = mirror(rows * GROUP)
    weight_copy.wait()
    spread_weights(weight, wide_ref, tall_ref)
    source_copy.wait()
    for g in range(groups):
        lhs = nn(turn, source_ref[:, g].reshape(rows * GROUP, chan)).astype(BF16)
        turned_ref[:, g] = lhs.reshape(rows, GROUP, chan)
    edit_copy.wait()


def inner_kernel(inv_root, turned_ref, pad, tall_ref, corr_ref, own_ref):
    rows, groups, _, chan = turned_ref.shape
    for g in range(groups):
        lhs = turned_ref[:, g].reshape(rows * GROUP, chan)
        for s in range(rows // 8):
            correlate_set(lhs, pad, 8 * s, g, inv_root, corr_ref, slice(0, rows), 2 * s * LANES)
    cols = groups * GROUP
    for q in range(rows // PER):
        start = (3 - q) * LANES
        for r in range(PER):
            lhs = corr_ref[q * PER + r].reshape(cols, 4 * LANES)
            own_ref[q * PER + r] = nn(lhs, tall_ref[r, start : start + 4 * LANES])


def edge_spot(parts, kind):
    me = lax.axis_index("space")
    above = lax.rem(me, 2) ^ 1 if kind == 0 else lax.rem(me, 2)
    inside = jnp.where(above == 1, me != parts - 1, me != 0)
    return above, inside


def fill_halo(pad_ref, row, halo_ref, inside):
    cols = halo_ref.shape[1]
    pad_ref[pl.ds(row, 8), RADIUS : RADIUS + cols] = jnp.where(
        inside, halo_ref[...], jnp.zeros(halo_ref.shape, BF16)
    )


def rim_scores(inv_root, parts, kind, turned_ref, halo_ref, pad, rim_ref):
    rows, groups, _, chan = turned_ref.shape
    half = rows // 2
    above, inside = edge_spot(parts, kind)
    fill_columns(pad, 0, 8, groups * GROUP)
    fill_halo(pad, 0, halo_ref, inside)
    start = half * above
    for g in range(groups):
        lhs = turned_ref[pl.ds(start, half), g].reshape(half * GROUP, chan)
        correlate_set(lhs, pad, 0, g, inv_root, rim_ref, slice(0, half), 0)
    return above


def rim_values(rim_ref, tall_ref, above, out_ref):
    half, groups, _, lanes = rim_ref.shape
    for i in range(half):
        q, r = i // PER, i % PER
        start = pl.multiple_of((1 - q) * LANES + above * 4 * LANES, LANES)
        lhs = rim_ref[i].reshape(groups * GROUP, lanes)
        out_ref[i] = nn(lhs, tall_ref[r, pl.ds(start, lanes), :])


def half_rows(above, own_ref, extra, corr_ref, rim, strip, bias_ref, head_ref, gate_ref, gate_at):
    half, groups = rim.shape[:2]
    cols = groups * GROUP
    rim_lanes, own_lanes = rim.shape[3], corr_ref.shape[3]

    @pl.when(above == 0)
    def _():
        strip[:, :, :, :rim_lanes] = rim[...]
        strip[:, :, :, rim_lanes:] = corr_ref[:half]

    @pl.when(above == 1)
    def _():
        strip[:, :, :, :own_lanes] = corr_ref[half:]
        strip[:, :, :, own_lanes:] = rim[...]

    bias, head = bias_ref[...], head_ref[...]
    kout = bias.shape[1]
    turn = mirror(cols)
    hidden = jnp.zeros((1, kout), F32)
    slopes = jnp.zeros((1, kout), F32)
    total = None
    for r in range(PER):
        rows = [q * PER + r for q in range(half // PER)]
        value = jnp.concatenate([own_ref[half * above + i] + extra[i] for i in rows], axis=0) + bias
        gating = jax.nn.sigmoid(value)
        act = value * gating
        slope = gating * (1.0 + value * (1.0 - gating))
        hidden = hidden + jnp.sum(act, axis=0, keepdims=True)
        slopes = slopes + jnp.sum(slope, axis=0, keepdims=True)
        pre = (slope * head).astype(BF16)
        for q, i in enumerate(rows):
            gate_ref[gate_at + i] = nn(turn, pre[q * cols : (q + 1) * cols]).astype(BF16)
        corr = [strip[i, :, :, i // PER * LANES : (i // PER + POS) * LANES] for i in rows]
        corr = jnp.concatenate([c.reshape(cols, POS * LANES) for c in corr], axis=0)
        level = jnp.where(jnp.abs(slope - 1.0) < 2.0**-9, 1.0, 0.0).astype(BF16)
        grad = tn(jnp.concatenate([pre, level], axis=1), corr)
        if r:
            grad = pltpu.roll(grad, POS * LANES - r * WIN, 1)
        total = grad if total is None else total + grad
    return hidden, slopes, total


def across_kernel(
    inv_root,
    parts,
    turned_ref,
    corr_ref,
    own_ref,
    halo_ref,
    tall_ref,
    bias_ref,
    head_ref,
    gate_ref,
    sums_ref,
    total_ref,
    pad,
    rim,
    extra,
    strip,
):
    above = rim_scores(inv_root, parts, 0, turned_ref, halo_ref, pad, rim)
    rim_values(rim, tall_ref, above, extra)
    hidden, slopes, total_ref[...] = half_rows(
        above, own_ref, extra, corr_ref, rim, strip, bias_ref, head_ref, gate_ref, 0
    )
    sums_ref[0:1] = hidden
    sums_ref[1:2] = slopes


def slice_kernel(edit_ref, across_ref, beyond_ref, sems):
    rows = edit_ref.shape[0]
    odd = lax.rem(lax.axis_index("space"), 2)
    copies = []
    count = sems.shape[0] // 2
    step = RADIUS // count
    for start, ref in ((odd, beyond_ref), (1 - odd, across_ref)):
        for i in range(count):
            block = edit_ref.at[pl.ds((rows - RADIUS) * start + i * step, step)]
            copies.append(
                pltpu.make_async_copy(
                    block, ref.at[i * step : (i + 1) * step], sems.at[len(copies)]
                )
            )
            copies[-1].start()
    for copy in copies:
        copy.wait()


def put_rows(stage, share, row, values):
    done = 0
    while done < values.shape[0]:
        piece, at = divmod(row + done, share - 1)
        count = min(values.shape[0] - done, share - 1 - at)
        start = piece * share + at
        stage[start : start + count] = values[done : done + count]
        done += count


def outer_kernel(
    inv_root,
    pixels,
    parts,
    turned_ref,
    corr_ref,
    own_ref,
    halo_ref,
    tall_ref,
    bias_ref,
    head_ref,
    near_gate_ref,
    near_sums_ref,
    near_total_ref,
    *rest,
):
    gate_ref, *piece_refs, pad, rim, extra, strip, stage = rest
    half = rim.shape[0]
    above = rim_scores(inv_root, parts, 1, turned_ref, halo_ref, pad, rim)
    rim_values(rim, tall_ref, above, extra)
    gate_ref[pl.ds(half * (1 - above), half)] = near_gate_ref[...]
    hidden, slopes, total = half_rows(
        above, own_ref, extra, corr_ref, rim, strip, bias_ref, head_ref, gate_ref, half * above
    )
    hidden = hidden + near_sums_ref[0:1]
    slopes = slopes + near_sums_ref[1:2]
    total = total + near_total_ref[...]
    head = head_ref[...]
    kout = head.shape[1]
    share = stage.shape[1] // parts
    stage[...] = jnp.zeros(stage.shape, F32)
    scale = 1.0 / pixels
    turned = jnp.transpose(total) * scale
    for dy in range(SPAN):
        for i in range(2):
            block = turned[dy * WIN : dy * WIN + SPAN, i * kout : (i + 1) * kout]
            put_rows(stage.at[i], share, dy * SPAN, block)
    put_rows(stage.at[0], share, STAT, jnp.concatenate([head * slopes, hidden], axis=0) * scale)
    score = jnp.sum(hidden * head, axis=1, keepdims=True) * scale
    for p in range(parts):
        stage[0, (p + 1) * share - 1 : (p + 1) * share] = jnp.broadcast_to(score, (1, kout))
    me = lax.axis_index("space")
    for k in range(parts):
        at = pl.ds(pl.multiple_of(partner(me, k, parts) * share, 8), share)
        encode(piece_refs[k], stage[0, at], stage[1, at])


def encode(ref, value, level):
    first = value.astype(BF16)
    left = value - first.astype(F32)
    second = left.astype(BF16)
    third = left - second.astype(F32)
    ref[0] = first
    ref[1] = second
    last = iota(value.shape, 0) == value.shape[0] - 1
    ref[2] = jnp.where(last, third, level).astype(BF16)


def decode(ref):
    third = ref[2].astype(F32)
    last = iota(third.shape, 0) == third.shape[0] - 1
    value = ref[0].astype(F32) + ref[1].astype(F32) + jnp.where(last, third, 0.0)
    return value, jnp.where(last, 0.0, third)


def merge_kernel(*refs):
    *came_refs, out_ref = refs
    value, level = decode(came_refs[0])
    for ref in came_refs[1:]:
        more, flat = decode(ref)
        value, level = value + more, level + flat
    encode(out_ref, value, level)


def back_chunks(gate_ref, wide_ref, r, rows, groups):
    quarter = rows // PER
    lhs = jnp.concatenate([gate_ref[q * PER + r] for q in range(quarter)], axis=0)
    out = []
    for pos in range(POS):
        grad = nn(lhs, wide_ref[r, :, (pos + 1) * LANES : (pos + 2) * LANES])
        grad = skew(grad.reshape(quarter * groups, GROUP, LANES), 0)
        out.append(grad.astype(BF16).reshape(quarter, groups, GROUP, LANES))
    return out


def rim_kernel(kind, parts, gate_ref, wide_ref, source_ref, out_ref, band, sums):
    rows, groups, _, chan = source_ref.shape
    half = rows // 2
    above, _ = edge_spot(parts, kind)
    first = 0 if gate_ref.shape[0] == half else half * above
    for i in range(half):
        q, r = i // PER, i % PER
        start = pl.multiple_of((1 - q) * LANES + above * 4 * LANES, LANES)
        grad = nn(gate_ref[first + i], wide_ref[r, :, pl.ds(start, 2 * LANES)])
        parts_of = skew_wide(grad.reshape(groups, GROUP, 2 * LANES), 0)
        band[i] = jnp.concatenate(parts_of, axis=2).astype(BF16)
    sums[...] = jnp.zeros(sums.shape, F32)
    for g in range(groups):
        lhs = band[:, g].reshape(half * GROUP, 2 * LANES)
        rhs = source_ref[pl.ds(half * above, half), g].reshape(half * GROUP, chan)
        sums[:, g * GROUP : g * GROUP + WIN, :] += tn(lhs, rhs).reshape(8, WIN, chan)
    out_ref[...] = sums[:, RADIUS : RADIUS + groups * GROUP].astype(BF16)


def back_kernel(
    parts,
    gate_ref,
    wide_ref,
    source_ref,
    own_pad,
    across_ref,
    beyond_ref,
    source_out,
    edit_out,
    pad,
    band,
    sums,
):
    rows, groups, _, chan = source_ref.shape
    half = rows // 2
    quarter = rows // PER
    for kind, ref in ((0, across_ref), (1, beyond_ref)):
        above, inside = edge_spot(parts, kind)
        fill_halo(pad, 8 * above, ref, inside)
    fill_columns(pad, 0, 16, groups * GROUP)
    zero = jnp.zeros((PER, groups, GROUP, LANES), BF16)
    for q, c in ((1, 0), (3, 2), (0, 5), (2, 7)):
        band[q * PER : (q + 1) * PER, :, :, c * LANES : (c + 1) * LANES] = zero
    for r in range(PER):
        for pos, part in enumerate(back_chunks(gate_ref, wide_ref, r, rows, groups)):
            for q in range(quarter):
                at = (q + pos) * LANES
                band[q * PER + r, :, :, at : at + LANES] = part[q]
    sums[...] = jnp.zeros(sums.shape, F32)

    def body(g, carry):
        start = g * GROUP
        near = source_ref[:, g].reshape(rows * GROUP, chan)
        for s in range(rows // 8):
            at = (2 + 2 * s) * LANES
            lhs = band[:, g, :, at : at + 2 * LANES].reshape(rows * GROUP, 2 * LANES)
            grad = tn(lhs, near).reshape(8, WIN, chan)
            sums[8 * s : 8 * s + 8, start : start + WIN, :] += grad
        for i in range(2):
            at = i * 2 * LANES
            lhs = band[i * half : (i + 1) * half, g, :, at : at + 6 * LANES]
            spots = [window(pad, 8 * i, 8, g), window(own_pad, 0, rows, g)]
            rhs = jnp.concatenate(spots[::-1] if i else spots, axis=0)
            grad = nn(lhs.reshape(half * GROUP, 6 * LANES), rhs)
            source_out[i * half : (i + 1) * half, g] = grad.reshape(half, GROUP, chan)
        return carry

    for g in range(groups):
        body(g, 0)
    cols = groups * GROUP
    edit_out[...] = sums[:, RADIUS : RADIUS + cols]


def partner(me, step, count):
    if count & (count - 1):
        return (me + step + count) % count
    return me ^ abs(step)


def judge_kernel(pairs, first_ref, second_ref, win_ref, head_ref, *rest):
    piece_refs = rest[:pairs]
    total_ref, grad_ref, loss_ref = rest[pairs:]
    share = total_ref.shape[0]
    me = lax.axis_index("pair")
    first, second, win = first_ref[...], second_ref[...], win_ref[...]
    hots, margin = [], jnp.zeros(first.shape, F32)
    planes = [decode(ref) for ref in piece_refs]
    head = head_ref[...]
    held = head.astype(BF16).astype(F32)
    for k in range(pairs):
        pid = partner(me, -k, pairs)
        hot = (first == pid).astype(F32) - (second == pid).astype(F32)
        score = planes[k][0][share - 1 : share, 0:1]
        margin = margin + hot * score
        hots.append(hot)
    sign = 2.0 * win.astype(F32) - 1.0
    loss = jnp.mean(jax.nn.softplus(-sign * margin), axis=1, keepdims=True)
    loss_ref[...] = jnp.broadcast_to(loss, loss_ref.shape)
    margin_grad = -sign * jax.nn.sigmoid(-sign * margin)
    total = jnp.zeros(total_ref.shape, F32)
    for k in range(pairs):
        grad = jnp.sum(margin_grad * hots[k], axis=1, keepdims=True)
        if k == 0:
            grad_ref[...] = jnp.broadcast_to(grad, grad_ref.shape)
        extra = (grad * head).astype(BF16).astype(F32) - grad * held
        total = total + grad * planes[k][0] + extra * planes[k][1]
    total_ref[...] = total.astype(total_ref.dtype)


def gather_kernel(parts, *rest):
    piece_refs = rest[:parts]
    loss_ref, conv_ref, bias_ref, head_ref, loss_out, stage = rest[parts:]
    loss_out[...] = loss_ref[...]
    share = piece_refs[0].shape[0]
    me = lax.axis_index("space")
    for k in range(parts):
        start = pl.multiple_of(partner(me, -k, parts) * share, 8)
        stage[pl.ds(start, share), :] = piece_refs[k][...].astype(F32)
    rows = conv_ref.shape[0]
    for piece in range(-(-rows // (share - 1))):
        row = piece * (share - 1)
        count = min(share - 1, rows - row)
        conv_ref[row : row + count] = stage[piece * share : piece * share + count]
    for i, ref in enumerate((bias_ref, head_ref)):
        piece, at = divmod(STAT + i, share - 1)
        ref[...] = stage[piece * share + at : piece * share + at + 1]


def finish_kernel(
    inv_root,
    parts,
    grad_ref,
    source_ref,
    edit_ref,
    across_ref,
    beyond_ref,
    source_hbm,
    edit_hbm,
    source_out,
    edit_out,
    sems,
):
    scale = grad_ref[0:1, 0:1].reshape(1, 1, 1) * inv_root
    rows = edit_ref.shape[0]
    copies = []

    def send(out, hbm, at):
        copies.append(pltpu.make_async_copy(out.at[at], hbm.at[at], sems.at[len(copies)]))
        copies[-1].start()

    for y in range(0, rows, 4):
        at = slice(y, y + 4)
        source_out[at] = (source_ref[at] * scale).astype(BF16)
        send(source_out, source_hbm, at)
    for kind, ref in ((0, across_ref), (1, beyond_ref)):
        above, inside = edge_spot(parts, kind)
        for y in (0, 4):
            at = pl.ds((rows - 8) * above + y, 4)
            extra = jnp.where(inside, ref[y : y + 4].astype(F32), 0.0)
            edit_out[at] = ((edit_ref[at] + extra) * scale).astype(BF16)
            send(edit_out, edit_hbm, at)
    for copy in copies:
        copy.wait()


def call(kernel, outs, scratch, flops, *args, far=(), far_out=False):
    nbytes = sum(a.size * a.dtype.itemsize for a in args)
    spaces = [pltpu.HBM if i in far else pltpu.VMEM for i in range(len(args))]
    return pl.pallas_call(
        kernel,
        out_shape=outs,
        in_specs=[pl.BlockSpec(memory_space=space) for space in spaces],
        **({"out_specs": [pl.BlockSpec(memory_space=pltpu.HBM)] * len(outs)} if far_out else {}),
        scratch_shapes=scratch,
        compiler_params=pltpu.CompilerParams(vmem_limit_bytes=VMEM_LIMIT),
        cost_estimate=pl.CostEstimate(flops=flops, bytes_accessed=nbytes, transcendentals=0),
    )(*map(pltpu.with_memory_space_constraint, args, spaces))


def result(dims, dtype=F32):
    return jax.ShapeDtypeStruct(dims, dtype)


def shape(dims, dtype=F32):
    return pltpu.VMEM(dims, dtype)


def around(axis, step):
    count = lax.axis_size(axis)
    return [(i, partner(i, step, count)) for i in range(count)]


def beyond_pairs(teams, space):
    table = []
    for team in range(teams):
        for i in range(space):
            other = i + 1 if i % 2 else i - 1
            to = (team, other) if 0 <= other < space else (team ^ 1 if team ^ 1 < teams else team, i)
            table.append((team * space + i, to[0] * space + to[1]))
    return table


def local(
    source_feats, edit_feats, conv_weight, conv_bias, head_weight, comp_first, comp_second, comp_win
):
    _, rows, columns, chan = source_feats.shape
    kout, disp = conv_weight.shape
    inv_root = chan ** (-0.5)
    space, pairs = lax.axis_size("space"), lax.axis_size("pair")
    pixels = rows * space * columns
    groups = columns // GROUP
    wide_cols = columns + 2 * RADIUS
    share = 8
    while (share - 1) * space < disp + 2:
        share += 8
    edit = edit_feats[0]
    source = source_feats.reshape(rows, groups, GROUP, chan)
    to_across = [(i, i ^ 1 if i ^ 1 < space else i) for i in range(space)]
    to_beyond = beyond_pairs(lax.axis_size("groups"), space)
    across, beyond = call(
        slice_kernel,
        (shape((RADIUS, columns, chan), BF16),) * 2,
        [pltpu.SemaphoreType.DMA((2,))],
        10**4,
        edit,
        far=(0,),
    )
    across = lax.ppermute(across, "space", to_across)
    beyond = lax.ppermute(beyond, ("groups", "space"), to_beyond)
    near = (rows, groups, GROUP, chan)
    rim_shape = (rows // 2, groups, GROUP, 8 * WIN)
    held, own_pad, turned, wide, tall = call(
        load_kernel,
        (
            shape(near, BF16),
            shape((rows, wide_cols, chan), BF16),
            shape(near, BF16),
            shape((PER, kout, (POS + 2) * LANES), BF16),
            shape((PER, (POS + 2) * LANES, kout), BF16),
        ),
        [pltpu.VMEM((disp, kout), BF16), pltpu.SemaphoreType.DMA((3,))],
        10**4,
        source,
        edit,
        conv_weight.T,
        far=(0, 1, 2),
    )
    corr, own = call(
        functools.partial(inner_kernel, inv_root),
        (shape((rows, groups, GROUP, rows * WIN), BF16), shape((rows, columns, kout))),
        [],
        2 * 10**9,
        turned,
        own_pad,
        tall,
    )
    work = [
        pltpu.VMEM((RADIUS, wide_cols, chan), BF16),
        pltpu.VMEM(rim_shape, BF16),
        pltpu.VMEM((rows // 2, columns, kout), F32),
        pltpu.VMEM((rows // 2, groups, GROUP, (rows + RADIUS) * WIN), BF16),
    ]
    near_gate, near_sums, near_total = call(
        functools.partial(across_kernel, inv_root, space),
        (
            shape((rows // 2, columns, kout), BF16),
            shape((2, kout)),
            shape((2 * kout, POS * LANES)),
        ),
        work,
        10**9,
        turned,
        corr,
        own,
        across,
        tall,
        conv_bias[None],
        head_weight[None],
    )

    def rim_terms(kind, gates):
        (terms,) = call(
            functools.partial(rim_kernel, kind, space),
            (shape((RADIUS, columns, chan), BF16),),
            [pltpu.VMEM(rim_shape, BF16), pltpu.VMEM((RADIUS, wide_cols, chan), F32)],
            10**9,
            gates,
            wide,
            held,
        )
        return terms

    terms, far = lax.optimization_barrier((rim_terms(0, near_gate), beyond))
    from_across = lax.ppermute(terms, "space", to_across)
    gate, *pieces = call(
        functools.partial(outer_kernel, inv_root, pixels, space),
        (shape((rows, columns, kout), BF16),) + (shape((3, share, kout), BF16),) * space,
        work + [pltpu.VMEM((2, share * space, kout), F32)],
        2 * 10**9,
        turned,
        corr,
        own,
        far,
        tall,
        conv_bias[None],
        head_weight[None],
        near_gate,
        near_sums,
        near_total,
    )
    came = [lax.ppermute(pieces[k], "space", around("space", k)) for k in reversed(range(1, space))]
    far_terms, *came = lax.optimization_barrier((rim_terms(1, gate), *came))
    from_beyond = lax.ppermute(far_terms, ("groups", "space"), to_beyond)
    (quarter,) = call(
        merge_kernel, (shape((3, share, kout), BF16),), [], 10**4, pieces[0], *came
    )
    source_sum, edit_sum = call(
        functools.partial(back_kernel, space),
        (shape((rows, groups, GROUP, chan)), shape((rows, columns, chan))),
        [
            pltpu.VMEM((2 * RADIUS, wide_cols, chan), BF16),
            pltpu.VMEM((rows, groups, GROUP, (rows + 2 * RADIUS) * WIN), BF16),
            pltpu.VMEM((rows, wide_cols, chan), F32),
        ],
        4 * 10**9,
        gate,
        wide,
        held,
        own_pad,
        across,
        beyond,
    )
    others = [quarter] + [lax.ppermute(quarter, "pair", around("pair", k)) for k in range(1, pairs)]
    *others, source_sum, edit_sum = lax.optimization_barrier((*others, source_sum, edit_sum))
    total, score_grad, loss = call(
        functools.partial(judge_kernel, pairs),
        (shape((share, kout), BF16), shape((8, LANES)), shape((1, LANES))),
        [],
        10**6,
        comp_first[None],
        comp_second[None],
        comp_win[None],
        head_weight[None],
        *others,
    )
    gathered = [total] + [lax.ppermute(total, "space", around("space", k)) for k in range(1, space)]
    source_grad, edit_grad = call(
        functools.partial(finish_kernel, inv_root, space),
        (result((rows, columns, chan), BF16),) * 2,
        [
            pltpu.VMEM((rows, columns, chan), BF16),
            pltpu.VMEM((rows, columns, chan), BF16),
            pltpu.SemaphoreType.DMA((8,)),
        ],
        10**7,
        score_grad,
        source_sum.reshape(rows, columns, chan),
        edit_sum,
        from_across,
        from_beyond,
        far_out=True,
    )
    *gathered, source_grad, edit_grad = lax.optimization_barrier((*gathered, source_grad, edit_grad))
    conv_grad, bias_grad, head_grad, loss = call(
        functools.partial(gather_kernel, space),
        (result((disp, kout)), result((1, kout)), result((1, kout)), result((1, LANES))),
        [pltpu.VMEM((share * space, kout), F32)],
        10**6,
        *gathered,
        loss,
    )
    return (
        source_grad[None],
        edit_grad[None],
        conv_grad.T,
        bias_grad[0],
        head_grad[0],
        loss[0, :1],
    )


def solution(mesh):
    in_specs = (
        P(("groups", "pair"), "space", None, None),
        P(("groups", "pair"), "space", None, None),
        P(),
        P(),
        P(),
        P("groups"),
        P("groups"),
        P("groups"),
    )
    out_specs = (
        P(("groups", "pair"), "space", None, None),
        P(("groups", "pair"), "space", None, None),
        P("groups", None),
        P("groups"),
        P("groups"),
        P("groups"),
    )
    return jax.shard_map(local, mesh=mesh, in_specs=in_specs, out_specs=out_specs, check_vma=False)
```
